32 devices in a mesh: dp: 8 (over z, y), head: 4 (over x, core).
Axes of the slice: x: 2, y: 2, z: 4, core: 2. Of those that a mesh axis runs over, the one named last changes fastest.
Arguments:
- inputs: bfloat16 [16384, 768], P(('dp', 'head')), may hold values from -6 to 6
- cotangent: bfloat16 [16384, 768], P(('dp', 'head')), may hold values from -12 to 12
- lengths: int32 [8, 4], P('dp'), may hold values from 0 to 2048, as said below
- norm1_gain: bfloat16 [768], replicated, may hold values from 0.25 to 1.75
- query_weight: bfloat16 [768, 768], P(None, 'head'), may hold values from -0.21875 to 0.21875
- query_bias: bfloat16 [768], P('head'), may hold values from -3 to 3
- key_weight: bfloat16 [768, 768], P(None, 'head'), may hold values from -0.21875 to 0.21875
- value_weight: bfloat16 [768, 768], P(None, 'head'), may hold values from -0.21875 to 0.21875
- value_bias: bfloat16 [768], P('head'), may hold values from -0.1875 to 0.1875
- inner_gain: bfloat16 [768], P('head'), may hold values from 0.25 to 1.75
- output_weight: bfloat16 [768, 768], P('head'), may hold values from -0.21875 to 0.21875
- output_bias: bfloat16 [768], replicated, may hold values from -1.75 to 1.75
- norm2_gain: bfloat16 [768], replicated, may hold values from 0.25 to 1.75
- hidden_weight: bfloat16 [768, 3072], P('dp', 'head'), may hold values from -0.21875 to 0.21875
- hidden_bias: bfloat16 [3072], P('head'), may hold values from -3 to 3
- hidden_gain: bfloat16 [3072], P('head'), may hold values from 0.25 to 1.75
- project_weight: bfloat16 [3072, 768], P('head', 'dp'), may hold values from -0.109375 to 0.109375
- project_bias: bfloat16 [768], replicated, may hold values from -1.75 to 1.75
Outputs:
- output: bfloat16 [16384, 768], P(('dp', 'head'))
- input_grad: float32 [16384, 768], P(('dp', 'head'))
- norm1_gain_grad: float32 [768], replicated
- query_weight_grad: float32 [768, 768], P(None, 'head')
- query_bias_grad: float32 [768], P('head')
- key_weight_grad: float32 [768, 768], P(None, 'head')
- value_weight_grad: float32 [768, 768], P(None, 'head')
- value_bias_grad: float32 [768], P('head')
- inner_gain_grad: float32 [768], P('head')
- output_weight_grad: float32 [768, 768], P('head')
- output_bias_grad: float32 [768], replicated
- norm2_gain_grad: float32 [768], replicated
- hidden_weight_grad: float32 [768, 3072], P('dp', 'head')
- hidden_bias_grad: float32 [3072], P('head')
- hidden_gain_grad: float32 [3072], P('head')
- project_weight_grad: float32 [3072, 768], P('head', 'dp')
- project_bias_grad: float32 [768], replicated
The draws below stay inside these ranges and needn't reach their ends.
Inputs may be any that keep to these rules, and one draw needn't show every extreme that they name: `lengths`: row s describes slot s. If its first entry exceeds 512, the slot holds one sequence of that length from its start and the other entries are 0; otherwise entry k, from 257 to 512, is the length of a sequence that starts at the k-th block of 512 tokens of the slot. Every draw has a slot that is one sequence of 2048 tokens and a slot of four sequences.
All inputs are finite; a program needn't handle non-finite values.
Results may differ from the reference program's by a relative error of at most 0.014.
Values may be sent and summed in bfloat16 or wider, within the bound.
No kernel may reach another device: no remote copies, remote signals or barrier semaphores. Data moves between devices by JAX's collectives and lax.ppermute only.
A program may use at most 192 MiB of HBM per device.

```python
import functools
import jax
import jax.numpy as jnp
from jax import lax

D = 768
HEADS = 12
HEAD_DIM = 64
FF = 3072
SHORT = 512
TOKENS = 16384
SLOT_COUNT = 8


def draw_lengths(key, part):
    slot_total = SLOT_COUNT
    key_list = jax.random.split(key, 5)
    chosen = jax.random.randint(key_list[0], (), 0, slot_total)
    second_row = (chosen + 1 + jax.random.randint(key_list[1], (), 0, slot_total - 1)) % slot_total
    row_index = jnp.arange(slot_total)
    coin_flip = jax.random.randint(key_list[2], (slot_total,), 0, 4) == 0
    longer = (coin_flip | (row_index == chosen)) & (row_index != second_row)
    long_length = 4 * SHORT - jax.random.randint(key_list[3], (slot_total,), 0, 2 * SHORT)
    long_length = jnp.where(row_index == chosen, 4 * SHORT, long_length)
    short_length = SHORT - jax.random.randint(key_list[4], (slot_total, 4), 0, SHORT // 2)
    long_rows = jnp.concatenate([long_length[:, None], jnp.zeros((slot_total, 3), jnp.int32)], axis=1)
    return jnp.where(longer[:, None], long_rows, short_length).astype(jnp.int32)


def strengthened(values, stream_key, source, target, shards_of, factor):
    def block_of(axis_at):
        return (jnp.arange(values.shape[axis_at]) // (values.shape[axis_at] // shards_of)).reshape((-1,) + (1,) * (values.ndim - 1 - axis_at))

    near = jax.random.permutation(stream_key, shards_of)[block_of(target)]
    second = (block_of(target) + shards_of // 2) % shards_of
    return jnp.where((block_of(source) == near) | (block_of(source) == second), factor * values, values)


def level_of(key, shape, pieces, smallest, high):
    def one(axis_at, blocks):
        draws = jax.random.uniform(jax.random.fold_in(jax.random.fold_in(key, 6), axis_at), (blocks,), jnp.float32, smallest / len(pieces), high / len(pieces))
        return jnp.repeat(jnp.exp(draws), shape[axis_at] // blocks).reshape((-1,) + (1,) * (len(shape) - axis_at - 1))

    level = one(*pieces[0])
    for cut in pieces[1:]:
        level = level * one(*cut)
    return level


def centred(key, shape, width, limit, cuts=(), held_as=jnp.bfloat16):
    values = jax.random.normal(key, shape, jnp.float32) * width
    if len(cuts) > 0:
        values = level_of(key, shape, cuts, -0.22, 0.18) * values
    return jnp.clip(values, min=-limit, max=limit).astype(held_as)


def bell_draw_with(own_key, extent, width, reach, pieces, heavy, held_as=jnp.bfloat16):
    values = width * jax.random.normal(own_key, extent, jnp.float32)
    if pieces:
        values = values * level_of(own_key, extent, pieces, -0.22, 0.18)
    return jnp.clip(strengthened(values, jax.random.fold_in(own_key, 3), *heavy), -reach, reach).astype(held_as)


def setup_inputs(seed: int = 0) -> dict:
    streams_of = jax.random.split(jax.random.key(seed), 19)
    inputs = centred(streams_of[0], (TOKENS, D), 1.0, 6.0, ((0, 32),))
    cotangent = bell_draw_with(streams_of[1], (TOKENS, D), 1.0, 12.0, ((0, 32),), (0, 1, 32, 2.75))
    lengths = draw_lengths(jax.random.fold_in(streams_of[18], 71), 0)
    norm1_gain = jnp.clip(1.0 + 0.15 * jax.random.normal(streams_of[3], (D,), jnp.float32), 0.25, 1.75).astype(jnp.bfloat16)
    query_weight = centred(streams_of[4], (D, D), D ** -0.5, 0.21875, ((1, 4),))
    query_bias = centred(streams_of[5], (D,), 0.5, 3.0, ((0, 4),))
    key_weight = centred(streams_of[6], (D, D), D ** -0.5, 0.21875, ((1, 4),))
    value_weight = centred(streams_of[7], (D, D), D ** -0.5, 0.21875, ((1, 4),))
    value_bias = centred(streams_of[8], (D,), 0.03, 0.1875, ((0, 4),))
    inner_gain = jnp.clip(1.0 + 0.15 * jax.random.normal(streams_of[9], (D,), jnp.float32), 0.25, 1.75).astype(jnp.bfloat16)
    output_weight = centred(streams_of[10], (D, D), D ** -0.5, 0.21875, ((0, 4),))
    output_bias = centred(streams_of[11], (D,), 0.3, 1.75)
    norm2_gain = jnp.clip(1.0 + 0.15 * jax.random.normal(streams_of[12], (D,), jnp.float32), 0.25, 1.75).astype(jnp.bfloat16)
    hidden_weight = centred(streams_of[13], (D, FF), D ** -0.5, 0.21875, ((0, 8), (1, 4)))
    hidden_bias = centred(streams_of[14], (FF,), 0.5, 3.0, ((0, 4),))
    hidden_gain = jnp.clip(1.0 + 0.15 * jax.random.normal(streams_of[15], (FF,), jnp.float32), 0.25, 1.75).astype(jnp.bfloat16)
    project_weight = centred(streams_of[16], (FF, D), FF ** -0.5, 0.109375, ((0, 4), (1, 8)))
    project_bias = centred(streams_of[17], (D,), 0.3, 1.75)
    return {"inputs": inputs, "cotangent": cotangent, "lengths": lengths, "norm1_gain": norm1_gain, "query_weight": query_weight, "query_bias": query_bias, "key_weight": key_weight, "value_weight": value_weight, "value_bias": value_bias, "inner_gain": inner_gain, "output_weight": output_weight, "output_bias": output_bias, "norm2_gain": norm2_gain, "hidden_weight": hidden_weight, "hidden_bias": hidden_bias, "hidden_gain": hidden_gain, "project_weight": project_weight, "project_bias": project_bias}


@jax.custom_vjp
def low(v):
    return lax.optimization_barrier(v.astype(jnp.bfloat16)).astype(jnp.float32)

@jax.custom_vjp
def low_back(v):
    return v

def low_keep(v):
    return (low(v), None)

def low_pass(kept, grad):
    return (grad,)

def back_keep(v):
    return (v, None)

def back_low(kept, grad):
    return (low(grad),)
low.defvjp(low_keep, low_pass)
low_back.defvjp(back_keep, back_low)
epsilon = 1e-05
excluded = -1e+30
highest = lax.Precision.HIGHEST

def token_groups(lengths):
    slot_span = 4 * SHORT
    position = jnp.arange(slot_span, dtype=jnp.int32)
    block_index = position // SHORT
    within = position % SHORT
    first_length = lengths[:, 0:1]
    selector = (block_index[:, None] == jnp.arange(4, dtype=jnp.int32)[None, :]).astype(jnp.int32)
    sub_length = lax.optimization_barrier(jnp.sum(selector[None, :, :] * lengths[:, None, :], axis=2))
    long_ids = jnp.where(position[None, :] < first_length, 0, 8)
    short_ids = jnp.where(within[None, :] < sub_length, block_index[None, :], block_index[None, :] + 4)
    return jnp.where(first_length > SHORT, long_ids, short_ids).astype(jnp.int32)

def layer_norm(values, norm_gain):
    centre = lax.optimization_barrier(jnp.mean(values, axis=-1, keepdims=True))
    spread = lax.optimization_barrier(jnp.mean(values * values, axis=-1, keepdims=True)) - centre * centre
    return (values - centre) * lax.rsqrt(spread + epsilon) * norm_gain

def exact_gelu(values):
    return jax.nn.gelu(values, approximate=False)

def matmul(left_side, right_side):
    return jnp.dot(left_side, right_side, precision=highest, preferred_element_type=jnp.float32)

def slot_attention(packed):
    queries, key_rows, value_rows, groups = packed
    slot_span = queries.shape[0]
    query_heads = queries.reshape(slot_span, HEADS, HEAD_DIM)
    key_heads = key_rows.reshape(slot_span, HEADS, HEAD_DIM)
    value_heads = value_rows.reshape(slot_span, HEADS, HEAD_DIM)
    scores = jnp.einsum('qhd,khd->hqk', query_heads, key_heads, precision=highest) * HEAD_DIM ** (-0.5)
    allowed = groups[:, None] == groups[None, :]
    scores = low_back(jnp.where(allowed[None], scores, excluded))
    soft_weights = low(jax.nn.softmax(scores, axis=-1))
    attended = jnp.einsum('hqk,khd->qhd', soft_weights, value_heads, precision=highest)
    return attended.reshape(slot_span, HEADS * HEAD_DIM)

def encoder_layer(inputs, norm1_gain, query_weight, query_bias, key_weight, value_weight, value_bias, inner_gain, output_weight, output_bias, norm2_gain, hidden_weight, hidden_bias, hidden_gain, project_weight, project_bias, groups):
    normed1 = low(layer_norm(inputs, norm1_gain))
    queries = low_back(low(matmul(normed1, query_weight) + query_bias))
    key_rows = low_back(low(matmul(normed1, key_weight)))
    value_rows = low_back(low(matmul(normed1, value_weight) + value_bias))
    slot_number = groups.shape[0]
    slot_span = groups.shape[1]
    attended = lax.map(jax.checkpoint(slot_attention), (queries.reshape(slot_number, slot_span, D), key_rows.reshape(slot_number, slot_span, D), value_rows.reshape(slot_number, slot_span, D), groups))
    attended = low_back(attended.reshape(slot_number * slot_span, D))
    context = low(layer_norm(attended, inner_gain))
    middle = inputs + low_back(matmul(context, output_weight) + output_bias)
    normed2 = low(layer_norm(middle, norm2_gain))
    hidden = low_back(matmul(normed2, hidden_weight) + hidden_bias)
    mixed_rows = low(layer_norm(exact_gelu(hidden), hidden_gain))
    return middle + low_back(matmul(mixed_rows, project_weight) + project_bias)

def reference(inputs, cotangent, lengths, norm1_gain, query_weight, query_bias, key_weight, value_weight, value_bias, inner_gain, output_weight, output_bias, norm2_gain, hidden_weight, hidden_bias, hidden_gain, project_weight, project_bias):
    groups = token_groups(lengths)
    floats = [array.astype(jnp.float32) for array in (inputs, norm1_gain, query_weight, query_bias, key_weight, value_weight, value_bias, inner_gain, output_weight, output_bias, norm2_gain, hidden_weight, hidden_bias, hidden_gain, project_weight, project_bias)]
    result, pullback = jax.vjp(functools.partial(encoder_layer, groups=groups), *floats)
    gradients = pullback(cotangent.astype(jnp.float32))
    return (result.astype(jnp.bfloat16), gradients[0], gradients[1], gradients[2], gradients[3], gradients[4], gradients[5], gradients[6], gradients[7], gradients[8], gradients[9], gradients[10], gradients[11], gradients[12], gradients[13], gradients[14], gradients[15])
```

```python
import functools
import math

import jax
import jax.numpy as jnp
from jax import lax
from jax.experimental import pallas as pl
from jax.experimental.pallas import tpu as pltpu
from jax.sharding import PartitionSpec as P

D = 768
HEAD_DIM = 64
FF = 3072
SHORT = 512
SLOT = 4 * SHORT

BF16 = jnp.bfloat16
F32 = jnp.float32
epsilon = 1e-05
excluded = 1e30
SCALE = HEAD_DIM ** (-0.5)
LOG2_SCALE = SCALE * math.log2(math.e)
LN2 = math.log(2.0)
QUERY_ROWS = 512
KEY_ROWS = 256
VMEM_LIMIT = 56 << 20


def nt(left, right):
    return lax.dot_general(left, right, (((1,), (1,)), ((), ())), preferred_element_type=F32)


def nn(left, right):
    return lax.dot_general(left, right, (((1,), (0,)), ((), ())), preferred_element_type=F32)


def tn(left, right):
    return lax.dot_general(left, right, (((0,), (0,)), ((), ())), preferred_element_type=F32)


def attention_forward_kernel(info, x0, x1, x2, x3, w_ref, b_ref, o_ref, lse_ref, q_ref, k_ref, v_ref):
    lane = lax.broadcasted_iota(jnp.int32, (SHORT, 128), 1)
    row = lax.broadcasted_iota(jnp.int32, (SHORT, 128), 0)
    for block, x_ref in enumerate((x0, x1, x2, x3)):
        rows = pl.ds(block * SHORT, SHORT)
        packed = (nn(x_ref[...], w_ref[0]) + b_ref[0]).astype(BF16)
        inside = jnp.where(row < info[1 + block], 1.0, 0.0).astype(F32)
        q_flags = jnp.where(lane == 0, inside, jnp.where(lane == 1, 1.0 - inside, 0.0))
        k_flags = jnp.where(
            lane == 0, (inside - 1.0) * excluded, jnp.where(lane == 1, inside * -excluded, 0.0)
        )
        q, k, v = packed[:, 0:64], packed[:, 64:128], packed[:, 128:192]
        scaled = k.astype(F32) * LOG2_SCALE
        high = scaled.astype(BF16)
        low = (scaled - high.astype(F32)).astype(BF16)
        q_ref[0, rows, :] = jnp.concatenate([q, q, q_flags.astype(BF16)], axis=1)
        k_ref[0, rows, :] = jnp.concatenate([high, low, k_flags.astype(BF16)], axis=1)
        v_ref[0, rows, :] = jnp.concatenate([v, jnp.ones((SHORT, 64), BF16)], axis=1)

    def block_of(start, keys):
        scores = nt(q_ref[0, pl.ds(start, QUERY_ROWS), :], k_ref[0, keys, :])
        top = jnp.max(scores, axis=1, keepdims=True)
        weights = jnp.exp2(scores - top).astype(BF16)
        out = nn(weights, v_ref[0, keys, :])
        out_lane = lax.broadcasted_iota(jnp.int32, (QUERY_ROWS, 128), 1)
        out = jnp.where(out_lane == 65, jnp.broadcast_to(top, (QUERY_ROWS, 128)), out).T
        total = out[64:65]
        o_ref[start // SHORT, :, pl.ds(start % SHORT, QUERY_ROWS)] = (
            out[0:64] * (1.0 / total)
        ).astype(BF16)
        lse_ref[0, :, pl.ds(start, QUERY_ROWS)] = out[65:66] + jnp.log2(total)

    longer = info[0] > SHORT

    @pl.when(longer)
    def _():
        for start in range(0, SLOT, QUERY_ROWS):
            block_of(start, pl.ds(0, SLOT))

    @pl.when(jnp.logical_not(longer))
    def _():
        for start in range(0, SLOT, QUERY_ROWS):
            block_of(start, pl.ds(start // SHORT * SHORT, SHORT))


def head_spec(*shape):
    return pl.BlockSpec((1,) + shape, lambda h, info: (h,) + (0,) * len(shape))


def whole_spec(*shape):
    return pl.BlockSpec(shape, lambda h, info: (0,) * len(shape))


def attention_forward(info, rows, weights, biases):
    heads = weights.shape[0]
    return pl.pallas_call(
        attention_forward_kernel,
        grid_spec=pltpu.PrefetchScalarGridSpec(
            num_scalar_prefetch=1,
            grid=(heads,),
            in_specs=[whole_spec(SHORT, D)] * 4 + [head_spec(D, 192), head_spec(1, 192)],
            out_specs=[
                pl.BlockSpec((4, HEAD_DIM, SHORT), lambda h, info: (0, h, 0)),
                head_spec(1, SLOT),
                head_spec(SLOT, 256),
                head_spec(SLOT, 256),
                head_spec(SLOT, 128),
            ],
        ),
        out_shape=[
            jax.ShapeDtypeStruct((4, heads * HEAD_DIM, SHORT), BF16),
            jax.ShapeDtypeStruct((heads, 1, SLOT), F32),
            jax.ShapeDtypeStruct((heads, SLOT, 256), BF16),
            jax.ShapeDtypeStruct((heads, SLOT, 256), BF16),
            jax.ShapeDtypeStruct((heads, SLOT, 128), BF16),
        ],
        compiler_params=pltpu.CompilerParams(
            dimension_semantics=("arbitrary",), vmem_limit_bytes=VMEM_LIMIT
        ),
        cost_estimate=pl.CostEstimate(
            flops=24_000_000_000, bytes_accessed=12_000_000, transcendentals=12_000_000
        ),
        name="attention_forward",
    )(info, *rows, weights, biases)


def attention_backward_kernel(
    info, g0, g1, g2, g3, o_ref, lse_ref, q_ref, k_ref, v_ref, w_ref, x0, x1, x2, x3,
    dx_ref, dw_ref, db_ref, grad, dq, delta, packed, dx,
):
    head = pl.program_id(0)
    for block, g_ref in enumerate((g0, g1, g2, g3)):
        g = g_ref[...].astype(F32)
        cols = pl.ds(block * SHORT, SHORT)
        delta[:, cols] = jnp.sum(g * o_ref[block].astype(F32), axis=0, keepdims=True)
        grad[cols, :] = g.T.astype(BF16)

    def block_of(start, queries, first):
        rows = pl.ds(start, KEY_ROWS)
        k = k_ref[0, rows, :]
        q = q_ref[0, queries, :]
        g = grad[queries, :]
        weights = jnp.exp2(nt(k, q) - lse_ref[0, :, queries])
        d_probs = nt(v_ref[0, rows, 0:64], g)
        d_scores = (weights * (d_probs - delta[:, queries])).astype(BF16)
        packed[rows, 128:192] = nn(weights.astype(BF16), g).astype(BF16)
        packed[rows, 64:128] = (nn(d_scores, q[:, 0:128])[:, 0:64] * SCALE).astype(BF16)
        term = tn(d_scores, k[:, 0:128])
        if first:
            dq[queries, :] = term
        else:
            dq[queries, :] += term

    longer = info[0] > SHORT

    @pl.when(longer)
    def _():
        for start in range(0, SLOT, KEY_ROWS):
            block_of(start, pl.ds(0, SLOT), start == 0)

    @pl.when(jnp.logical_not(longer))
    def _():
        for start in range(0, SLOT, KEY_ROWS):
            block_of(start, pl.ds(start // SHORT * SHORT, SHORT), start % SHORT == 0)

    total = dq[...]
    packed[:, 0:64] = ((total[:, 0:64] + total[:, 64:128]) * LN2).astype(BF16)
    d_weight = jnp.zeros((192, D), F32)
    d_bias = jnp.zeros((1, 192), F32)
    for block, x_ref in enumerate((x0, x1, x2, x3)):
        rows = pl.ds(block * SHORT, SHORT)
        part = packed[rows, :]
        d_weight += tn(part, x_ref[...])
        d_bias += jnp.sum(part.astype(F32), axis=0, keepdims=True)
        term = nt(part, w_ref[0])

        @pl.when(head == 0)
        def _():
            dx[rows, :] = term

        @pl.when(head != 0)
        def _():
            dx[rows, :] += term

        @pl.when(head == pl.num_programs(0) - 1)
        def _():
            dx_ref[block] = dx[rows, :].astype(BF16)

    dw_ref[0] = d_weight.T
    db_ref[0] = d_bias


def attention_backward(info, grads, attended, lse, queries, keys, values, weights, rows):
    heads = weights.shape[0]
    grad_spec = pl.BlockSpec((HEAD_DIM, SHORT), lambda h, info: (h, 0))
    return pl.pallas_call(
        attention_backward_kernel,
        grid_spec=pltpu.PrefetchScalarGridSpec(
            num_scalar_prefetch=1,
            grid=(heads,),
            in_specs=[grad_spec] * 4
            + [
                pl.BlockSpec((4, HEAD_DIM, SHORT), lambda h, info: (0, h, 0)),
                head_spec(1, SLOT),
                head_spec(SLOT, 256),
                head_spec(SLOT, 256),
                head_spec(SLOT, 128),
                head_spec(D, 192),
            ]
            + [whole_spec(SHORT, D)] * 4,
            out_specs=[whole_spec(4, SHORT, D), head_spec(D, 192), head_spec(1, 192)],
            scratch_shapes=[
                pltpu.VMEM((SLOT, HEAD_DIM), BF16),
                pltpu.VMEM((SLOT, 128), F32),
                pltpu.VMEM((1, SLOT), F32),
                pltpu.VMEM((SLOT, 192), BF16),
                pltpu.VMEM((SLOT, D), F32),
            ],
        ),
        out_shape=[
            jax.ShapeDtypeStruct((4, SHORT, D), BF16),
            jax.ShapeDtypeStruct((heads, D, 192), F32),
            jax.ShapeDtypeStruct((heads, 1, 192), F32),
        ],
        compiler_params=pltpu.CompilerParams(
            dimension_semantics=("arbitrary",), vmem_limit_bytes=VMEM_LIMIT
        ),
        cost_estimate=pl.CostEstimate(
            flops=44_000_000_000, bytes_accessed=14_000_000, transcendentals=12_000_000
        ),
        name="attention_backward",
    )(info, *grads, attended, lse, queries, keys, values, weights, *rows)


def normed(values, axis):
    centre = jnp.mean(values, axis=axis, keepdims=True)
    spread = jnp.mean(values * values, axis=axis, keepdims=True) - centre * centre
    scaling = lax.rsqrt(spread + epsilon)
    return (values - centre) * scaling, scaling


def norm_back(scaled, unit, scaling, axis):
    first = jnp.mean(scaled, axis=axis, keepdims=True)
    second = jnp.mean(scaled * unit, axis=axis, keepdims=True)
    return scaling * (scaled - first - unit * second)


def swap(values, distance):
    count = lax.axis_size("head")
    return lax.ppermute(values, "head", [(i, i ^ distance) for i in range(count)])


def local(
    inputs,
    cotangent,
    lengths,
    norm1_gain,
    query_weight,
    query_bias,
    key_weight,
    value_weight,
    value_bias,
    inner_gain,
    output_weight,
    output_bias,
    norm2_gain,
    hidden_weight,
    hidden_bias,
    hidden_gain,
    project_weight,
    project_bias,
):
    everywhere = ("dp", "head")
    dp_count = lax.axis_size("dp")
    me = lax.axis_index("head")
    heads = query_weight.shape[1] // HEAD_DIM
    shard_rows = hidden_weight.shape[0]
    slice_cols = hidden_weight.shape[1]

    first_length = lengths[0, 0]
    limits = [
        jnp.where(first_length > SHORT, first_length - SHORT * (me ^ r), lengths[0, me ^ r])
        for r in range(4)
    ]
    info = jnp.stack([first_length] + limits).astype(jnp.int32)

    shards = jnp.concatenate([hidden_weight, project_weight.T], axis=0)
    gathered = lax.all_gather(shards, everywhere, axis=0, tiled=False)
    gathered = gathered.reshape(dp_count, 4, 2, shard_rows, slice_cols)

    def whole_weight(which):
        return gathered[:, :, which].transpose(0, 2, 1, 3).reshape(D, FF)

    weight_in, weight_out = whole_weight(0), whole_weight(1)
    vectors = lax.all_gather(jnp.stack([hidden_bias, hidden_gain]), "head", axis=1, tiled=True)
    hidden_bias_all = vectors[0].astype(F32)
    hidden_gain_all = vectors[1].astype(F32)

    input_share = inputs.astype(F32)
    unit1, scaling1 = normed(input_share, 1)
    gain1 = norm1_gain.astype(F32)
    normed1 = (unit1 * gain1).astype(BF16)
    near = swap(normed1, 1)
    across = swap(normed1, 2)
    far = swap(across, 1)
    rows = (normed1, near, across, far)

    def per_head(weight):
        return weight.reshape(-1, heads, HEAD_DIM)

    zero_bias = jnp.zeros_like(query_bias)
    packed_weight = jnp.concatenate(
        [per_head(query_weight), per_head(key_weight), per_head(value_weight)], axis=2
    ).transpose(1, 0, 2)
    packed_bias = (
        jnp.concatenate(
            [b.reshape(heads, 1, HEAD_DIM) for b in (query_bias, zero_bias, value_bias)], axis=2
        )
    ).astype(F32)
    attended_heads, lse, queries, keys, values = attention_forward(
        info, rows, packed_weight, packed_bias
    )

    def exchange(pieces):
        return [pieces[0]] + [swap(pieces[r], r) for r in (1, 2, 3)]

    attended = jnp.concatenate(exchange([attended_heads[r] for r in range(4)]), axis=0).astype(F32)
    out_near = swap(output_weight, 1)
    out_across = swap(output_weight, 2)
    out_far = swap(out_across, 1)
    out_weight = jnp.concatenate([output_weight, out_near, out_across, out_far], axis=0)
    inner_all = jnp.concatenate([inner_gain] + [swap(inner_gain, r) for r in (1, 2, 3)])
    inner_all = inner_all.astype(F32)[:, None]

    unit_c, scaling_c = normed(attended, 0)
    context = (unit_c * inner_all).astype(BF16)
    branch = tn(context, out_weight)
    middle = input_share + (branch + output_bias.astype(F32))
    unit2, scaling2 = normed(middle, 1)
    gain2 = norm2_gain.astype(F32)
    normed2 = (unit2 * gain2).astype(BF16)

    hidden = nn(normed2, weight_in) + hidden_bias_all
    activated, gelu_pull = jax.vjp(lambda v: jax.nn.gelu(v, approximate=False), hidden)
    unit_h, scaling_h = normed(activated, 1)
    mixed = (unit_h * hidden_gain_all).astype(BF16)
    projected = nt(mixed, weight_out)
    output = (middle + (projected + project_bias.astype(F32))).astype(BF16)

    d_output = cotangent.astype(F32)
    project_bias_part = jnp.sum(d_output, axis=0)
    project_part = tn(cotangent, mixed)
    d_mixed = nn(cotangent, weight_out)
    hidden_gain_part = jnp.sum(d_mixed * unit_h, axis=0)
    d_activated = norm_back(d_mixed * hidden_gain_all, unit_h, scaling_h, 1)
    d_hidden = gelu_pull(d_activated)[0].astype(BF16)
    hidden_bias_part = jnp.sum(d_hidden.astype(F32), axis=0)
    hidden_part = tn(normed2, d_hidden)
    d_normed2 = nt(d_hidden, weight_in)
    norm2_part = jnp.sum(d_normed2 * unit2, axis=0)
    d_middle = d_output + norm_back(d_normed2 * gain2, unit2, scaling2, 1)
    d_branch = d_middle.astype(BF16)
    output_bias_part = jnp.sum(d_branch.astype(F32), axis=0)

    d_context = nt(out_weight, d_branch)
    out_part = nn(context, d_branch)
    inner_part = jnp.sum(d_context * unit_c, axis=1)
    d_attended = norm_back(d_context * inner_all, unit_c, scaling_c, 0).astype(BF16)
    pieces = d_attended.reshape(4, -1, SHORT)
    grads = exchange([pieces[r] for r in range(4)])

    def owned(part):
        blocks = part.astype(BF16).reshape(dp_count, shard_rows, 4, slice_cols)
        return blocks.transpose(0, 2, 1, 3)

    both = jnp.stack([owned(hidden_part), owned(project_part)], axis=2)
    both = both.reshape(dp_count * 4 * 2 * shard_rows, slice_cols)
    both = lax.psum_scatter(both, everywhere, scatter_dimension=0, tiled=True).astype(F32)
    hidden_grad, project_grad = both[:shard_rows], both[shard_rows:].T

    d_rows, d_weight, d_bias = attention_backward(
        info, grads, attended_heads, lse, queries, keys, values, packed_weight, rows
    )
    near_rows = swap(d_rows[1::2], 1)
    own_sum = d_rows[0].astype(F32) + near_rows[0].astype(F32)
    across_sum = (d_rows[2].astype(F32) + near_rows[1].astype(F32)).astype(BF16)
    d_normed1 = own_sum + swap(across_sum, 2).astype(F32)
    norm1_part = jnp.sum(d_normed1 * unit1, axis=0)
    input_grad = d_middle + norm_back(d_normed1 * gain1, unit1, scaling1, 1)

    out_pieces = out_part.reshape(4, -1, D).astype(BF16)
    out_near_part = swap(out_pieces[1::2], 1)
    out_own = out_pieces[0].astype(F32) + out_near_part[0].astype(F32)
    out_cross = (out_pieces[2].astype(F32) + out_near_part[1].astype(F32)).astype(BF16)
    out_own = out_own + swap(out_cross, 2).astype(F32)

    weight_totals = lax.psum((d_weight, out_own), "dp")
    by_kind = weight_totals[0].reshape(heads, D, 3, HEAD_DIM).transpose(2, 1, 0, 3)
    by_kind = by_kind.reshape(3, D, heads * HEAD_DIM)
    bias_total = lax.psum(d_bias, "dp").reshape(heads, 3, HEAD_DIM)

    shared = lax.psum(
        (
            norm1_part,
            norm2_part,
            project_bias_part,
            output_bias_part,
            hidden_gain_part,
            hidden_bias_part,
        ),
        everywhere,
    )
    own_cols = lambda v: lax.dynamic_slice_in_dim(v, me * slice_cols, slice_cols)
    inner_blocks = inner_part.reshape(4, -1)
    inner_own = inner_blocks[0] + sum(swap(inner_blocks[r], r) for r in (1, 2, 3))
    inner_total = lax.psum(inner_own, "dp")
    return (
        output,
        input_grad,
        shared[0],
        by_kind[0],
        bias_total[:, 0].reshape(-1),
        by_kind[1],
        by_kind[2],
        bias_total[:, 2].reshape(-1),
        inner_total,
        weight_totals[1],
        shared[3],
        shared[1],
        hidden_grad,
        own_cols(shared[5]),
        own_cols(shared[4]),
        project_grad,
        shared[2],
    )


def solution(mesh):
    rows = P(("dp", "head"), None)
    columns = P(None, "head")
    head = P("head")
    return jax.shard_map(
        local,
        mesh=mesh,
        in_specs=(
            rows, rows, P("dp", None), P(), columns, head, columns, columns, head, head,
            P("head", None), P(), P(), P("dp", "head"), head, head, P("head", "dp"), P(),
        ),
        out_specs=(
            rows, rows, P(), columns, head, columns, columns, head, head, P("head", None),
            P(), P(), P("dp", "head"), head, head, P("head", "dp"), P(),
        ),
        check_vma=False,
    )
```

```python
import functools
import math

import jax
import jax.numpy as jnp
from jax import lax
from jax.experimental import pallas as pl
from jax.experimental.pallas import tpu as pltpu
from jax.sharding import PartitionSpec as P

D = 768
HEAD_DIM = 64
FF = 3072
SHORT = 512
SLOT = 4 * SHORT

BF16 = jnp.bfloat16
F32 = jnp.float32
epsilon = 1e-05
excluded = 1e30
SCALE = HEAD_DIM ** (-0.5)
LOG2_SCALE = SCALE * math.log2(math.e)
LN2 = math.log(2.0)
QUERY_ROWS = 512
KEY_ROWS = 256
VMEM_LIMIT = 56 << 20


def nt(left, right):
    return lax.dot_general(left, right, (((1,), (1,)), ((), ())), preferred_element_type=F32)


def nn(left, right):
    return lax.dot_general(left, right, (((1,), (0,)), ((), ())), preferred_element_type=F32)


def tn(left, right):
    return lax.dot_general(left, right, (((0,), (0,)), ((), ())), preferred_element_type=F32)


def attention_forward_kernel(info, x0, x1, x2, x3, w_ref, b_ref, o_ref, lse_ref, q_ref, k_ref, v_ref):
    lane = lax.broadcasted_iota(jnp.int32, (SHORT, 128), 1)
    row = lax.broadcasted_iota(jnp.int32, (SHORT, 128), 0)
    for block, x_ref in enumerate((x0, x1, x2, x3)):
        rows = pl.ds(block * SHORT, SHORT)
        packed = (nn(x_ref[...], w_ref[0]) + b_ref[0]).astype(BF16)
        inside = jnp.where(row < info[1 + block], 1.0, 0.0).astype(F32)
        q_flags = jnp.where(lane == 0, inside, jnp.where(lane == 1, 1.0 - inside, 0.0))
        k_flags = jnp.where(
            lane == 0, (inside - 1.0) * excluded, jnp.where(lane == 1, inside * -excluded, 0.0)
        )
        q, k, v = packed[:, 0:64], packed[:, 64:128], packed[:, 128:192]
        scaled = k.astype(F32) * LOG2_SCALE
        high = scaled.astype(BF16)
        low = (scaled - high.astype(F32)).astype(BF16)
        q_ref[0, rows, :] = jnp.concatenate([q, q, q_flags.astype(BF16)], axis=1)
        k_ref[0, rows, :] = jnp.concatenate([high, low, k_flags.astype(BF16)], axis=1)
        v_ref[0, rows, :] = jnp.concatenate([v, jnp.ones((SHORT, 64), BF16)], axis=1)

    def block_of(start, keys):
        scores = nt(q_ref[0, pl.ds(start, QUERY_ROWS), :], k_ref[0, keys, :])
        top = jnp.max(scores, axis=1, keepdims=True)
        weights = jnp.exp2(scores - top).astype(BF16)
        out = nn(weights, v_ref[0, keys, :])
        out_lane = lax.broadcasted_iota(jnp.int32, (QUERY_ROWS, 128), 1)
        out = jnp.where(out_lane == 65, jnp.broadcast_to(top, (QUERY_ROWS, 128)), out).T
        total = out[64:65]
        o_ref[start // SHORT, :, pl.ds(start % SHORT, QUERY_ROWS)] = (
            out[0:64] * (1.0 / total)
        ).astype(BF16)
        lse_ref[0, :, pl.ds(start, QUERY_ROWS)] = out[65:66] + jnp.log2(total)

    longer = info[0] > SHORT

    @pl.when(longer)
    def _():
        for start in range(0, SLOT, QUERY_ROWS):
            block_of(start, pl.ds(0, SLOT))

    @pl.when(jnp.logical_not(longer))
    def _():
        for start in range(0, SLOT, QUERY_ROWS):
            block_of(start, pl.ds(start // SHORT * SHORT, SHORT))


def head_spec(*shape):
    return pl.BlockSpec((1,) + shape, lambda h, info: (h,) + (0,) * len(shape))


def whole_spec(*shape):
    return pl.BlockSpec(shape, lambda h, info: (0,) * len(shape))


def attention_forward(info, rows, weights, biases):
    heads = weights.shape[0]
    return pl.pallas_call(
        attention_forward_kernel,
        grid_spec=pltpu.PrefetchScalarGridSpec(
            num_scalar_prefetch=1,
            grid=(heads,),
            in_specs=[whole_spec(SHORT, D)] * 4 + [head_spec(D, 192), head_spec(1, 192)],
            out_specs=[
                pl.BlockSpec((4, HEAD_DIM, SHORT), lambda h, info: (0, h, 0)),
                head_spec(1, SLOT),
                head_spec(SLOT, 256),
                head_spec(SLOT, 256),
                head_spec(SLOT, 128),
            ],
        ),
        out_shape=[
            jax.ShapeDtypeStruct((4, heads * HEAD_DIM, SHORT), BF16),
            jax.ShapeDtypeStruct((heads, 1, SLOT), F32),
            jax.ShapeDtypeStruct((heads, SLOT, 256), BF16),
            jax.ShapeDtypeStruct((heads, SLOT, 256), BF16),
            jax.ShapeDtypeStruct((heads, SLOT, 128), BF16),
        ],
        compiler_params=pltpu.CompilerParams(
            dimension_semantics=("arbitrary",), vmem_limit_bytes=VMEM_LIMIT
        ),
        cost_estimate=pl.CostEstimate(
            flops=24_000_000_000, bytes_accessed=12_000_000, transcendentals=12_000_000
        ),
        name="attention_forward",
    )(info, *rows, weights, biases)


def attention_backward_kernel(
    info, g0, g1, g2, g3, o_ref, lse_ref, q_ref, k_ref, v_ref, w_ref, x0, x1, x2, x3,
    dx_ref, dw_ref, grad, dq, delta, packed, dx,
):
    head = pl.program_id(0)
    for block, g_ref in enumerate((g0, g1, g2, g3)):
        g = g_ref[...].astype(F32)
        cols = pl.ds(block * SHORT, SHORT)
        delta[:, cols] = jnp.sum(g * o_ref[block].astype(F32), axis=0, keepdims=True)
        grad[cols, :] = g.T.astype(BF16)

    def block_of(start, queries, first):
        rows = pl.ds(start, KEY_ROWS)
        k = k_ref[0, rows, :]
        q = q_ref[0, queries, :]
        g = grad[queries, :]
        weights = jnp.exp2(nt(k, q) - lse_ref[0, :, queries])
        d_probs = nt(v_ref[0, rows, 0:64], g)
        d_scores = (weights * (d_probs - delta[:, queries])).astype(BF16)
        packed[rows, 128:192] = nn(weights.astype(BF16), g).astype(BF16)
        packed[rows, 64:128] = (nn(d_scores, q[:, 0:128])[:, 0:64] * SCALE).astype(BF16)
        term = tn(d_scores, k[:, 0:128])
        if first:
            dq[queries, :] = term
        else:
            dq[queries, :] += term

    longer = info[0] > SHORT

    @pl.when(longer)
    def _():
        for start in range(0, SLOT, KEY_ROWS):
            block_of(start, pl.ds(0, SLOT), start == 0)

    @pl.when(jnp.logical_not(longer))
    def _():
        for start in range(0, SLOT, KEY_ROWS):
            block_of(start, pl.ds(start // SHORT * SHORT, SHORT), start % SHORT == 0)

    total = dq[...]
    packed[:, 0:64] = ((total[:, 0:64] + total[:, 64:128]) * LN2).astype(BF16)
    d_weight = jnp.zeros((192, D), F32)
    d_bias = jnp.zeros((192, 128), F32)
    ones = jnp.ones((SHORT, 128), BF16)
    for block, x_ref in enumerate((x0, x1, x2, x3)):
        rows = pl.ds(block * SHORT, SHORT)
        part = packed[rows, :]
        d_weight += tn(part, x_ref[...])
        d_bias += tn(part, ones)
        term = nt(part, w_ref[0])

        @pl.when(head == 0)
        def _():
            dx[rows, :] = term

        @pl.when(head != 0)
        def _():
            dx[rows, :] += term

        @pl.when(head == pl.num_programs(0) - 1)
        def _():
            dx_ref[block] = dx[rows, :].astype(BF16)

    d_weight = d_weight.T
    gain_term = jnp.sum(w_ref[0].astype(F32) * d_weight, axis=1, keepdims=True)
    lane = lax.broadcasted_iota(jnp.int32, (D, HEAD_DIM), 1)
    d_bias = jnp.concatenate([d_bias[:, 0:HEAD_DIM], jnp.zeros((D - 192, HEAD_DIM), F32)], axis=0)
    extra = jnp.where(lane == 0, gain_term, jnp.where(lane == 1, d_bias, 0.0))
    dw_ref[0] = jnp.concatenate([d_weight, extra], axis=1).astype(BF16)


def attention_backward(info, grads, attended, lse, queries, keys, values, weights, rows):
    heads = weights.shape[0]
    grad_spec = pl.BlockSpec((HEAD_DIM, SHORT), lambda h, info: (h, 0))
    return pl.pallas_call(
        attention_backward_kernel,
        grid_spec=pltpu.PrefetchScalarGridSpec(
            num_scalar_prefetch=1,
            grid=(heads,),
            in_specs=[grad_spec] * 4
            + [
                pl.BlockSpec((4, HEAD_DIM, SHORT), lambda h, info: (0, h, 0)),
                head_spec(1, SLOT),
                head_spec(SLOT, 256),
                head_spec(SLOT, 256),
                head_spec(SLOT, 128),
                head_spec(D, 192),
            ]
            + [whole_spec(SHORT, D)] * 4,
            out_specs=[whole_spec(4, SHORT, D), head_spec(D, 256)],
            scratch_shapes=[
                pltpu.VMEM((SLOT, HEAD_DIM), BF16),
                pltpu.VMEM((SLOT, 128), F32),
                pltpu.VMEM((1, SLOT), F32),
                pltpu.VMEM((SLOT, 192), BF16),
                pltpu.VMEM((SLOT, D), F32),
            ],
        ),
        out_shape=[
            jax.ShapeDtypeStruct((4, SHORT, D), BF16),
            jax.ShapeDtypeStruct((heads, D, 256), BF16),
        ],
        compiler_params=pltpu.CompilerParams(
            dimension_semantics=("arbitrary",), vmem_limit_bytes=VMEM_LIMIT
        ),
        cost_estimate=pl.CostEstimate(
            flops=44_000_000_000, bytes_accessed=14_000_000, transcendentals=12_000_000
        ),
        name="attention_backward",
    )(info, *grads, attended, lse, queries, keys, values, weights, *rows)


def rows_normed(values):
    centre = jnp.mean(values, axis=1, keepdims=True)
    spread = jnp.mean(values * values, axis=1, keepdims=True) - centre * centre
    scaling = lax.rsqrt(spread + epsilon)
    return (values - centre) * scaling, scaling


def rows_back(scaled, unit, scaling):
    first = jnp.mean(scaled, axis=1, keepdims=True)
    second = jnp.mean(scaled * unit, axis=1, keepdims=True)
    return scaling * (scaled - first - unit * second)


def lanes_folded(values):
    return sum(values[:, c : c + 128] for c in range(0, values.shape[1], 128))


def token_kernel(
    info, a0, a1, a2, a3, p0, p1, p2, p3, x_ref, cot_ref, vec_ref, w_in, w_out,
    out_ref, middle_grad_ref, attended_grad_ref, in_keep, in_send, out_keep, out_send, o_grad_ref, vec_out_ref,
    attended, unit_c, context, weight_o, middle, normed2, unit2, flipped, cot_flipped, activated, slope, d_mixed,
    fold_a, fold_b, fold_c, fold_d, projected, d_normed2, columns,
):
    step = pl.program_id(0)
    phase = step // 4
    r = jnp.where(phase == 2, 3 - step % 4, step % 4)
    tokens = x_ref.shape[0]
    ff_slice = w_in.shape[-1]
    ff = 4 * ff_slice
    packs = (p0, p1, p2, p3)
    inner_rows = a0.shape[0]

    def col(name):
        return columns[:, name : name + 1]

    def set_col(name, value):
        columns[:, name : name + 1] = value

    @pl.when(step == 0)
    def _():
        for i, a_ref in enumerate((a0, a1, a2, a3)):
            attended[i * inner_rows : (i + 1) * inner_rows, :] = a_ref[...].astype(F32)
            weight_o[i * inner_rows : (i + 1) * inner_rows, :] = packs[i][0:inner_rows, 0:D]
        values = attended[...]
        centre = jnp.mean(values, axis=0, keepdims=True)
        spread = jnp.mean(values * values, axis=0, keepdims=True) - centre * centre
        scaling = lax.rsqrt(spread + epsilon)
        unit = (values - centre) * scaling
        unit_c[...] = unit
        attended[0:1, :] = scaling
        for i in range(4):
            part = slice(i * inner_rows, (i + 1) * inner_rows)
            gain = packs[i][0:inner_rows, D : D + 1].astype(F32)
            context[part, :] = (unit[part] * gain).astype(BF16)
        branch = tn(context[...], weight_o[...])
        total = x_ref[...].astype(F32) + (branch + vec_ref[0:1, :])
        middle[...] = total
        unit, scaling = rows_normed(total)
        unit2[...] = unit
        set_col(0, scaling)
        scaled = (unit * vec_ref[1:2, :]).astype(BF16)
        normed2[...] = scaled
        flipped[...] = scaled.T
        cot_flipped[...] = cot_ref[...].T
        for ref in (fold_a, fold_b, fold_c, fold_d, projected, d_normed2):
            ref[...] = jnp.zeros_like(ref)

    def pack_row(row):
        value = packs[0][inner_rows : inner_rows + 16, 0:ff_slice].astype(F32)
        for i in range(1, 4):
            other = packs[i][inner_rows : inner_rows + 16, 0:ff_slice].astype(F32)
            value = jnp.where(r == i, other, value)
        return value[row : row + 1]

    def weight(ref):
        return ref[...].reshape(D, ff_slice)

    @pl.when(phase == 0)
    def _():
        hidden = nn(normed2[...], weight(w_in)) + pack_row(0)
        density = jnp.exp(hidden * hidden * -0.5) * (1.0 / math.sqrt(2.0 * math.pi))
        share = 0.5 * (1.0 + lax.erf(hidden * math.sqrt(0.5)))
        value = hidden * share
        activated[r] = value
        slope[r] = share + hidden * density
        fold_a[...] += lanes_folded(value)
        fold_b[...] += lanes_folded(value * value)

    @pl.when(step == 4)
    def _():
        centre = jnp.sum(fold_a[...], axis=1, keepdims=True) * (1.0 / ff)
        spread = jnp.sum(fold_b[...], axis=1, keepdims=True) * (1.0 / ff) - centre * centre
        set_col(1, centre)
        set_col(2, lax.rsqrt(spread + epsilon))

    @pl.when(phase == 1)
    def _():
        gain = pack_row(1)
        unit = (activated[r] - col(1)) * col(2)
        mixed = (unit * gain).astype(BF16)
        projected[...] += nt(mixed, weight(w_out))
        part = nn(cot_flipped[...], mixed).astype(BF16)

        @pl.when(r % 2 == 0)
        def _():
            out_keep[0] = part

        @pl.when(r % 2 == 1)
        def _():
            out_send[0] = part

        grad = nn(cot_ref[...], weight(w_out))
        vec_out_ref[r, 0:1, :] = jnp.sum(grad * unit, axis=0, keepdims=True)
        scaled = grad * gain
        d_mixed[r] = scaled
        fold_c[...] += lanes_folded(scaled)
        fold_d[...] += lanes_folded(scaled * unit)

    @pl.when(step == 8)
    def _():
        set_col(3, jnp.sum(fold_c[...], axis=1, keepdims=True) * (1.0 / ff))
        set_col(4, jnp.sum(fold_d[...], axis=1, keepdims=True) * (1.0 / ff))
        out_ref[...] = (middle[...] + (projected[...] + vec_ref[2:3, :])).astype(BF16)

    @pl.when(phase == 2)
    def _():
        unit = (activated[r] - col(1)) * col(2)
        grad = (slope[r] * (col(2) * (d_mixed[r] - col(3) - unit * col(4)))).astype(BF16)
        vec_out_ref[r, 1:2, :] = jnp.sum(grad.astype(F32), axis=0, keepdims=True)
        part = nn(flipped[...], grad).astype(BF16)

        @pl.when(r % 2 == 0)
        def _():
            in_keep[0] = part

        @pl.when(r % 2 == 1)
        def _():
            in_send[0] = part

        d_normed2[...] += nt(grad, weight(w_in))

    @pl.when(step == 11)
    def _():
        cot = cot_ref[...].astype(F32)
        grad = d_normed2[...]
        unit = unit2[...]
        d_middle = cot + rows_back(grad * vec_ref[1:2, :], unit, col(0))
        middle_grad_ref[...] = d_middle
        d_branch = d_middle.astype(BF16)
        norm2_part = jnp.sum(grad * unit, axis=0, keepdims=True)
        project_bias_part = jnp.sum(cot, axis=0, keepdims=True)
        output_bias_part = jnp.sum(d_branch.astype(F32), axis=0, keepdims=True)
        d_context = nt(weight_o[...], d_branch)
        o_grad_ref[...] = nn(context[...], d_branch).astype(BF16).reshape(o_grad_ref.shape)
        unit = unit_c[...]
        inner_part = jnp.sum(d_context * unit, axis=1, keepdims=True)
        inner_part = jnp.broadcast_to(inner_part, (D, 128)).T[0:1]
        first = jnp.zeros((1, tokens), F32)
        second = jnp.zeros((1, tokens), F32)
        for i in range(4):
            rows = slice(i * inner_rows, (i + 1) * inner_rows)
            scaled = d_context[rows] * packs[i][0:inner_rows, D : D + 1].astype(F32)
            first += jnp.sum(scaled, axis=0, keepdims=True)
            second += jnp.sum(scaled * unit[rows], axis=0, keepdims=True)
        first, second = first * (1.0 / D), second * (1.0 / D)
        scaling = attended[0:1, :]
        for i in range(4):
            rows = slice(i * inner_rows, (i + 1) * inner_rows)
            scaled = d_context[rows] * packs[i][0:inner_rows, D : D + 1].astype(F32)
            attended_grad_ref[i] = (scaling * (scaled - first - unit[rows] * second)).astype(BF16)
            vec_out_ref[i, 2:3, 0:inner_rows] = inner_part[:, rows]
            vec_out_ref[i, 2:3, inner_rows:D] = jnp.zeros((1, D - inner_rows), F32)
            vec_out_ref[i, 3:4, :] = norm2_part
            vec_out_ref[i, 4:5, :] = project_bias_part
            vec_out_ref[i, 5:6, :] = output_bias_part
            vec_out_ref[i, 6:8, :] = jnp.zeros((2, D), F32)


def token_section(info, attended, packs, inputs, cotangent, vectors, gathered):
    tokens = inputs.shape[0]
    inner_rows = attended[0].shape[0]
    count, _, _, shard_rows, ff_slice = gathered.shape
    fixed = lambda *shape: pl.BlockSpec(shape, lambda s, info: (0,) * len(shape))

    def weight_spec(which, pick):
        return pl.BlockSpec(
            (count, None, None, shard_rows, ff_slice), lambda s, info: (0, info[5] ^ pick(s), which, 0, 0)
        )

    first_pick = lambda s: jnp.where(s < 4, s, jnp.where(s < 8, 3, 11 - s))
    second_pick = lambda s: jnp.clip(s - 4, 0, 3)
    in_pick = lambda s: jnp.clip(11 - s, 0, 3)
    kept = lambda pick: pl.BlockSpec((1, D, ff_slice), lambda s, info: (pick(s) // 2, 0, 0))
    return pl.pallas_call(
        token_kernel,
        grid_spec=pltpu.PrefetchScalarGridSpec(
            num_scalar_prefetch=1,
            grid=(12,),
            in_specs=[fixed(*a.shape) for a in attended]
            + [fixed(*p.shape) for p in packs]
            + [fixed(tokens, D), fixed(tokens, D), fixed(8, D)]
            + [weight_spec(0, first_pick), weight_spec(1, second_pick)],
            out_specs=[
                fixed(tokens, D),
                fixed(tokens, D),
                fixed(4, inner_rows, tokens),
                kept(in_pick),
                kept(in_pick),
                kept(second_pick),
                kept(second_pick),
                fixed(4, inner_rows, D),
                fixed(4, 8, D),
            ],
            scratch_shapes=[
                pltpu.VMEM((D, tokens), F32),
                pltpu.VMEM((D, tokens), F32),
                pltpu.VMEM((D, tokens), BF16),
                pltpu.VMEM((D, D), BF16),
                pltpu.VMEM((tokens, D), F32),
                pltpu.VMEM((tokens, D), BF16),
                pltpu.VMEM((tokens, D), F32),
                pltpu.VMEM((D, tokens), BF16),
                pltpu.VMEM((D, tokens), BF16),
                pltpu.VMEM((4, tokens, ff_slice), F32),
                pltpu.VMEM((4, tokens, ff_slice), F32),
                pltpu.VMEM((4, tokens, ff_slice), F32),
                pltpu.VMEM((tokens, 128), F32),
                pltpu.VMEM((tokens, 128), F32),
                pltpu.VMEM((tokens, 128), F32),
                pltpu.VMEM((tokens, 128), F32),
                pltpu.VMEM((tokens, D), F32),
                pltpu.VMEM((tokens, D), F32),
                pltpu.VMEM((tokens, 128), F32),
            ],
        ),
        out_shape=[
            jax.ShapeDtypeStruct((tokens, D), BF16),
            jax.ShapeDtypeStruct((tokens, D), F32),
            jax.ShapeDtypeStruct((4, inner_rows, tokens), BF16),
            jax.ShapeDtypeStruct((2, D, ff_slice), BF16),
            jax.ShapeDtypeStruct((2, D, ff_slice), BF16),
            jax.ShapeDtypeStruct((2, D, ff_slice), BF16),
            jax.ShapeDtypeStruct((2, D, ff_slice), BF16),
            jax.ShapeDtypeStruct((4, inner_rows, D), BF16),
            jax.ShapeDtypeStruct((4, 8, D), F32),
        ],
        compiler_params=pltpu.CompilerParams(
            dimension_semantics=("arbitrary",), vmem_limit_bytes=60 << 20
        ),
        cost_estimate=pl.CostEstimate(
            flops=20_000_000_000, bytes_accessed=30_000_000, transcendentals=4_000_000
        ),
        name="token_section",
    )(info, *attended, *packs, inputs, cotangent, vectors, gathered, gathered)


def swap(values, distance):
    count = lax.axis_size("head")
    return lax.ppermute(values, "head", [(i, i ^ distance) for i in range(count)])


def dp_swap(values, distance):
    count = lax.axis_size("dp")
    return lax.ppermute(values, "dp", [(i, i ^ distance) for i in range(count)])


def pick(values, index, axis):
    return lax.dynamic_index_in_dim(values, index, axis, keepdims=False)


def wide(values):
    return values.astype(F32)


def reduce_near(values, axis):
    near = lax.axis_index("dp") & 1
    got = dp_swap(pick(values, 1 - near, axis).astype(BF16), 1)
    return wide(pick(values, near, axis)) + wide(got)


def reduce_far(values, axis):
    far = lax.axis_index("dp") >> 1
    got = [
        dp_swap(pick(values, far ^ m, axis).astype(BF16), 2 * m) for m in range(1, values.shape[axis])
    ]
    return wide(pick(values, far, axis)) + sum(wide(g) for g in got)


def spread_far(values):
    far = lax.axis_index("dp") >> 1
    count = lax.axis_size("dp") // 2
    total = jnp.zeros((count,) + values.shape, values.dtype)
    total = lax.dynamic_update_index_in_dim(total, values, far, 0)
    for m in range(1, count):
        total = lax.dynamic_update_index_in_dim(total, dp_swap(values, 2 * m), far ^ m, 0)
    return total


def spread_near(values, axis):
    near = lax.axis_index("dp") & 1
    got = dp_swap(values, 1)
    return jnp.stack(
        [jnp.where(near == 0, values, got), jnp.where(near == 0, got, values)], axis=axis
    )


def local(
    inputs,
    cotangent,
    lengths,
    norm1_gain,
    query_weight,
    query_bias,
    key_weight,
    value_weight,
    value_bias,
    inner_gain,
    output_weight,
    output_bias,
    norm2_gain,
    hidden_weight,
    hidden_bias,
    hidden_gain,
    project_weight,
    project_bias,
):
    dp_count = lax.axis_size("dp")
    far_count = dp_count // 2
    me = lax.axis_index("head")
    heads = query_weight.shape[1] // HEAD_DIM
    shard_rows = hidden_weight.shape[0]
    slice_cols = hidden_weight.shape[1]
    inner_rows = output_weight.shape[0]

    first_length = lengths[0, 0]
    limits = [
        jnp.where(first_length > SHORT, first_length - SHORT * (me ^ r), lengths[0, me ^ r])
        for r in range(4)
    ]
    info = jnp.stack([first_length] + limits + [me]).astype(jnp.int32)

    shards = jnp.concatenate([hidden_weight, project_weight.T], axis=0)
    gathered = lax.all_gather(shards, ("dp", "head"), axis=0, tiled=False)
    gathered = gathered.reshape(dp_count, 4, 2, shard_rows, slice_cols)
    if shard_rows % 16:
        gathered = gathered.transpose(1, 2, 0, 3, 4).reshape(1, 4, 2, D, slice_cols)

    input_share = wide(inputs)
    unit1, scaling1 = rows_normed(input_share)
    gain1 = wide(norm1_gain)
    normed1 = (unit1 * gain1).astype(BF16)
    near = swap(normed1, 1)
    across = swap(normed1, 2)
    far = swap(across, 1)
    rows = (normed1, near, across, far)

    pack = jnp.concatenate(
        [
            jnp.pad(jnp.concatenate([output_weight, inner_gain[:, None]], axis=1), ((0, 0), (0, 127))),
            jnp.pad(jnp.stack([hidden_bias, hidden_gain]), ((0, 14), (0, D + 128 - slice_cols))),
        ],
        axis=0,
    )
    pack_across = swap(pack, 2)
    packs = (pack, swap(pack, 1), pack_across, swap(pack_across, 1))

    def per_head(weight):
        return weight.reshape(-1, heads, HEAD_DIM)

    zero_bias = jnp.zeros_like(query_bias)
    packed_weight = jnp.concatenate(
        [per_head(query_weight), per_head(key_weight), per_head(value_weight)], axis=2
    ).transpose(1, 0, 2)
    packed_bias = wide(
        jnp.concatenate(
            [b.reshape(heads, 1, HEAD_DIM) for b in (query_bias, zero_bias, value_bias)], axis=2
        )
    )
    attended_heads, lse, queries, keys, values = attention_forward(
        info, rows, packed_weight, packed_bias
    )

    def exchange(pieces):
        return [pieces[0]] + [swap(pieces[r], r) for r in (1, 2, 3)]

    attended = exchange([attended_heads[r] for r in range(4)])
    vectors = jnp.concatenate(
        [wide(jnp.stack([output_bias, norm2_gain, project_bias])), jnp.zeros((5, D), F32)], axis=0
    )
    (
        output, d_middle, attended_grad, in_keep, in_send, out_keep, out_send, o_grad, vec_parts
    ) = token_section(info, attended, packs, inputs, cotangent, vectors, gathered)

    in_got, out_got = swap(in_send, 1), swap(out_send, 1)
    side = jnp.concatenate(
        [
            o_grad.reshape(4, far_count, 2, inner_rows // dp_count, D),
            jnp.broadcast_to(vec_parts.astype(BF16)[:, None, None], (4, far_count, 2, 8, D)),
        ],
        axis=3,
    )
    side_got = swap(side[1::2], 1)
    grads = exchange([attended_grad[r] for r in range(4)])

    across_sum = (wide(in_keep[1]) + wide(in_got[1])).astype(BF16)
    across_got = swap(across_sum, 2)
    blocks = (2, far_count, 2, shard_rows, slice_cols)
    out_sum = wide(out_keep.reshape(blocks)) + wide(out_got.reshape(blocks))
    out_sum = jnp.concatenate([out_sum, wide(side[0::2]) + wide(side_got)], axis=3)
    out_sum = reduce_near(out_sum, 2)

    d_rows, d_weight = attention_backward(
        info, grads, attended_heads, lse, queries, keys, values, packed_weight, rows
    )
    in_sum = wide(in_keep[0]) + wide(in_got[0]) + wide(across_got)
    in_sum = reduce_near(in_sum.reshape(blocks[1:]), 1)
    hidden_grad = reduce_far(in_sum, 0)
    out_sum = reduce_far(out_sum, 1)
    out_sum = out_sum[0] + wide(swap(out_sum[1].astype(BF16), 2))
    project_grad = out_sum[:shard_rows].T
    o_chunk = out_sum[shard_rows:-8].astype(BF16)
    vec_total = out_sum[-8:]

    near_rows = swap(d_rows[1::2], 1)
    own_sum = wide(d_rows[0]) + wide(near_rows[0])
    cross_sum = (wide(d_rows[2]) + wide(near_rows[1])).astype(BF16)
    d_normed1 = own_sum + wide(swap(cross_sum, 2))
    input_grad = d_middle + rows_back(d_normed1 * gain1, unit1, scaling1)

    part = d_weight.reshape(heads, 2, far_count, D // dp_count, 256)
    part = reduce_near(part, 1)
    part = reduce_far(part, 1).astype(BF16)
    part = spread_near(spread_far(part), 0)
    total = wide(part.transpose(2, 0, 1, 3, 4).reshape(heads, D, 256))
    by_kind = [
        jnp.concatenate([total[h, :, k * 64 : k * 64 + 64] for h in range(heads)], axis=1)
        for k in range(3)
    ]
    bias = [total[:, k * 64 : k * 64 + 64, 193].reshape(-1) for k in (0, 2)]
    o_total = wide(spread_near(spread_far(o_chunk), 1).reshape(inner_rows, D))
    norm1_total = total[:, :, 192].sum(axis=0)
    norm1_total = norm1_total + swap(norm1_total, 1)
    norm1_total = (norm1_total + swap(norm1_total, 2)) / gain1
    return (
        output,
        input_grad,
        norm1_total,
        by_kind[0],
        bias[0],
        by_kind[1],
        by_kind[2],
        bias[1],
        vec_total[2, :inner_rows],
        o_total,
        vec_total[5],
        vec_total[3],
        hidden_grad,
        vec_total[1],
        vec_total[0],
        project_grad,
        vec_total[4],
    )


def solution(mesh):
    rows = P(("dp", "head"), None)
    columns = P(None, "head")
    head = P("head")
    return jax.shard_map(
        local,
        mesh=mesh,
        in_specs=(
            rows, rows, P("dp", None), P(), columns, head, columns, columns, head, head,
            P("head", None), P(), P(), P("dp", "head"), head, head, P("head", "dp"), P(),
        ),
        out_specs=(
            rows, rows, P(), columns, head, columns, columns, head, head, P("head", None),
            P(), P(), P("dp", "head"), head, head, P("head", "dp"), P(),
        ),
        check_vma=False,
    )
```

```python
import functools
import math

import jax
import jax.numpy as jnp
from jax import lax
from jax.experimental import pallas as pl
from jax.experimental.pallas import tpu as pltpu
from jax.sharding import PartitionSpec as P

D = 768
HEAD_DIM = 64
FF = 3072
SHORT = 512
SLOT = 4 * SHORT

BF16 = jnp.bfloat16
F32 = jnp.float32
epsilon = 1e-05
excluded = 1e30
SCALE = HEAD_DIM ** (-0.5)
LOG2_SCALE = SCALE * math.log2(math.e)
LN2 = math.log(2.0)
QUERY_ROWS = 512
KEY_ROWS = 256
VMEM_LIMIT = 56 << 20


def nt(left, right):
    return lax.dot_general(left, right, (((1,), (1,)), ((), ())), preferred_element_type=F32)


def nn(left, right):
    return lax.dot_general(left, right, (((1,), (0,)), ((), ())), preferred_element_type=F32)


def tn(left, right):
    return lax.dot_general(left, right, (((0,), (0,)), ((), ())), preferred_element_type=F32)


def attention_forward_kernel(info, x0, x1, x2, x3, w_ref, b_ref, o_ref, lse_ref, q_ref, k_ref, v_ref):
    lane = lax.broadcasted_iota(jnp.int32, (SHORT, 128), 1)
    row = lax.broadcasted_iota(jnp.int32, (SHORT, 128), 0)
    for block, x_ref in enumerate((x0, x1, x2, x3)):
        rows = pl.ds(block * SHORT, SHORT)
        packed = (nt(x_ref[...], w_ref[0]) + b_ref[0]).astype(BF16)
        inside = jnp.where(row < info[1 + block], 1.0, 0.0).astype(F32)
        q_flags = jnp.where(lane == 0, inside, jnp.where(lane == 1, 1.0 - inside, 0.0))
        k_flags = jnp.where(
            lane == 0, (inside - 1.0) * excluded, jnp.where(lane == 1, inside * -excluded, 0.0)
        )
        q, k, v = packed[:, 0:64], packed[:, 64:128], packed[:, 128:192]
        scaled = k.astype(F32) * LOG2_SCALE
        high = scaled.astype(BF16)
        low = (scaled - high.astype(F32)).astype(BF16)
        q_ref[0, rows, :] = jnp.concatenate([q, q, q_flags.astype(BF16)], axis=1)
        k_ref[0, rows, :] = jnp.concatenate([high, low, k_flags.astype(BF16)], axis=1)
        v_ref[0, rows, :] = jnp.concatenate([v, jnp.ones((SHORT, 64), BF16)], axis=1)

    def block_of(start, keys):
        scores = nt(q_ref[0, pl.ds(start, QUERY_ROWS), :], k_ref[0, keys, :])
        top = jnp.max(scores, axis=1, keepdims=True)
        weights = jnp.exp2(scores - top).astype(BF16)
        out = nn(weights, v_ref[0, keys, :])
        out_lane = lax.broadcasted_iota(jnp.int32, (QUERY_ROWS, 128), 1)
        out = jnp.where(out_lane == 65, jnp.broadcast_to(top, (QUERY_ROWS, 128)), out).T
        total = out[64:65]
        o_ref[start // SHORT, :, pl.ds(start % SHORT, QUERY_ROWS)] = (
            out[0:64] * (1.0 / total)
        ).astype(BF16)
        lse_ref[0, :, pl.ds(start, QUERY_ROWS)] = out[65:66] + jnp.log2(total)

    longer = info[0] > SHORT

    @pl.when(longer)
    def _():
        for start in range(0, SLOT, QUERY_ROWS):
            block_of(start, pl.ds(0, SLOT))

    @pl.when(jnp.logical_not(longer))
    def _():
        for start in range(0, SLOT, QUERY_ROWS):
            block_of(start, pl.ds(start // SHORT * SHORT, SHORT))


def head_spec(*shape):
    return pl.BlockSpec((1,) + shape, lambda h, info: (h,) + (0,) * len(shape))


def whole_spec(*shape):
    return pl.BlockSpec(shape, lambda h, info: (0,) * len(shape))


def attention_forward(info, rows, weights, biases):
    heads = weights.shape[0]
    return pl.pallas_call(
        attention_forward_kernel,
        grid_spec=pltpu.PrefetchScalarGridSpec(
            num_scalar_prefetch=1,
            grid=(heads,),
            in_specs=[whole_spec(SHORT, D)] * 4 + [head_spec(192, D), head_spec(1, 192)],
            out_specs=[
                pl.BlockSpec((4, HEAD_DIM, SHORT), lambda h, info: (0, h, 0)),
                head_spec(1, SLOT),
                head_spec(SLOT, 256),
                head_spec(SLOT, 256),
                head_spec(SLOT, 128),
            ],
        ),
        out_shape=[
            jax.ShapeDtypeStruct((4, heads * HEAD_DIM, SHORT), BF16),
            jax.ShapeDtypeStruct((heads, 1, SLOT), F32),
            jax.ShapeDtypeStruct((heads, SLOT, 256), BF16),
            jax.ShapeDtypeStruct((heads, SLOT, 256), BF16),
            jax.ShapeDtypeStruct((heads, SLOT, 128), BF16),
        ],
        compiler_params=pltpu.CompilerParams(
            dimension_semantics=("arbitrary",), vmem_limit_bytes=VMEM_LIMIT
        ),
        cost_estimate=pl.CostEstimate(
            flops=24_000_000_000, bytes_accessed=12_000_000, transcendentals=12_000_000
        ),
        name="attention_forward",
    )(info, *rows, weights, biases)


def attention_backward_kernel(head, last, *refs):
    info, g0, g1, g2, g3, o_ref, lse_ref, q_ref, k_ref, v_ref = refs[:10]
    x_refs = refs[10:14]
    rest = list(refs[14:])
    if last:
        w_ref = rest.pop(0)
        earlier = [rest.pop(0) for _ in range(head)]
        d_weights = [rest.pop(0) for _ in range(head)]
        dw_ref, dx_keep, dx_send, gain_ref, grad, dq, delta, packed, x_all, sems = rest
    else:
        packed_ref, dw_ref, grad, dq, delta, packed, x_all, sems = rest
    copies = [
        pltpu.make_async_copy(x_ref, x_all.at[block], sems.at[block]) for block, x_ref in enumerate(x_refs)
    ]
    for copy in copies:
        copy.start()
    for block, g_ref in enumerate((g0, g1, g2, g3)):
        g = g_ref[...].astype(F32)
        cols = pl.ds(block * SHORT, SHORT)
        delta[:, cols] = jnp.sum(g * o_ref[block].astype(F32), axis=0, keepdims=True)
        grad[cols, :] = g.T.astype(BF16)

    def block_of(start, queries, first):
        rows = pl.ds(start, KEY_ROWS)
        k = k_ref[0, rows, :]
        q = q_ref[0, queries, :]
        g = grad[queries, :]
        weights = jnp.exp2(nt(k, q) - lse_ref[0, :, queries])
        d_probs = nt(v_ref[0, rows, 0:64], g)
        d_scores = (weights * (d_probs - delta[:, queries])).astype(BF16)
        packed[rows, 128:192] = nn(weights.astype(BF16), g).astype(BF16)
        packed[rows, 64:128] = (nn(d_scores, q[:, 0:128])[:, 0:64] * SCALE).astype(BF16)
        term = tn(d_scores, k[:, 0:128])
        if first:
            dq[queries, :] = term
        else:
            dq[queries, :] += term

    longer = info[0] > SHORT

    @pl.when(longer)
    def _():
        for start in range(0, SLOT, KEY_ROWS):
            block_of(start, pl.ds(0, SLOT), start == 0)

    @pl.when(jnp.logical_not(longer))
    def _():
        for start in range(0, SLOT, KEY_ROWS):
            block_of(start, pl.ds(start // SHORT * SHORT, SHORT), start % SHORT == 0)

    total = dq[...]
    packed[:, 0:64] = ((total[:, 0:64] + total[:, 64:128]) * LN2).astype(BF16)
    if last:
        for block in range(4):
            rows = pl.ds(block * SHORT, SHORT)
            term = nn(packed[rows, :], w_ref[head])
            for other in range(head):
                term += nn(earlier[other][rows, :], w_ref[other])
            out = dx_send if block % 2 else dx_keep
            out[block // 2] = term.astype(BF16)
    else:
        packed_ref[...] = packed[...]
    for copy in copies:
        copy.wait()
    d_weight = jnp.zeros((192, D), F32)
    d_bias = jnp.zeros((1, 192), F32)
    for block in range(4):
        part = packed[pl.ds(block * SHORT, SHORT), :]
        d_weight += tn(part, x_all[block])
        d_bias += jnp.sum(part.astype(F32), axis=0, keepdims=True)
    dw_ref[0:192, :] = d_weight.astype(BF16)
    d_bias = jnp.concatenate([d_bias, jnp.zeros((1, D - 192), F32)], axis=1)
    row = lax.broadcasted_iota(jnp.int32, (64, D), 0)
    dw_ref[192:256, :] = jnp.where(row == 0, d_bias, 0.0).astype(BF16)
    if last:
        gain = jnp.sum(d_weight * w_ref[head].astype(F32), axis=0, keepdims=True)
        for other in range(head):
            gain += jnp.sum(
                d_weights[other][0:192, :].astype(F32) * w_ref[other].astype(F32), axis=0, keepdims=True
            )
        gain_ref[...] = jnp.broadcast_to(gain, (8, D))


def attention_backward(
    head, info, grads, attended, lse, queries, keys, values, rows, weights, earlier, d_weights
):
    last = head == queries.shape[0] - 1
    one = lambda *shape: pl.BlockSpec((1,) + shape, lambda i, info: (head,) + (0,) * len(shape))
    in_specs = (
        [pl.BlockSpec((HEAD_DIM, SHORT), lambda i, info: (head, 0))] * 4
        + [pl.BlockSpec((4, HEAD_DIM, SHORT), lambda i, info: (0, head, 0))]
        + [one(1, SLOT), one(SLOT, 256), one(SLOT, 256), one(SLOT, 128)]
        + [pl.BlockSpec(memory_space=pl.ANY)] * 4
    )
    operands = [*grads, attended, lse, queries, keys, values, *rows]
    out_specs = [whole_spec(256, D)]
    out_shape = [jax.ShapeDtypeStruct((256, D), BF16)]
    if last:
        in_specs += [whole_spec(*weights.shape)]
        in_specs += [whole_spec(SLOT, 192)] * head + [whole_spec(256, D)] * head
        operands += [weights, *earlier, *d_weights]
        out_specs += [whole_spec(2, SHORT, D)] * 2 + [whole_spec(8, D)]
        out_shape += [jax.ShapeDtypeStruct((2, SHORT, D), BF16)] * 2 + [jax.ShapeDtypeStruct((8, D), F32)]
    else:
        out_specs = [whole_spec(SLOT, 192)] + out_specs
        out_shape = [jax.ShapeDtypeStruct((SLOT, 192), BF16)] + out_shape
    return pl.pallas_call(
        functools.partial(attention_backward_kernel, head, last),
        grid_spec=pltpu.PrefetchScalarGridSpec(
            num_scalar_prefetch=1,
            grid=(1,),
            in_specs=in_specs,
            out_specs=out_specs,
            scratch_shapes=[
                pltpu.VMEM((SLOT, HEAD_DIM), BF16),
                pltpu.VMEM((SLOT, 128), F32),
                pltpu.VMEM((1, SLOT), F32),
                pltpu.VMEM((SLOT, 192), BF16),
                pltpu.VMEM((4, SHORT, D), BF16),
                pltpu.SemaphoreType.DMA((4,)),
            ],
        ),
        out_shape=out_shape,
        compiler_params=pltpu.CompilerParams(
            dimension_semantics=("arbitrary",), vmem_limit_bytes=VMEM_LIMIT
        ),
        cost_estimate=pl.CostEstimate(
            flops=15_000_000_000, bytes_accessed=8_000_000, transcendentals=4_000_000
        ),
        name="attention_backward",
    )(info, *operands)


def finish_kernel(info, *refs):
    halves, (q_out, k_out, v_out, bias_out), whole = refs[:-5], refs[-5:-1], refs[-1]
    heads = len(halves) // 2
    near, far = info[6], info[7]
    for h in range(heads):
        for n in range(2):
            half = halves[2 * h + n]
            count, rows, _ = half.shape
            for m in range(count):
                start = ((near ^ n) * count + (far ^ m)) * rows
                whole[h, pl.ds(pl.multiple_of(start, rows), rows), :] = half[m]
    for kind, out in enumerate((q_out, k_out, v_out)):
        for h in range(heads):
            part = whole[h, kind * HEAD_DIM : (kind + 1) * HEAD_DIM, :].astype(F32)
            out[:, h * HEAD_DIM : (h + 1) * HEAD_DIM] = part.T
    for h in range(heads):
        bias_out[h] = whole[h, 192:208, :].astype(F32)[0:8]


def finish(info, halves):
    heads = len(halves) // 2
    fixed = lambda *shape: pl.BlockSpec(shape, lambda i, info: (0,) * len(shape))
    return pl.pallas_call(
        finish_kernel,
        grid_spec=pltpu.PrefetchScalarGridSpec(
            num_scalar_prefetch=1,
            grid=(1,),
            in_specs=[fixed(*half.shape) for half in halves],
            out_specs=[fixed(D, heads * HEAD_DIM)] * 3 + [fixed(heads, 8, D)],
            scratch_shapes=[pltpu.VMEM((heads, 256, D), BF16)],
        ),
        out_shape=[jax.ShapeDtypeStruct((D, heads * HEAD_DIM), F32)] * 3
        + [jax.ShapeDtypeStruct((heads, 8, D), F32)],
        name="finish",
    )(info, *halves)


def input_grad_kernel(x_ref, gain_ref, middle_ref, keep_ref, near_ref, got_ref, out_ref):
    unit, scaling = rows_normed(x_ref[...].astype(F32))
    grad = keep_ref[0].astype(F32) + near_ref[0].astype(F32) + got_ref[...].astype(F32)
    out_ref[...] = middle_ref[...] + rows_back(grad * gain_ref[...], unit, scaling)


def input_gradient(inputs, gain, d_middle, keep, near, got):
    fixed = lambda *shape: pl.BlockSpec(shape, lambda i: (0,) * len(shape))
    tokens = inputs.shape[0]
    first = pl.BlockSpec((1, tokens, D), lambda i: (0, 0, 0))
    return pl.pallas_call(
        input_grad_kernel,
        grid=(1,),
        in_specs=[fixed(tokens, D), fixed(1, D), fixed(tokens, D), first, first, fixed(tokens, D)],
        out_specs=fixed(tokens, D),
        out_shape=jax.ShapeDtypeStruct((tokens, D), F32),
        name="input_gradient",
    )(inputs, gain, d_middle, keep, near, got)


def rows_normed(values):
    centre = jnp.mean(values, axis=1, keepdims=True)
    spread = jnp.mean(values * values, axis=1, keepdims=True) - centre * centre
    scaling = lax.rsqrt(spread + epsilon)
    return (values - centre) * scaling, scaling


def rows_back(scaled, unit, scaling):
    first = jnp.mean(scaled, axis=1, keepdims=True)
    second = jnp.mean(scaled * unit, axis=1, keepdims=True)
    return scaling * (scaled - first - unit * second)


def lanes_folded(values):
    return sum(values[:, c : c + 128] for c in range(0, values.shape[1], 128))


def token_kernel(
    info, a0, a1, a2, a3, p0, p1, p2, p3, x_ref, cot_ref, vec_ref, w_in, w_out,
    out_ref, middle_grad_ref, attended_grad_ref, in_keep, in_send, out_keep, out_send, o_grad_ref, vec_out_ref,
    attended, unit_c, context, weight_o, middle, normed2, unit2, flipped, cot_flipped, activated, slope, d_mixed,
    fold_a, fold_b, fold_c, fold_d, projected, d_normed2, columns,
):
    step = pl.program_id(0)
    phase = step // 4
    r = jnp.where(phase == 2, 3 - step % 4, step % 4)
    tokens = x_ref.shape[0]
    ff_slice = w_in.shape[-1]
    ff = 4 * ff_slice
    packs = (p0, p1, p2, p3)
    inner_rows = a0.shape[0]

    def col(name):
        return columns[:, name : name + 1]

    def set_col(name, value):
        columns[:, name : name + 1] = value

    @pl.when(step == 0)
    def _():
        for i, a_ref in enumerate((a0, a1, a2, a3)):
            attended[i * inner_rows : (i + 1) * inner_rows, :] = a_ref[...].astype(F32)
            weight_o[i * inner_rows : (i + 1) * inner_rows, :] = packs[i][0:inner_rows, 0:D]
        values = attended[...]
        centre = jnp.mean(values, axis=0, keepdims=True)
        spread = jnp.mean(values * values, axis=0, keepdims=True) - centre * centre
        scaling = lax.rsqrt(spread + epsilon)
        unit = (values - centre) * scaling
        unit_c[...] = unit
        attended[0:1, :] = scaling
        for i in range(4):
            part = slice(i * inner_rows, (i + 1) * inner_rows)
            gain = packs[i][0:inner_rows, D : D + 1].astype(F32)
            context[part, :] = (unit[part] * gain).astype(BF16)
        branch = tn(context[...], weight_o[...])
        total = x_ref[...].astype(F32) + (branch + vec_ref[0:1, :])
        middle[...] = total
        unit, scaling = rows_normed(total)
        unit2[...] = unit
        set_col(0, scaling)
        scaled = (unit * vec_ref[1:2, :]).astype(BF16)
        normed2[...] = scaled
        flipped[...] = scaled.T
        cot_flipped[...] = cot_ref[...].T
        for ref in (fold_a, fold_b, fold_c, fold_d, projected, d_normed2):
            ref[...] = jnp.zeros_like(ref)

    def pack_row(row):
        value = packs[0][inner_rows : inner_rows + 16, 0:ff_slice].astype(F32)
        for i in range(1, 4):
            other = packs[i][inner_rows : inner_rows + 16, 0:ff_slice].astype(F32)
            value = jnp.where(r == i, other, value)
        return value[row : row + 1]

    def weight(ref):
        return ref[...].reshape(D, ff_slice)

    @pl.when(phase == 0)
    def _():
        hidden = nn(normed2[...], weight(w_in)) + pack_row(0)
        density = jnp.exp(hidden * hidden * -0.5) * (1.0 / math.sqrt(2.0 * math.pi))
        share = 0.5 * (1.0 + lax.erf(hidden * math.sqrt(0.5)))
        value = hidden * share
        activated[r] = value
        slope[r] = share + hidden * density
        fold_a[...] += lanes_folded(value)
        fold_b[...] += lanes_folded(value * value)

    @pl.when(step == 4)
    def _():
        centre = jnp.sum(fold_a[...], axis=1, keepdims=True) * (1.0 / ff)
        spread = jnp.sum(fold_b[...], axis=1, keepdims=True) * (1.0 / ff) - centre * centre
        set_col(1, centre)
        set_col(2, lax.rsqrt(spread + epsilon))

    @pl.when(phase == 1)
    def _():
        gain = pack_row(1)
        unit = (activated[r] - col(1)) * col(2)
        mixed = (unit * gain).astype(BF16)
        projected[...] += nt(mixed, weight(w_out))
        part = nn(cot_flipped[...], mixed).astype(BF16)

        @pl.when(r % 2 == 0)
        def _():
            out_keep[0] = part

        @pl.when(r % 2 == 1)
        def _():
            out_send[0] = part

        grad = nn(cot_ref[...], weight(w_out))
        vec_out_ref[r, 0:1, :] = jnp.sum(grad * unit, axis=0, keepdims=True)
        scaled = grad * gain
        d_mixed[r] = scaled
        fold_c[...] += lanes_folded(scaled)
        fold_d[...] += lanes_folded(scaled * unit)

    @pl.when(step == 8)
    def _():
        set_col(3, jnp.sum(fold_c[...], axis=1, keepdims=True) * (1.0 / ff))
        set_col(4, jnp.sum(fold_d[...], axis=1, keepdims=True) * (1.0 / ff))
        out_ref[...] = (middle[...] + (projected[...] + vec_ref[2:3, :])).astype(BF16)

    @pl.when(phase == 2)
    def _():
        unit = (activated[r] - col(1)) * col(2)
        grad = (slope[r] * (col(2) * (d_mixed[r] - col(3) - unit * col(4)))).astype(BF16)
        vec_out_ref[r, 1:2, :] = jnp.sum(grad.astype(F32), axis=0, keepdims=True)
        part = nn(flipped[...], grad).astype(BF16)

        @pl.when(r % 2 == 0)
        def _():
            in_keep[0] = part

        @pl.when(r % 2 == 1)
        def _():
            in_send[0] = part

        d_normed2[...] += nt(grad, weight(w_in))

    @pl.when(step == 11)
    def _():
        cot = cot_ref[...].astype(F32)
        grad = d_normed2[...]
        unit = unit2[...]
        d_middle = cot + rows_back(grad * vec_ref[1:2, :], unit, col(0))
        middle_grad_ref[...] = d_middle
        d_branch = d_middle.astype(BF16)
        norm2_part = jnp.sum(grad * unit, axis=0, keepdims=True)
        project_bias_part = jnp.sum(cot, axis=0, keepdims=True)
        output_bias_part = jnp.sum(d_branch.astype(F32), axis=0, keepdims=True)
        d_context = nt(weight_o[...], d_branch)
        o_grad_ref[...] = nn(context[...], d_branch).astype(BF16).reshape(o_grad_ref.shape)
        unit = unit_c[...]
        inner_part = jnp.sum(d_context * unit, axis=1, keepdims=True)
        inner_part = jnp.broadcast_to(inner_part, (D, 128)).T[0:1]
        first = jnp.zeros((1, tokens), F32)
        second = jnp.zeros((1, tokens), F32)
        for i in range(4):
            rows = slice(i * inner_rows, (i + 1) * inner_rows)
            scaled = d_context[rows] * packs[i][0:inner_rows, D : D + 1].astype(F32)
            first += jnp.sum(scaled, axis=0, keepdims=True)
            second += jnp.sum(scaled * unit[rows], axis=0, keepdims=True)
        first, second = first * (1.0 / D), second * (1.0 / D)
        scaling = attended[0:1, :]
        for i in range(4):
            rows = slice(i * inner_rows, (i + 1) * inner_rows)
            scaled = d_context[rows] * packs[i][0:inner_rows, D : D + 1].astype(F32)
            attended_grad_ref[i] = (scaling * (scaled - first - unit[rows] * second)).astype(BF16)
            vec_out_ref[i, 2:3, 0:inner_rows] = inner_part[:, rows]
            vec_out_ref[i, 2:3, inner_rows:D] = jnp.zeros((1, D - inner_rows), F32)
            vec_out_ref[i, 3:4, :] = norm2_part
            vec_out_ref[i, 4:5, :] = project_bias_part
            vec_out_ref[i, 5:6, :] = output_bias_part
            vec_out_ref[i, 6:8, :] = jnp.zeros((2, D), F32)


def token_section(info, attended, packs, inputs, cotangent, vectors, gathered):
    tokens = inputs.shape[0]
    inner_rows = attended[0].shape[0]
    count, _, _, shard_rows, ff_slice = gathered.shape
    fixed = lambda *shape: pl.BlockSpec(shape, lambda s, info: (0,) * len(shape))

    def weight_spec(which, pick):
        return pl.BlockSpec(
            (count, None, None, shard_rows, ff_slice), lambda s, info: (0, info[5] ^ pick(s), which, 0, 0)
        )

    first_pick = lambda s: jnp.where(s < 4, s, jnp.where(s < 8, 3, 11 - s))
    second_pick = lambda s: jnp.clip(s - 4, 0, 3)
    in_pick = lambda s: jnp.clip(11 - s, 0, 3)
    kept = lambda pick: pl.BlockSpec((1, D, ff_slice), lambda s, info: (pick(s) // 2, 0, 0))
    return pl.pallas_call(
        token_kernel,
        grid_spec=pltpu.PrefetchScalarGridSpec(
            num_scalar_prefetch=1,
            grid=(12,),
            in_specs=[fixed(*a.shape) for a in attended]
            + [fixed(*p.shape) for p in packs]
            + [fixed(tokens, D), fixed(tokens, D), fixed(8, D)]
            + [weight_spec(0, first_pick), weight_spec(1, second_pick)],
            out_specs=[
                fixed(tokens, D),
                fixed(tokens, D),
                fixed(4, inner_rows, tokens),
                kept(in_pick),
                kept(in_pick),
                kept(second_pick),
                kept(second_pick),
                fixed(4, inner_rows, D),
                fixed(4, 8, D),
            ],
            scratch_shapes=[
                pltpu.VMEM((D, tokens), F32),
                pltpu.VMEM((D, tokens), F32),
                pltpu.VMEM((D, tokens), BF16),
                pltpu.VMEM((D, D), BF16),
                pltpu.VMEM((tokens, D), F32),
                pltpu.VMEM((tokens, D), BF16),
                pltpu.VMEM((tokens, D), F32),
                pltpu.VMEM((D, tokens), BF16),
                pltpu.VMEM((D, tokens), BF16),
                pltpu.VMEM((4, tokens, ff_slice), F32),
                pltpu.VMEM((4, tokens, ff_slice), F32),
                pltpu.VMEM((4, tokens, ff_slice), F32),
                pltpu.VMEM((tokens, 128), F32),
                pltpu.VMEM((tokens, 128), F32),
                pltpu.VMEM((tokens, 128), F32),
                pltpu.VMEM((tokens, 128), F32),
                pltpu.VMEM((tokens, D), F32),
                pltpu.VMEM((tokens, D), F32),
                pltpu.VMEM((tokens, 128), F32),
            ],
        ),
        out_shape=[
            jax.ShapeDtypeStruct((tokens, D), BF16),
            jax.ShapeDtypeStruct((tokens, D), F32),
            jax.ShapeDtypeStruct((4, inner_rows, tokens), BF16),
            jax.ShapeDtypeStruct((2, D, ff_slice), BF16),
            jax.ShapeDtypeStruct((2, D, ff_slice), BF16),
            jax.ShapeDtypeStruct((2, D, ff_slice), BF16),
            jax.ShapeDtypeStruct((2, D, ff_slice), BF16),
            jax.ShapeDtypeStruct((4, inner_rows, D), BF16),
            jax.ShapeDtypeStruct((4, 8, D), F32),
        ],
        compiler_params=pltpu.CompilerParams(
            dimension_semantics=("arbitrary",), vmem_limit_bytes=60 << 20
        ),
        cost_estimate=pl.CostEstimate(
            flops=20_000_000_000, bytes_accessed=30_000_000, transcendentals=4_000_000
        ),
        name="token_section",
    )(info, *attended, *packs, inputs, cotangent, vectors, gathered, gathered)


def swap(values, distance):
    count = lax.axis_size("head")
    return lax.ppermute(values, "head", [(i, i ^ distance) for i in range(count)])


def dp_swap(values, distance):
    count = lax.axis_size("dp")
    return lax.ppermute(values, "dp", [(i, i ^ distance) for i in range(count)])


def pick(values, index, axis):
    return lax.dynamic_index_in_dim(values, index, axis, keepdims=False)


def wide(values):
    return values.astype(F32)


def swap_near(values, axis):
    near = lax.axis_index("dp") & 1
    return dp_swap(pick(values, 1 - near, axis).astype(BF16), 1)


def keep_near(values, axis):
    return pick(values, lax.axis_index("dp") & 1, axis)


def keep_far(values, axis):
    return pick(values, lax.axis_index("dp") >> 1, axis)


def far_of(values, m, axis):
    return pick(values, (lax.axis_index("dp") >> 1) ^ m, axis).astype(BF16)


def far_swaps(payload):
    count = lax.axis_size("dp") // 2
    return [dp_swap(payload(m), 2 * m) for m in range(1, count)]


def after(value, *others):
    return lax.optimization_barrier((value,) + others)[0]


def local(
    inputs,
    cotangent,
    lengths,
    norm1_gain,
    query_weight,
    query_bias,
    key_weight,
    value_weight,
    value_bias,
    inner_gain,
    output_weight,
    output_bias,
    norm2_gain,
    hidden_weight,
    hidden_bias,
    hidden_gain,
    project_weight,
    project_bias,
):
    dp_count = lax.axis_size("dp")
    far_count = dp_count // 2
    me = lax.axis_index("head")
    heads = query_weight.shape[1] // HEAD_DIM
    shard_rows = hidden_weight.shape[0]
    slice_cols = hidden_weight.shape[1]
    inner_rows = output_weight.shape[0]

    first_length = lengths[0, 0]
    limits = [
        jnp.where(first_length > SHORT, first_length - SHORT * (me ^ r), lengths[0, me ^ r])
        for r in range(4)
    ]
    place = lax.axis_index("dp")
    info = jnp.stack([first_length] + limits + [me, place & 1, place >> 1]).astype(jnp.int32)

    shards = jnp.concatenate([hidden_weight, project_weight.T], axis=0)
    gathered = lax.all_gather(shards, ("dp", "head"), axis=0, tiled=False)
    gathered = gathered.reshape(dp_count, 4, 2, shard_rows, slice_cols)
    if shard_rows % 16:
        gathered = gathered.transpose(1, 2, 0, 3, 4).reshape(1, 4, 2, D, slice_cols)

    input_share = wide(inputs)
    unit1, scaling1 = rows_normed(input_share)
    gain1 = wide(norm1_gain)
    normed1 = (unit1 * gain1).astype(BF16)
    near = swap(normed1, 1)
    across = swap(normed1, 2)
    far = swap(across, 1)
    rows = (normed1, near, across, far)

    pack = jnp.concatenate(
        [
            jnp.pad(jnp.concatenate([output_weight, inner_gain[:, None]], axis=1), ((0, 0), (0, 127))),
            jnp.pad(jnp.stack([hidden_bias, hidden_gain]), ((0, 14), (0, D + 128 - slice_cols))),
        ],
        axis=0,
    )
    pack_across = swap(pack, 2)
    packs = (pack, swap(pack, 1), pack_across, swap(pack_across, 1))

    def per_head(weight):
        return weight.reshape(-1, heads, HEAD_DIM)

    zero_bias = jnp.zeros_like(query_bias)
    packed_weight = jnp.concatenate(
        [per_head(query_weight), per_head(key_weight), per_head(value_weight)], axis=2
    ).transpose(1, 2, 0)
    packed_bias = wide(
        jnp.concatenate(
            [b.reshape(heads, 1, HEAD_DIM) for b in (query_bias, zero_bias, value_bias)], axis=2
        )
    )
    attended_heads, lse, queries, keys, values = attention_forward(
        info, rows, packed_weight, packed_bias
    )

    def exchange(pieces):
        return [pieces[0]] + [swap(pieces[r], r) for r in (1, 2, 3)]

    attended = exchange([attended_heads[r] for r in range(4)])
    vectors = jnp.concatenate(
        [wide(jnp.stack([output_bias, norm2_gain, project_bias])), jnp.zeros((5, D), F32)], axis=0
    )
    (
        output, d_middle, attended_grad, in_keep, in_send, out_keep, out_send, o_grad, vec_parts
    ) = token_section(info, attended, packs, inputs, cotangent, vectors, gathered)

    grads = exchange([attended_grad[r] for r in range(4)])
    in_got, out_got = swap(in_send, 1), swap(out_send, 1)
    side = jnp.concatenate(
        [
            o_grad.reshape(4, far_count, 2, inner_rows // dp_count, D),
            jnp.broadcast_to(vec_parts.astype(BF16)[:, None, None], (4, far_count, 2, 8, D)),
        ],
        axis=3,
    )
    side_got = swap(side[1::2], 1)
    across_sum = (wide(in_keep[1]) + wide(in_got[1])).astype(BF16)
    blocks = (2, far_count, 2, shard_rows, slice_cols)
    out_sum = wide(out_keep.reshape(blocks)) + wide(out_got.reshape(blocks))
    out_sum = jnp.concatenate([out_sum, wide(side[0::2]) + wide(side_got)], axis=3)
    out_sent = pick(out_sum, 1 - (place & 1), 2).astype(BF16)
    across_sum, out_sent = lax.optimization_barrier((across_sum, out_sent))
    across_got = swap(across_sum, 2)
    out_near = dp_swap(out_sent, 1)

    shared = (grads, attended_heads, lse, queries, keys, values, rows, packed_weight)
    packed, d_weight = [], []
    info_now = after(info, across_sum, out_sent)

    head_rows = 256 // dp_count
    by_place = lambda v: v.reshape(2, far_count, head_rows, D)
    near_got, half, far_got, quarter = {}, {}, {}, {}

    def start_near(h):
        sent = pick(by_place(d_weight[h]), 1 - (place & 1), 0)
        near_got[h] = dp_swap(sent, 1)
        return sent

    def end_near(h):
        half[h] = (wide(keep_near(by_place(d_weight[h]), 0)) + wide(near_got[h])).astype(BF16)

    for h in range(heads):
        result = attention_backward(h, info_now, *shared, packed, d_weight)
        if h < heads - 1:
            packed.append(result[0])
            d_weight.append(result[1])
        else:
            d_weight.append(result[0])
            dx_keep, dx_send, gain_part = result[1:]
        waits = []
        if h == 0:
            waits += [start_near(0), d_weight[0]]
        if h == 1:
            in_sum = wide(in_keep[0]) + wide(in_got[0]) + wide(across_got)
            in_sum = in_sum.reshape(blocks[1:])
            in_sent = pick(in_sum, 1 - (place & 1), 1).astype(BF16)
            out_half = keep_near(out_sum, 2) + wide(out_near)
            end_near(0)
            far_payload = [
                jnp.concatenate([far_of(out_half, m, 1).reshape(-1, D), far_of(half[0], m, 0)], axis=0)
                for m in range(1, far_count)
            ]
            in_sent, near_sent, *far_payload = lax.optimization_barrier(
                (in_sent, pick(by_place(d_weight[1]), 1 - (place & 1), 0), *far_payload)
            )
            in_near = dp_swap(in_sent, 1)
            near_got[1] = dp_swap(near_sent, 1)
            out_far = [dp_swap(p, 2 * m) for m, p in zip(range(1, far_count), far_payload)]
            waits += [in_sent, near_sent, *far_payload]
        info_now = after(info, *waits)

    (d_weight[2], dx_keep, dx_send, gain_part, near_got[1], in_near, *out_far) = lax.optimization_barrier(
        (d_weight[2], dx_keep, dx_send, gain_part, near_got[1], in_near, *out_far)
    )
    gain_sum = gain_part + swap(gain_part, 1)
    near_rows = swap(dx_send, 1)
    near_got[2] = dp_swap(pick(by_place(d_weight[2]), 1 - (place & 1), 0), 1)
    cross_sum = (wide(dx_keep[1]) + wide(near_rows[1])).astype(BF16)
    gain_sum = gain_sum + swap(gain_sum, 2)
    cross_got = swap(cross_sum, 2)
    out_rows = out_half.shape[2]
    out_total = keep_far(out_half, 1) + sum(
        wide(g[: 2 * out_rows].reshape(2, out_rows, D)) for g in out_far
    )
    quarter[0] = (wide(keep_far(half[0], 0)) + sum(wide(g[2 * out_rows :]) for g in out_far)).astype(BF16)
    out_total = out_total[0] + wide(swap(out_total[1].astype(BF16), 2))
    end_near(1)
    in_half = keep_near(in_sum, 1) + wide(in_near)
    first_far = far_swaps(
        lambda m: jnp.concatenate([quarter[0], far_of(half[1], m, 0), far_of(in_half, m, 0)], axis=0)
    )
    hr = head_rows
    whole = {0: after(jnp.stack([quarter[0]] + [g[:hr] for g in first_far]), cross_sum)}
    quarter[1] = (wide(keep_far(half[1], 0)) + sum(wide(g[hr : 2 * hr]) for g in first_far)).astype(BF16)
    hidden_grad = keep_far(in_half, 0) + sum(wide(g[2 * hr :]) for g in first_far)

    end_near(2)
    o_chunk = out_total[shard_rows:-8].astype(BF16)
    other = {0: dp_swap(whole[0], 1)}
    quarter[1] = after(quarter[1], cross_sum)
    second_far = far_swaps(lambda m: jnp.concatenate([quarter[1], far_of(half[2], m, 0)], axis=0))
    whole[1] = jnp.stack([quarter[1]] + [g[:hr] for g in second_far])
    quarter[2] = (wide(keep_far(half[2], 0)) + sum(wide(g[hr:]) for g in second_far)).astype(BF16)

    def in_two(values):
        high = values.astype(BF16)
        low = (values - wide(high)).astype(BF16)
        return jnp.concatenate([high[0:4], low[0:4]], axis=0)

    def from_two(rows_of):
        return wide(rows_of[0:1]) + wide(rows_of[4:5])

    other[1] = dp_swap(whole[1], 1)
    o_rows = o_chunk.shape[0]
    third = jnp.concatenate([quarter[2], o_chunk, in_two(gain_sum)], axis=0)
    third_far = far_swaps(lambda m: third)
    whole[2] = jnp.stack([quarter[2]] + [g[:hr] for g in third_far])
    o_own = jnp.stack([o_chunk] + [g[hr : hr + o_rows] for g in third_far])
    gain_sum = gain_sum + sum(from_two(g[hr + o_rows :]) for g in third_far)
    last_sent = jnp.concatenate([whole[2].reshape(-1, D), o_own.reshape(-1, D), in_two(gain_sum)], axis=0)
    last_near = dp_swap(after(last_sent, cross_got), 1)
    other[2] = last_near[: far_count * hr].reshape(whole[2].shape)
    o_other = last_near[far_count * hr : far_count * (hr + o_rows)].reshape(o_own.shape)
    norm1_total = (gain_sum[0:1] + from_two(last_near[far_count * (hr + o_rows) :]))[0] / gain1

    input_grad = input_gradient(inputs, gain1[None], d_middle, dx_keep, near_rows, cross_got)
    def in_order(own, neighbour):
        total = jnp.zeros((2, far_count) + own.shape[1:], own.dtype)
        for m in range(far_count):
            for n, part in enumerate((own, neighbour)):
                total = lax.dynamic_update_slice(
                    total, part[m][None, None], ((place & 1) ^ n, (place >> 1) ^ m, 0, 0)
                )
        return total

    halves = [half_of[h] for h in range(heads) for half_of in (whole, other)]
    finish_info = info
    if hr % 16:
        totals = [in_order(whole[h], other[h]) for h in range(heads)]
        halves = [t[n].reshape(1, -1, D) for t in totals for n in range(2)]
        finish_info = jnp.zeros_like(info)
    query_grad, key_grad, value_grad, bias_rows = finish(finish_info, halves)
    bias_rows = bias_rows[:, 0, :192]
    o_total = wide(in_order(o_own, o_other).transpose(1, 0, 2, 3).reshape(inner_rows, D))
    project_grad = out_total[:shard_rows].T
    vec_total = out_total[-8:]
    return (
        output,
        input_grad,
        norm1_total,
        query_grad,
        bias_rows[:, 0:64].reshape(-1),
        key_grad,
        value_grad,
        bias_rows[:, 128:192].reshape(-1),
        vec_total[2, :inner_rows],
        o_total,
        vec_total[5],
        vec_total[3],
        hidden_grad,
        vec_total[1],
        vec_total[0],
        project_grad,
        vec_total[4],
    )


def solution(mesh):
    rows = P(("dp", "head"), None)
    columns = P(None, "head")
    head = P("head")
    return jax.shard_map(
        local,
        mesh=mesh,
        in_specs=(
            rows, rows, P("dp", None), P(), columns, head, columns, columns, head, head,
            P("head", None), P(), P(), P("dp", "head"), head, head, P("head", "dp"), P(),
        ),
        out_specs=(
            rows, rows, P(), columns, head, columns, columns, head, head, P("head", None),
            P(), P(), P("dp", "head"), head, head, P("head", "dp"), P(),
        ),
        check_vma=False,
    )
```

```python
import functools
import math

import jax
import jax.numpy as jnp
from jax import lax
from jax.experimental import pallas as pl
from jax.experimental.pallas import tpu as pltpu
from jax.sharding import PartitionSpec as P

D = 768
HEAD_DIM = 64
FF = 3072
SHORT = 512
SLOT = 4 * SHORT

BF16 = jnp.bfloat16
F32 = jnp.float32
epsilon = 1e-05
excluded = 1e30
SCALE = HEAD_DIM ** (-0.5)
LOG2_SCALE = SCALE * math.log2(math.e)
LN2 = math.log(2.0)
QUERY_ROWS = 512
KEY_ROWS = 256
VMEM_LIMIT = 56 << 20


def nt(left, right):
    return lax.dot_general(left, right, (((1,), (1,)), ((), ())), preferred_element_type=F32)


def nn(left, right):
    return lax.dot_general(left, right, (((1,), (0,)), ((), ())), preferred_element_type=F32)


def tn(left, right):
    return lax.dot_general(left, right, (((0,), (0,)), ((), ())), preferred_element_type=F32)


def attention_forward_kernel(before, info, *refs):
    x_refs, (w_ref, b_ref), earlier = refs[0:4], refs[4:6], refs[6 : 6 + 4 * (before > 0)]
    *o_refs, lse_ref, q_ref, k_ref, v_ref = refs[6 + len(earlier) :]
    head = pl.program_id(0)
    lane = lax.broadcasted_iota(jnp.int32, (SHORT, 128), 1)
    row = lax.broadcasted_iota(jnp.int32, (SHORT, 128), 0)
    for o_ref, early in zip(o_refs, earlier):

        @pl.when(head == 0)
        def _():
            o_ref[0 : before * HEAD_DIM, :] = early[...]

    for block, x_ref in enumerate(x_refs):
        rows = pl.ds(block * SHORT, SHORT)
        packed = (nt(x_ref[...], w_ref[0]) + b_ref[0]).astype(BF16)
        inside = jnp.where(row < info[1 + block], 1.0, 0.0).astype(F32)
        q_flags = jnp.where(lane == 0, inside, jnp.where(lane == 1, 1.0 - inside, 0.0))
        k_flags = jnp.where(
            lane == 0, (inside - 1.0) * excluded, jnp.where(lane == 1, inside * -excluded, 0.0)
        )
        q, k, v = packed[:, 0:64], packed[:, 64:128], packed[:, 128:192]
        scaled = k.astype(F32) * LOG2_SCALE
        high = scaled.astype(BF16)
        low = (scaled - high.astype(F32)).astype(BF16)
        q_ref[0, rows, :] = jnp.concatenate([q, q, q_flags.astype(BF16)], axis=1)
        k_ref[0, rows, :] = jnp.concatenate([high, low, k_flags.astype(BF16)], axis=1)
        v_ref[0, rows, :] = jnp.concatenate([v, jnp.ones((SHORT, 64), BF16)], axis=1)

    out_rows = pl.ds(pl.multiple_of((before + head) * HEAD_DIM, HEAD_DIM), HEAD_DIM)

    def block_of(start, keys):
        scores = nt(q_ref[0, pl.ds(start, QUERY_ROWS), :], k_ref[0, keys, :])
        top = jnp.max(scores, axis=1, keepdims=True)
        weights = jnp.exp2(scores - top).astype(BF16)
        out = nn(weights, v_ref[0, keys, :])
        out_lane = lax.broadcasted_iota(jnp.int32, (QUERY_ROWS, 128), 1)
        out = jnp.where(out_lane == 65, jnp.broadcast_to(top, (QUERY_ROWS, 128)), out).T
        total = out[64:65]
        o_refs[start // SHORT][out_rows, pl.ds(start % SHORT, QUERY_ROWS)] = (
            out[0:64] * (1.0 / total)
        ).astype(BF16)
        lse_ref[0, :, pl.ds(start, QUERY_ROWS)] = out[65:66] + jnp.log2(total)

    longer = info[0] > SHORT

    @pl.when(longer)
    def _():
        for start in range(0, SLOT, QUERY_ROWS):
            block_of(start, pl.ds(0, SLOT))

    @pl.when(jnp.logical_not(longer))
    def _():
        for start in range(0, SLOT, QUERY_ROWS):
            block_of(start, pl.ds(start // SHORT * SHORT, SHORT))


def head_spec(*shape):
    return pl.BlockSpec((1,) + shape, lambda h, info: (h,) + (0,) * len(shape))


def whole_spec(*shape):
    return pl.BlockSpec(shape, lambda h, info: (0,) * len(shape))


def attention_forward(info, rows, weights, biases, before, count, earlier):
    out_rows = (before + count) * HEAD_DIM
    later = lambda *shape: pl.BlockSpec((1,) + shape, lambda h, info: (before + h,) + (0,) * len(shape))
    return pl.pallas_call(
        functools.partial(attention_forward_kernel, before),
        grid_spec=pltpu.PrefetchScalarGridSpec(
            num_scalar_prefetch=1,
            grid=(count,),
            in_specs=[whole_spec(SHORT, D)] * 4
            + [later(192, D), later(1, 192)]
            + [whole_spec(before * HEAD_DIM, SHORT)] * len(earlier),
            out_specs=[whole_spec(out_rows, SHORT)] * 4
            + [head_spec(1, SLOT), head_spec(SLOT, 256), head_spec(SLOT, 256), head_spec(SLOT, 128)],
        ),
        out_shape=[jax.ShapeDtypeStruct((out_rows, SHORT), BF16)] * 4
        + [
            jax.ShapeDtypeStruct((count, 1, SLOT), F32),
            jax.ShapeDtypeStruct((count, SLOT, 256), BF16),
            jax.ShapeDtypeStruct((count, SLOT, 256), BF16),
            jax.ShapeDtypeStruct((count, SLOT, 128), BF16),
        ],
        compiler_params=pltpu.CompilerParams(
            dimension_semantics=("arbitrary",), vmem_limit_bytes=VMEM_LIMIT
        ),
        cost_estimate=pl.CostEstimate(
            flops=8_000_000_000 * count, bytes_accessed=4_000_000 * count, transcendentals=4_000_000 * count
        ),
        name="attention_forward",
    )(info, *rows, weights, biases, *earlier)


def attention_backward_kernel(head, last, *refs):
    info, *pieces = refs[:9]
    lse_ref, q_ref, k_ref, v_ref = refs[9:13]
    x_refs = refs[13:17]
    rest = list(refs[17:])
    if last:
        w_ref = rest.pop(0)
        earlier = [rest.pop(0) for _ in range(head)]
        d_weights = [rest.pop(0) for _ in range(head)]
        dw_ref, dx_keep, dx_send, gain_ref, grad, dq, delta, packed, x_all, sems = rest
    else:
        packed_ref, dw_ref, grad, dq, delta, packed, x_all, sems = rest
    copies = [
        pltpu.make_async_copy(x_ref, x_all.at[block], sems.at[block]) for block, x_ref in enumerate(x_refs)
    ]
    for copy in copies:
        copy.start()
    for block, (g_ref, o_ref) in enumerate(zip(pieces[:4], pieces[4:])):
        g = g_ref[...].astype(F32)
        cols = pl.ds(block * SHORT, SHORT)
        delta[:, cols] = jnp.sum(g * o_ref[...].astype(F32), axis=0, keepdims=True)
        grad[cols, :] = g.T.astype(BF16)

    def block_of(start, queries, first):
        rows = pl.ds(start, KEY_ROWS)
        k = k_ref[0, rows, :]
        q = q_ref[0, queries, :]
        g = grad[queries, :]
        weights = jnp.exp2(nt(k, q) - lse_ref[0, :, queries])
        d_probs = nt(v_ref[0, rows, 0:64], g)
        d_scores = (weights * (d_probs - delta[:, queries])).astype(BF16)
        packed[rows, 128:192] = nn(weights.astype(BF16), g).astype(BF16)
        packed[rows, 64:128] = (nn(d_scores, q[:, 0:128])[:, 0:64] * SCALE).astype(BF16)
        term = tn(d_scores, k[:, 0:128])
        if first:
            dq[queries, :] = term
        else:
            dq[queries, :] += term

    longer = info[0] > SHORT

    @pl.when(longer)
    def _():
        for start in range(0, SLOT, KEY_ROWS):
            block_of(start, pl.ds(0, SLOT), start == 0)

    @pl.when(jnp.logical_not(longer))
    def _():
        for start in range(0, SLOT, KEY_ROWS):
            block_of(start, pl.ds(start // SHORT * SHORT, SHORT), start % SHORT == 0)

    total = dq[...]
    packed[:, 0:64] = ((total[:, 0:64] + total[:, 64:128]) * LN2).astype(BF16)
    if last:
        for block in range(4):
            rows = pl.ds(block * SHORT, SHORT)
            term = nn(packed[rows, :], w_ref[head])
            for other in range(head):
                term += nn(earlier[other][rows, :], w_ref[other])
            out = dx_send if block % 2 else dx_keep
            out[block // 2] = term.astype(BF16)
    else:
        packed_ref[...] = packed[...]
    for copy in copies:
        copy.wait()
    d_weight = jnp.zeros((192, D), F32)
    d_bias = jnp.zeros((1, 192), F32)
    for block in range(4):
        part = packed[pl.ds(block * SHORT, SHORT), :]
        d_weight += tn(part, x_all[block])
        d_bias += jnp.sum(part.astype(F32), axis=0, keepdims=True)
    dw_ref[0:192, :] = d_weight.astype(BF16)
    d_bias = jnp.concatenate([d_bias, jnp.zeros((1, D - 192), F32)], axis=1)
    row = lax.broadcasted_iota(jnp.int32, (64, D), 0)
    dw_ref[192:256, :] = jnp.where(row == 0, d_bias, 0.0).astype(BF16)
    if last:
        gain = jnp.sum(d_weight * w_ref[head].astype(F32), axis=0, keepdims=True)
        for other in range(head):
            gain += jnp.sum(
                d_weights[other][0:192, :].astype(F32) * w_ref[other].astype(F32), axis=0, keepdims=True
            )
        gain_ref[...] = jnp.broadcast_to(gain, (8, D))


def attention_backward(head, last, info, grads, attended, saved, local_head, rows, weights, earlier, d_weights):
    one = lambda *shape: pl.BlockSpec((1,) + shape, lambda i, info: (local_head,) + (0,) * len(shape))
    in_specs = (
        [pl.BlockSpec((HEAD_DIM, SHORT), lambda i, info: (head, 0))] * 8
        + [one(1, SLOT), one(SLOT, 256), one(SLOT, 256), one(SLOT, 128)]
        + [pl.BlockSpec(memory_space=pl.ANY)] * 4
    )
    operands = [*grads, *attended, *saved, *rows]
    out_specs = [whole_spec(256, D)]
    out_shape = [jax.ShapeDtypeStruct((256, D), BF16)]
    if last:
        in_specs += [whole_spec(*weights.shape)]
        in_specs += [whole_spec(SLOT, 192)] * head + [whole_spec(256, D)] * head
        operands += [weights, *earlier, *d_weights]
        out_specs += [whole_spec(2, SHORT, D)] * 2 + [whole_spec(8, D)]
        out_shape += [jax.ShapeDtypeStruct((2, SHORT, D), BF16)] * 2 + [jax.ShapeDtypeStruct((8, D), F32)]
    else:
        out_specs = [whole_spec(SLOT, 192)] + out_specs
        out_shape = [jax.ShapeDtypeStruct((SLOT, 192), BF16)] + out_shape
    return pl.pallas_call(
        functools.partial(attention_backward_kernel, head, last),
        grid_spec=pltpu.PrefetchScalarGridSpec(
            num_scalar_prefetch=1,
            grid=(1,),
            in_specs=in_specs,
            out_specs=out_specs,
            scratch_shapes=[
                pltpu.VMEM((SLOT, HEAD_DIM), BF16),
                pltpu.VMEM((SLOT, 128), F32),
                pltpu.VMEM((1, SLOT), F32),
                pltpu.VMEM((SLOT, 192), BF16),
                pltpu.VMEM((4, SHORT, D), BF16),
                pltpu.SemaphoreType.DMA((4,)),
            ],
        ),
        out_shape=out_shape,
        compiler_params=pltpu.CompilerParams(
            dimension_semantics=("arbitrary",), vmem_limit_bytes=VMEM_LIMIT
        ),
        cost_estimate=pl.CostEstimate(
            flops=15_000_000_000, bytes_accessed=8_000_000, transcendentals=4_000_000
        ),
        name="attention_backward",
    )(info, *operands)


def finish_kernel(info, *refs):
    halves, (q_out, k_out, v_out, bias_out), whole = refs[:-5], refs[-5:-1], refs[-1]
    heads = len(halves) // 2
    near, far = info[6], info[7]
    for h in range(heads):
        for n in range(2):
            half = halves[2 * h + n]
            count, rows, _ = half.shape
            for m in range(count):
                start = ((near ^ n) * count + (far ^ m)) * rows
                whole[h, pl.ds(pl.multiple_of(start, rows), rows), :] = half[m]
    for kind, out in enumerate((q_out, k_out, v_out)):
        for h in range(heads):
            part = whole[h, kind * HEAD_DIM : (kind + 1) * HEAD_DIM, :].astype(F32)
            out[h * HEAD_DIM : (h + 1) * HEAD_DIM, :] = part
    for h in range(heads):
        bias_out[h] = whole[h, 192:208, :].astype(F32)[0:8]


def finish(info, halves):
    heads = len(halves) // 2
    fixed = lambda *shape: pl.BlockSpec(shape, lambda i, info: (0,) * len(shape))
    return pl.pallas_call(
        finish_kernel,
        grid_spec=pltpu.PrefetchScalarGridSpec(
            num_scalar_prefetch=1,
            grid=(1,),
            in_specs=[fixed(*half.shape) for half in halves],
            out_specs=[fixed(heads * HEAD_DIM, D)] * 3 + [fixed(heads, 8, D)],
            scratch_shapes=[pltpu.VMEM((heads, 256, D), BF16)],
        ),
        out_shape=[jax.ShapeDtypeStruct((heads * HEAD_DIM, D), F32)] * 3
        + [jax.ShapeDtypeStruct((heads, 8, D), F32)],
        name="finish",
    )(info, *halves)


def first_norm_kernel(x_ref, gain_ref, out_ref):
    unit, _ = rows_normed(x_ref[...].astype(F32))
    out_ref[...] = (unit * gain_ref[...]).astype(BF16)


def first_norm(inputs, gain):
    return pl.pallas_call(
        first_norm_kernel,
        out_shape=jax.ShapeDtypeStruct(inputs.shape, BF16),
        name="first_norm",
    )(inputs, gain)


def input_grad_kernel(x_ref, gain_ref, middle_ref, keep_ref, near_ref, got_ref, out_ref):
    unit, scaling = rows_normed(x_ref[...].astype(F32))
    grad = keep_ref[0].astype(F32) + near_ref[0].astype(F32) + got_ref[...].astype(F32)
    out_ref[...] = middle_ref[...] + rows_back(grad * gain_ref[...], unit, scaling)


def input_gradient(inputs, gain, d_middle, keep, near, got):
    fixed = lambda *shape: pl.BlockSpec(shape, lambda i: (0,) * len(shape))
    tokens = inputs.shape[0]
    first = pl.BlockSpec((1, tokens, D), lambda i: (0, 0, 0))
    return pl.pallas_call(
        input_grad_kernel,
        grid=(1,),
        in_specs=[fixed(tokens, D), fixed(1, D), fixed(tokens, D), first, first, fixed(tokens, D)],
        out_specs=fixed(tokens, D),
        out_shape=jax.ShapeDtypeStruct((tokens, D), F32),
        name="input_gradient",
    )(inputs, gain, d_middle, keep, near, got)


def rows_normed(values):
    centre = jnp.mean(values, axis=1, keepdims=True)
    spread = jnp.mean(values * values, axis=1, keepdims=True) - centre * centre
    scaling = lax.rsqrt(spread + epsilon)
    return (values - centre) * scaling, scaling


def rows_back(scaled, unit, scaling):
    first = jnp.mean(scaled, axis=1, keepdims=True)
    second = jnp.mean(scaled * unit, axis=1, keepdims=True)
    return scaling * (scaled - first - unit * second)


def lanes_folded(values):
    return sum(values[:, c : c + 128] for c in range(0, values.shape[1], 128))


def token_kernel(pieces, source_count, info, *refs):
    sources = refs[:source_count]
    a_refs = refs[source_count : source_count + 4]
    packs = refs[source_count + 4 : source_count + 8]
    x_ref, cot_ref, vec_ref = refs[source_count + 8 : source_count + 11]
    out_ref, middle_grad_ref, g0, g1, g2, g3, in_keep, in_send, out_keep, out_send, side_keep, side_send = refs[
        source_count + 11 : source_count + 23
    ]
    w_in, w_out, staged, activated, slope, d_mixed, unit_c, middle, unit2, vec_out_ref, in_sems, out_sems = refs[source_count + 23 :]
    tokens = x_ref.shape[0]
    ff_slice = w_in.shape[-1]
    ff = 4 * ff_slice
    inner_rows = a_refs[0].shape[0]

    loads = {}
    for which, target in ((0, w_in), (1, w_out)):
        for r in range(4):
            loads[which, r] = [
                pltpu.make_async_copy(source, target.at[r, pl.ds(start, source.shape[0])], in_sems.at[which, r, i])
                for i, (source, start) in enumerate(pieces(info, sources, which, r))
            ]
    for which in range(2):
        for r in range(4):
            for copy in loads[which, r]:
                copy.start()

    stores = {}

    def store(which, r, value):
        staged[r] = value.astype(BF16)
        target = ((in_keep, in_send), (out_keep, out_send))[which][r % 2]
        stores[r] = pltpu.make_async_copy(staged.at[r], target.at[r // 2], out_sems.at[which, r])
        stores[r].start()

    values = jnp.concatenate([a_ref[...] for a_ref in a_refs], axis=0).astype(F32)
    centre = jnp.mean(values, axis=0, keepdims=True)
    spread = jnp.mean(values * values, axis=0, keepdims=True) - centre * centre
    scaling_c = lax.rsqrt(spread + epsilon)
    unit = (values - centre) * scaling_c
    unit_c[...] = unit
    gain_c = jnp.concatenate([p[0:inner_rows, D : D + 1] for p in packs], axis=0).astype(F32)
    context = (unit * gain_c).astype(BF16)
    weight_o = jnp.concatenate([p[0:inner_rows, 0:D] for p in packs], axis=0)
    total = x_ref[...].astype(F32) + (tn(context, weight_o) + vec_ref[0:1, :])
    middle[...] = total
    unit, scaling2 = rows_normed(total)
    unit2[...] = unit
    normed2 = (unit * vec_ref[1:2, :]).astype(BF16)
    flipped = normed2.T
    cot = cot_ref[...]
    cot_flipped = cot.T
    rows_below = [p[inner_rows : inner_rows + 16, 0:ff_slice].astype(F32) for p in packs]

    fold_a = jnp.zeros((tokens, 128), F32)
    fold_b = jnp.zeros((tokens, 128), F32)
    for r in range(4):
        for copy in loads[0, r]:
            copy.wait()
        hidden = nn(normed2, w_in[r]) + rows_below[r][0:1]
        density = jnp.exp(hidden * hidden * -0.5) * (1.0 / math.sqrt(2.0 * math.pi))
        share = 0.5 * (1.0 + lax.erf(hidden * math.sqrt(0.5)))
        value = hidden * share
        activated[r] = value
        slope[r] = share + hidden * density
        fold_a += lanes_folded(value)
        fold_b += lanes_folded(value * value)
    centre = jnp.sum(fold_a, axis=1, keepdims=True) * (1.0 / ff)
    spread = jnp.sum(fold_b, axis=1, keepdims=True) * (1.0 / ff) - centre * centre
    scaling = lax.rsqrt(spread + epsilon)

    fold_a = jnp.zeros((tokens, 128), F32)
    fold_b = jnp.zeros((tokens, 128), F32)
    projected = jnp.zeros((tokens, D), F32)
    for r in range(4):
        for copy in loads[1, r]:
            copy.wait()
        gain = rows_below[r][1:2]
        unit = (activated[r] - centre) * scaling
        activated[r] = unit
        mixed = (unit * gain).astype(BF16)
        projected += nt(mixed, w_out[r])
        store(1, r, nn(cot_flipped, mixed))
        grad = nn(cot, w_out[r])
        vec_out_ref[r, 0:1, :] = jnp.sum(grad * unit, axis=0, keepdims=True)
        scaled = grad * gain
        d_mixed[r] = scaled
        fold_a += lanes_folded(scaled)
        fold_b += lanes_folded(scaled * unit)
    first = jnp.sum(fold_a, axis=1, keepdims=True) * (1.0 / ff)
    second = jnp.sum(fold_b, axis=1, keepdims=True) * (1.0 / ff)
    out_ref[...] = (middle[...] + (projected + vec_ref[2:3, :])).astype(BF16)

    d_normed2 = jnp.zeros((tokens, D), F32)
    for r in range(4):
        grad = (slope[r] * (scaling * (d_mixed[r] - first - activated[r] * second))).astype(BF16)
        vec_out_ref[r, 1:2, :] = jnp.sum(grad.astype(F32), axis=0, keepdims=True)
        stores[r].wait()
        store(0, r, nn(flipped, grad))
        d_normed2 += nt(grad, w_in[r])

    cot = cot.astype(F32)
    unit = unit2[...]
    d_middle = cot + rows_back(d_normed2 * vec_ref[1:2, :], unit, scaling2)
    middle_grad_ref[...] = d_middle
    d_branch = d_middle.astype(BF16)
    norm2_part = jnp.sum(d_normed2 * unit, axis=0, keepdims=True)
    project_bias_part = jnp.sum(cot, axis=0, keepdims=True)
    output_bias_part = jnp.sum(d_branch.astype(F32), axis=0, keepdims=True)
    d_context = nt(weight_o, d_branch)
    o_grad = nn(context, d_branch)
    unit = unit_c[...]
    inner_part = jnp.sum(d_context * unit, axis=1, keepdims=True)
    inner_part = jnp.broadcast_to(inner_part, (D, 128)).T[0:1]
    scaled = d_context * gain_c
    first = jnp.mean(scaled, axis=0, keepdims=True)
    second = jnp.mean(scaled * unit, axis=0, keepdims=True)
    grad = (scaling_c * (scaled - first - unit * second)).astype(BF16)
    for i, g_ref in enumerate((g0, g1, g2, g3)):
        rows = slice(i * inner_rows, (i + 1) * inner_rows)
        g_ref[...] = grad[rows]
        vec_out_ref[i, 2:3, 0:inner_rows] = inner_part[:, rows]
        vec_out_ref[i, 2:3, inner_rows:D] = jnp.zeros((1, D - inner_rows), F32)
        vec_out_ref[i, 3:4, :] = norm2_part
        vec_out_ref[i, 4:5, :] = project_bias_part
        vec_out_ref[i, 5:6, :] = output_bias_part
        vec_out_ref[i, 6:8, :] = jnp.zeros((2, D), F32)
    count, side_rows, _ = side_keep.shape[1:]
    for i in range(4):
        side = (side_keep, side_send)[i % 2]
        vectors = vec_out_ref[i]
        for d in range(count):
            start = i * inner_rows + d * (side_rows - 8)
            block = jnp.concatenate([o_grad[start : start + side_rows - 8], vectors], axis=0)
            side[i // 2, d] = block.astype(BF16)
    for r in range(4):
        stores[r].wait()


def token_section(info, attended, packs, inputs, cotangent, vectors, sources, pieces, piece_count, count):
    tokens = inputs.shape[0]
    inner_rows = attended[0].shape[0]
    ff_slice = sources[0].shape[-1]
    fixed = lambda *shape: pl.BlockSpec(shape, lambda s, info: (0,) * len(shape))
    anywhere = pl.BlockSpec(memory_space=pl.ANY)
    grad_piece = jax.ShapeDtypeStruct((inner_rows, tokens), BF16)
    grad_pair = jax.ShapeDtypeStruct((2, D, ff_slice), BF16)
    return pl.pallas_call(
        functools.partial(token_kernel, pieces, len(sources)),
        grid_spec=pltpu.PrefetchScalarGridSpec(
            num_scalar_prefetch=1,
            grid=(1,),
            in_specs=[anywhere] * len(sources)
            + [fixed(*a.shape) for a in attended]
            + [fixed(*p.shape) for p in packs]
            + [fixed(tokens, D), fixed(tokens, D), fixed(8, D)],
            out_specs=[fixed(tokens, D), fixed(tokens, D)]
            + [fixed(inner_rows, tokens)] * 4
            + [anywhere] * 4
            + [fixed(2, count, inner_rows // count + 8, D)] * 2,
            scratch_shapes=[
                pltpu.VMEM((4, D, ff_slice), BF16),
                pltpu.VMEM((4, D, ff_slice), BF16),
                pltpu.VMEM((4, D, ff_slice), BF16),
                pltpu.VMEM((4, tokens, ff_slice), F32),
                pltpu.VMEM((4, tokens, ff_slice), F32),
                pltpu.VMEM((4, tokens, ff_slice), F32),
                pltpu.VMEM((D, tokens), F32),
                pltpu.VMEM((tokens, D), F32),
                pltpu.VMEM((tokens, D), F32),
                pltpu.VMEM((4, 8, D), F32),
                pltpu.SemaphoreType.DMA((2, 4, piece_count)),
                pltpu.SemaphoreType.DMA((2, 4)),
            ],
        ),
        out_shape=[
            jax.ShapeDtypeStruct((tokens, D), BF16),
            jax.ShapeDtypeStruct((tokens, D), F32),
            *[grad_piece] * 4,
            *[grad_pair] * 4,
            *[jax.ShapeDtypeStruct((2, count, inner_rows // count + 8, D), BF16)] * 2,
        ],
        compiler_params=pltpu.CompilerParams(
            dimension_semantics=("arbitrary",), vmem_limit_bytes=60 << 20
        ),
        cost_estimate=pl.CostEstimate(
            flops=20_000_000_000, bytes_accessed=30_000_000, transcendentals=4_000_000
        ),
        name="token_section",
    )(info, *sources, *attended, *packs, inputs, cotangent, vectors)


def swap(values, distance):
    count = lax.axis_size("head")
    return lax.ppermute(values, "head", [(i, i ^ distance) for i in range(count)])


def dp_swap(values, distance):
    count = lax.axis_size("dp")
    return lax.ppermute(values, "dp", [(i, i ^ distance) for i in range(count)])


def pick(values, index, axis):
    return lax.dynamic_index_in_dim(values, index, axis, keepdims=False)


def wide(values):
    return values.astype(F32)


def swap_near(values, axis):
    near = lax.axis_index("dp") & 1
    return dp_swap(pick(values, 1 - near, axis).astype(BF16), 1)


def keep_near(values, axis):
    return pick(values, lax.axis_index("dp") & 1, axis)


def keep_far(values, axis):
    return pick(values, lax.axis_index("dp") >> 1, axis)


def far_of(values, m, axis):
    return pick(values, (lax.axis_index("dp") >> 1) ^ m, axis).astype(BF16)


def far_swaps(payload):
    count = lax.axis_size("dp") // 2
    return [dp_swap(payload(m), 2 * m) for m in range(1, count)]


def after(value, *others):
    return lax.optimization_barrier((value,) + others)[0]


def local(
    inputs,
    cotangent,
    lengths,
    norm1_gain,
    query_weight,
    query_bias,
    key_weight,
    value_weight,
    value_bias,
    inner_gain,
    output_weight,
    output_bias,
    norm2_gain,
    hidden_weight,
    hidden_bias,
    hidden_gain,
    project_weight,
    project_bias,
):
    dp_count = lax.axis_size("dp")
    far_count = dp_count // 2
    me = lax.axis_index("head")
    heads = query_weight.shape[1] // HEAD_DIM
    shard_rows = hidden_weight.shape[0]
    slice_cols = hidden_weight.shape[1]
    inner_rows = output_weight.shape[0]

    first_length = lengths[0, 0]
    limits = [
        jnp.where(first_length > SHORT, first_length - SHORT * (me ^ r), lengths[0, me ^ r])
        for r in range(4)
    ]
    place = lax.axis_index("dp")
    info = jnp.stack([first_length] + limits + [me, place & 1, place >> 1]).astype(jnp.int32)

    first_weight, second_weight = hidden_weight, project_weight.T
    straight = shard_rows % 16 == 0

    gain1 = wide(norm1_gain)
    normed1 = first_norm(inputs, gain1[None])
    near = swap(normed1, 1)
    across = swap(normed1, 2)

    if straight:
        both = jnp.concatenate([first_weight, second_weight], axis=0)
        both_far = [both] + far_swaps(lambda m: both)

    pack = jnp.concatenate(
        [
            jnp.pad(jnp.concatenate([output_weight, inner_gain[:, None]], axis=1), ((0, 0), (0, 127))),
            jnp.pad(jnp.stack([hidden_bias, hidden_gain]), ((0, 14), (0, D + 128 - slice_cols))),
        ],
        axis=0,
    )
    pack_across = swap(pack, 2)
    pack_near = swap(pack, 1)

    def per_head(weight):
        return weight.T.reshape(heads, HEAD_DIM, D)

    zero_bias = jnp.zeros_like(query_bias)
    packed_weight = jnp.concatenate(
        [per_head(query_weight), per_head(key_weight), per_head(value_weight)], axis=1
    )
    packed_bias = wide(
        jnp.concatenate(
            [b.reshape(heads, 1, HEAD_DIM) for b in (query_bias, zero_bias, value_bias)], axis=2
        )
    )
    across, info, packed_weight, packed_bias, pack = lax.optimization_barrier(
        (across, info, packed_weight, packed_bias, pack)
    )
    far = swap(across, 1)
    rows = (normed1, near, across, far)
    waits = []
    if straight:
        first_own = jnp.stack([w[:shard_rows] for w in both_far])
        second_own = jnp.stack([w[shard_rows:] for w in both_far])
        first_own, second_own = lax.optimization_barrier((first_own, second_own))
        first_near = dp_swap(first_own, 1)
        second_across = swap(second_own, 2)
        waits = [first_own, second_own]
    early = attention_forward(after(info, *waits), rows, packed_weight, packed_bias, 0, 1, [])
    waits = []
    if straight:
        pack_across, first_near, second_across, early = lax.optimization_barrier(
            (pack_across, first_near, second_across, early)
        )
        first_block = jnp.stack([first_own, first_near])
        second_block = jnp.stack([second_own, second_across])
        first_across = swap(first_block, 2)
        second_near = dp_swap(second_block, 1)
        first_sides = [first_block, swap(first_block, 1), first_across]
        second_sides = [second_block, second_near, swap(second_block, 1)]
        waits = [first_block, second_block, first_sides[1], second_sides[2]]
    pack_far = swap(pack_across, 1)
    packs = (pack, pack_near, pack_across, pack_far)
    info_now = after(info, early[0], pack_far, pack_near, *waits)
    late = attention_forward(info_now, rows, packed_weight, packed_bias, 1, heads - 1, early[:4])
    attended_heads = late[:4]

    def exchange(pieces):
        return [pieces[0]] + [swap(pieces[r], r) for r in (1, 2, 3)]

    attended = exchange(attended_heads)
    vectors = jnp.concatenate(
        [wide(jnp.stack([output_bias, norm2_gain, project_bias])), jnp.zeros((5, D), F32)], axis=0
    )
    if straight:
        first_across, second_near, *attended = lax.optimization_barrier((first_across, second_near, *attended))
        first_sides.append(swap(first_across, 1))
        second_sides.append(swap(second_near, 1))
        sources = first_sides + second_sides

        def pieces(info, refs, which, r):
            found = []
            for n in range(2):
                for m in range(far_count):
                    start = ((info[7] ^ m) * 2 + (info[6] ^ n)) * shard_rows
                    if which == 0:
                        source = refs[r].at[n, m]
                    else:
                        source = refs[4 + (r % 2) * 2 + n].at[r // 2, m]
                    found.append((source, pl.multiple_of(start, shard_rows)))
            return found

        piece_count = dp_count
    else:
        shards = jnp.concatenate([first_weight, second_weight], axis=0)
        gathered = lax.all_gather(shards, ("dp", "head"), axis=0, tiled=False)
        gathered = gathered.reshape(dp_count, 4, 2, shard_rows, slice_cols)
        sources = [gathered.transpose(1, 2, 0, 3, 4).reshape(4, 2, D, slice_cols)]
        pieces = lambda info, refs, which, r: [(refs[0].at[info[5] ^ r, which], 0)]
        piece_count = 1
    output, d_middle, *rest = token_section(
        info, attended, packs, inputs, cotangent, vectors, sources, pieces, piece_count,
        dp_count if straight else 8,
    )
    attended_grad, (in_keep, in_send, out_keep, out_send, side_keep, side_send) = rest[:4], rest[4:]

    grads = exchange(attended_grad)
    out_got, in_got = swap(out_send, 1), swap(in_send, 1)
    if side_keep.shape[1] != dp_count:
        def recut(side):
            o_part = side[:, :, :-8].reshape(2, dp_count, -1, D)
            vec_part = jnp.broadcast_to(side[:, 0:1, -8:], (2, dp_count, 8, D))
            return jnp.concatenate([o_part, vec_part], axis=2)

        side_keep, side_send = recut(side_keep), recut(side_send)
    side_got = swap(side_send, 1)
    by_pair = lambda v: v.reshape(far_count, 2, -1, D)
    blocks = (far_count, 2, shard_rows, slice_cols)

    def out_part(q, take):
        weight = wide(take(out_keep[q].reshape(blocks))) + wide(take(out_got[q].reshape(blocks)))
        return jnp.concatenate([weight, wide(take(by_pair(side_keep[q]))) + wide(take(by_pair(side_got[q])))], axis=1)

    mine = lambda v: pick(v, place & 1, 1)
    theirs = lambda v: pick(v, 1 - (place & 1), 1)
    head_rows = 256 // dp_count
    by_place = lambda v: v.reshape(2, far_count, head_rows, D)
    other_half = lambda v: pick(by_place(v), 1 - (place & 1), 0)

    def half_sum(d_w, got):
        return (wide(keep_near(by_place(d_w), 0)) + wide(got)).astype(BF16)

    def saved_of(h):
        return (early[4:], 0) if h == 0 else (late[4:], h - 1)

    def head_step(h, info, packed, d_weights):
        saved, local_head = saved_of(h)
        return attention_backward(
            h, h == heads - 1, info, grads, attended_heads, saved, local_head, rows, packed_weight, packed, d_weights
        )

    across_sent = (wide(in_keep[1]) + wide(in_got[1])).astype(BF16)
    own_sent = out_part(0, theirs).astype(BF16)
    lane_halves = (slice(0, slice_cols // 2), slice(slice_cols // 2, slice_cols))
    across_halves = [across_sent[:, lanes] for lanes in lane_halves]
    own_sent, across_halves, grads = lax.optimization_barrier((own_sent, across_halves, grads))
    across_got_a = swap(across_halves[0], 2)
    own_near = dp_swap(own_sent, 1)
    packed_0, d_weight_0 = head_step(0, after(info, own_sent, *across_halves), [], [])

    packed_0, d_weight_0, own_near, across_got_a, across_halves[1] = lax.optimization_barrier(
        (packed_0, d_weight_0, own_near, across_got_a, across_halves[1])
    )
    across_got_b = swap(across_halves[1], 2)
    own_half = out_part(0, mine) + wide(own_near)
    own_payload = [far_of(own_half, m, 0) for m in range(1, far_count)]
    cross_sent = out_part(1, theirs).astype(BF16)
    sent_0 = other_half(d_weight_0)
    sent_0, cross_sent, *own_payload = lax.optimization_barrier((sent_0, cross_sent, *own_payload))
    got_0 = dp_swap(sent_0, 1)
    cross_near = dp_swap(cross_sent, 1)
    own_far = [dp_swap(p, 2 * (m + 1)) for m, p in enumerate(own_payload)]
    packed_1, d_weight_1 = head_step(1, after(info, sent_0, cross_sent, *own_payload), [packed_0], [d_weight_0])

    packed_1, d_weight_1, got_0, cross_near, across_got_b, *own_far = lax.optimization_barrier(
        (packed_1, d_weight_1, got_0, cross_near, across_got_b, *own_far)
    )
    half_0 = half_sum(d_weight_0, got_0)
    cross_half = out_part(1, mine) + wide(cross_near)
    cross_payload = [
        jnp.concatenate([far_of(half_0, m, 0), far_of(cross_half, m, 0)], axis=0) for m in range(1, far_count)
    ]
    across_got = jnp.concatenate([across_got_a, across_got_b], axis=1)
    in_sum = (wide(in_keep[0]) + wide(in_got[0]) + wide(across_got)).reshape(blocks)
    in_sent = theirs(in_sum).astype(BF16)
    sent_1 = other_half(d_weight_1)
    sent_1, in_sent, *cross_payload = lax.optimization_barrier((sent_1, in_sent, *cross_payload))
    got_1 = dp_swap(sent_1, 1)
    in_near = dp_swap(in_sent, 1)
    cross_far = [dp_swap(p, 2 * (m + 1)) for m, p in enumerate(cross_payload)]
    d_weight_2, dx_keep, dx_send, gain_part = head_step(
        2, after(info, sent_1, in_sent, *cross_payload), [packed_0, packed_1], [d_weight_0, d_weight_1]
    )

    d_weight_2, dx_keep, dx_send, gain_part, got_1, in_near, *cross_far = lax.optimization_barrier(
        (d_weight_2, dx_keep, dx_send, gain_part, got_1, in_near, *cross_far)
    )
    hr = head_rows
    near_rows = swap(dx_send, 1)
    gain_sum = gain_part + swap(gain_part, 2)
    got_2 = dp_swap(other_half(d_weight_2), 1)
    quarter_0 = (wide(keep_far(half_0, 0)) + sum(wide(g[:hr]) for g in cross_far)).astype(BF16)
    half_1 = half_sum(d_weight_1, got_1)
    step_1 = far_swaps(lambda m: jnp.concatenate([quarter_0, far_of(half_1, m, 0)], axis=0))
    cross_total = keep_far(cross_half, 0) + sum(wide(g[hr:]) for g in cross_far)
    cross_sum = (wide(dx_keep[1]) + wide(near_rows[1])).astype(BF16)
    cross_sum, cross_total = lax.optimization_barrier((cross_sum, cross_total))
    gain_sum = gain_sum + swap(gain_sum, 1)
    out_got_across = swap(cross_total.astype(BF16), 2)
    cross_got = swap(cross_sum, 2)

    whole_0 = jnp.stack([quarter_0] + [g[:hr] for g in step_1])
    quarter_1 = (wide(keep_far(half_1, 0)) + sum(wide(g[hr:]) for g in step_1)).astype(BF16)
    half_2 = half_sum(d_weight_2, got_2)
    quarter_1, whole_0, half_2 = (after(v, cross_sum) for v in (quarter_1, whole_0, half_2))
    other_0 = dp_swap(whole_0, 1)
    payload_2 = [jnp.concatenate([quarter_1, far_of(half_2, m, 0)], axis=0) for m in range(1, far_count)]
    step_2 = [dp_swap(p, 2 * (m + 1)) for m, p in enumerate(payload_2)]
    in_half = after(mine(in_sum) + wide(in_near), *payload_2)
    in_far = far_swaps(lambda m: far_of(in_half, m, 0))
    own_total = keep_far(own_half, 0) + sum(wide(g) for g in own_far)
    out_total = own_total + wide(out_got_across)
    o_chunk = out_total[shard_rows:-8].astype(BF16)
    o_rows = o_chunk.shape[0]
    vec_total = out_total[-8:]

    def in_two(values):
        high = values.astype(BF16)
        low = (values - wide(high)).astype(BF16)
        return jnp.concatenate([high[0:4], low[0:4]], axis=0)

    def from_two(rows_of):
        return wide(rows_of[0:1]) + wide(rows_of[4:5])

    whole_1 = jnp.stack([quarter_1] + [g[:hr] for g in step_2])
    quarter_2 = (wide(keep_far(half_2, 0)) + sum(wide(g[hr:]) for g in step_2)).astype(BF16)
    other_1 = dp_swap(whole_1, 1)
    third = jnp.concatenate([quarter_2, o_chunk, in_two(gain_sum)], axis=0)
    step_3 = far_swaps(lambda m: third)
    whole_2 = jnp.stack([quarter_2] + [g[:hr] for g in step_3])
    o_own = jnp.stack([o_chunk] + [g[hr : hr + o_rows] for g in step_3])
    gain_sum = gain_sum + sum(from_two(g[hr + o_rows :]) for g in step_3)
    last_sent = jnp.concatenate([whole_2.reshape(-1, D), o_own.reshape(-1, D), in_two(gain_sum)], axis=0)
    last_near = dp_swap(after(last_sent, cross_got), 1)
    other_2 = last_near[: far_count * hr].reshape(whole_2.shape)
    o_other = last_near[far_count * hr : far_count * (hr + o_rows)].reshape(o_own.shape)
    norm1_total = (gain_sum[0:1] + from_two(last_near[far_count * (hr + o_rows) :]))[0] / gain1
    hidden_grad = keep_far(in_half, 0) + sum(wide(g) for g in in_far)

    input_grad = input_gradient(inputs, gain1[None], d_middle, dx_keep, near_rows, cross_got)

    def in_order(own, neighbour):
        total = jnp.zeros((2, far_count) + own.shape[1:], own.dtype)
        for m in range(far_count):
            for n, part in enumerate((own, neighbour)):
                total = lax.dynamic_update_slice(
                    total, part[m][None, None], ((place & 1) ^ n, (place >> 1) ^ m, 0, 0)
                )
        return total

    halves = [whole_0, other_0, whole_1, other_1, whole_2, other_2]
    finish_info = info
    if hr % 16:
        totals = [in_order(halves[2 * h], halves[2 * h + 1]) for h in range(heads)]
        halves = [t[n].reshape(1, -1, D) for t in totals for n in range(2)]
        finish_info = jnp.zeros_like(info)
    query_grad, key_grad, value_grad, bias_rows = finish(finish_info, halves)
    bias_rows = bias_rows[:, 0, :192]
    o_total = wide(in_order(o_own, o_other).transpose(1, 0, 2, 3).reshape(inner_rows, D))
    project_grad = out_total[:shard_rows].T
    return (
        output,
        input_grad,
        norm1_total,
        query_grad.T,
        bias_rows[:, 0:64].reshape(-1),
        key_grad.T,
        value_grad.T,
        bias_rows[:, 128:192].reshape(-1),
        vec_total[2, :inner_rows],
        o_total,
        vec_total[5],
        vec_total[3],
        hidden_grad,
        vec_total[1],
        vec_total[0],
        project_grad,
        vec_total[4],
    )


def solution(mesh):
    rows = P(("dp", "head"), None)
    columns = P(None, "head")
    head = P("head")
    return jax.shard_map(
        local,
        mesh=mesh,
        in_specs=(
            rows, rows, P("dp", None), P(), columns, head, columns, columns, head, head,
            P("head", None), P(), P(), P("dp", "head"), head, head, P("head", "dp"), P(),
        ),
        out_specs=(
            rows, rows, P(), columns, head, columns, columns, head, head, P("head", None),
            P(), P(), P("dp", "head"), head, head, P("head", "dp"), P(),
        ),
        check_vma=False,
    )
```

```python
import functools
import math

import jax
import jax.numpy as jnp
from jax import lax
from jax.experimental import pallas as pl
from jax.experimental.pallas import tpu as pltpu
from jax.sharding import PartitionSpec as P

D = 768
HEAD_DIM = 64
FF = 3072
SHORT = 512
SLOT = 4 * SHORT

BF16 = jnp.bfloat16
F32 = jnp.float32
epsilon = 1e-05
excluded = 1e30
SCALE = HEAD_DIM ** (-0.5)
LOG2_SCALE = SCALE * math.log2(math.e)
LN2 = math.log(2.0)
QUERY_ROWS = 512
KEY_ROWS = 256
VMEM_LIMIT = 56 << 20


def nt(left, right):
    return lax.dot_general(left, right, (((1,), (1,)), ((), ())), preferred_element_type=F32)


def nn(left, right):
    return lax.dot_general(left, right, (((1,), (0,)), ((), ())), preferred_element_type=F32)


def tn(left, right):
    return lax.dot_general(left, right, (((0,), (0,)), ((), ())), preferred_element_type=F32)


def attention_forward_kernel(before, info, *refs):
    x_refs, (w_ref, b_ref), earlier = refs[0:4], refs[4:6], refs[6 : 6 + 4 * (before > 0)]
    *o_refs, lse_ref, q_ref, k_ref, v_ref = refs[6 + len(earlier) :]
    head = pl.program_id(0)
    lane = lax.broadcasted_iota(jnp.int32, (SHORT, 128), 1)
    row = lax.broadcasted_iota(jnp.int32, (SHORT, 128), 0)
    for o_ref, early in zip(o_refs, earlier):

        @pl.when(head == 0)
        def _():
            o_ref[0 : before * HEAD_DIM, :] = early[...]

    for block, x_ref in enumerate(x_refs):
        rows = pl.ds(block * SHORT, SHORT)
        packed = (nt(x_ref[...], w_ref[0]) + b_ref[0]).astype(BF16)
        inside = jnp.where(row < info[1 + block], 1.0, 0.0).astype(F32)
        q_flags = jnp.where(lane == 0, inside, jnp.where(lane == 1, 1.0 - inside, 0.0))
        k_flags = jnp.where(
            lane == 0, (inside - 1.0) * excluded, jnp.where(lane == 1, inside * -excluded, 0.0)
        )
        q, k, v = packed[:, 0:64], packed[:, 64:128], packed[:, 128:192]
        scaled = k.astype(F32) * LOG2_SCALE
        high = scaled.astype(BF16)
        low = (scaled - high.astype(F32)).astype(BF16)
        q_ref[0, rows, :] = jnp.concatenate([q, q, q_flags.astype(BF16)], axis=1)
        k_ref[0, rows, :] = jnp.concatenate([high, low, k_flags.astype(BF16)], axis=1)
        v_ref[0, rows, :] = jnp.concatenate([v, jnp.ones((SHORT, 64), BF16)], axis=1)

    out_rows = pl.ds(pl.multiple_of((before + head) * HEAD_DIM, HEAD_DIM), HEAD_DIM)

    def block_of(start, keys):
        scores = nt(q_ref[0, pl.ds(start, QUERY_ROWS), :], k_ref[0, keys, :])
        top = jnp.max(scores, axis=1, keepdims=True)
        weights = jnp.exp2(scores - top).astype(BF16)
        out = nn(weights, v_ref[0, keys, :])
        out_lane = lax.broadcasted_iota(jnp.int32, (QUERY_ROWS, 128), 1)
        out = jnp.where(out_lane == 65, jnp.broadcast_to(top, (QUERY_ROWS, 128)), out).T
        total = out[64:65]
        o_refs[start // SHORT][out_rows, pl.ds(start % SHORT, QUERY_ROWS)] = (
            out[0:64] * (1.0 / total)
        ).astype(BF16)
        lse_ref[0, :, pl.ds(start, QUERY_ROWS)] = out[65:66] + jnp.log2(total)

    longer = info[0] > SHORT

    @pl.when(longer)
    def _():
        for start in range(0, SLOT, QUERY_ROWS):
            block_of(start, pl.ds(0, SLOT))

    @pl.when(jnp.logical_not(longer))
    def _():
        for start in range(0, SLOT, QUERY_ROWS):
            block_of(start, pl.ds(start // SHORT * SHORT, SHORT))


def head_spec(*shape):
    return pl.BlockSpec((1,) + shape, lambda h, info: (h,) + (0,) * len(shape))


def whole_spec(*shape):
    return pl.BlockSpec(shape, lambda h, info: (0,) * len(shape))


def attention_forward(info, rows, weights, biases, before, count, earlier):
    out_rows = (before + count) * HEAD_DIM
    later = lambda *shape: pl.BlockSpec((1,) + shape, lambda h, info: (before + h,) + (0,) * len(shape))
    return pl.pallas_call(
        functools.partial(attention_forward_kernel, before),
        grid_spec=pltpu.PrefetchScalarGridSpec(
            num_scalar_prefetch=1,
            grid=(count,),
            in_specs=[whole_spec(SHORT, D)] * 4
            + [later(192, D), later(1, 192)]
            + [whole_spec(before * HEAD_DIM, SHORT)] * len(earlier),
            out_specs=[whole_spec(out_rows, SHORT)] * 4
            + [head_spec(1, SLOT), head_spec(SLOT, 256), head_spec(SLOT, 256), head_spec(SLOT, 128)],
        ),
        out_shape=[jax.ShapeDtypeStruct((out_rows, SHORT), BF16)] * 4
        + [
            jax.ShapeDtypeStruct((count, 1, SLOT), F32),
            jax.ShapeDtypeStruct((count, SLOT, 256), BF16),
            jax.ShapeDtypeStruct((count, SLOT, 256), BF16),
            jax.ShapeDtypeStruct((count, SLOT, 128), BF16),
        ],
        compiler_params=pltpu.CompilerParams(
            dimension_semantics=("arbitrary",), vmem_limit_bytes=VMEM_LIMIT
        ),
        cost_estimate=pl.CostEstimate(
            flops=8_000_000_000 * count, bytes_accessed=4_000_000 * count, transcendentals=4_000_000 * count
        ),
        name="attention_forward",
    )(info, *rows, weights, biases, *earlier)


def attention_backward_kernel(*refs):
    info, *pieces = refs[:9]
    lse_ref, q_ref, k_ref, v_ref = refs[9:13]
    x_refs = refs[13:17]
    rest = list(refs[17:])
    packed_ref, dw_ref, grad, dq, delta, packed, x_all, sems = rest
    copies = [
        pltpu.make_async_copy(x_ref, x_all.at[block], sems.at[block]) for block, x_ref in enumerate(x_refs)
    ]
    for copy in copies:
        copy.start()
    for block, (g_ref, o_ref) in enumerate(zip(pieces[:4], pieces[4:])):
        g = g_ref[...].astype(F32)
        cols = pl.ds(block * SHORT, SHORT)
        delta[:, cols] = jnp.sum(g * o_ref[...].astype(F32), axis=0, keepdims=True)
        grad[cols, :] = g.T.astype(BF16)

    def block_of(start, queries, first):
        rows = pl.ds(start, KEY_ROWS)
        k = k_ref[0, rows, :]
        q = q_ref[0, queries, :]
        g = grad[queries, :]
        weights = jnp.exp2(nt(k, q) - lse_ref[0, :, queries])
        d_probs = nt(v_ref[0, rows, 0:64], g)
        d_scores = (weights * (d_probs - delta[:, queries])).astype(BF16)
        packed[rows, 128:192] = nn(weights.astype(BF16), g).astype(BF16)
        packed[rows, 64:128] = (nn(d_scores, q[:, 0:128])[:, 0:64] * SCALE).astype(BF16)
        term = tn(d_scores, k[:, 0:128])
        if first:
            dq[queries, :] = term
        else:
            dq[queries, :] += term

    longer = info[0] > SHORT

    @pl.when(longer)
    def _():
        for start in range(0, SLOT, KEY_ROWS):
            block_of(start, pl.ds(0, SLOT), start == 0)

    @pl.when(jnp.logical_not(longer))
    def _():
        for start in range(0, SLOT, KEY_ROWS):
            block_of(start, pl.ds(start // SHORT * SHORT, SHORT), start % SHORT == 0)

    total = dq[...]
    packed[:, 0:64] = ((total[:, 0:64] + total[:, 64:128]) * LN2).astype(BF16)
    packed_ref[...] = packed[...]
    for copy in copies:
        copy.wait()
    d_weight = jnp.zeros((192, D), F32)
    d_bias = jnp.zeros((1, 192), F32)
    for block in range(4):
        part = packed[pl.ds(block * SHORT, SHORT), :]
        d_weight += tn(part, x_all[block])
        d_bias += jnp.sum(part.astype(F32), axis=0, keepdims=True)
    dw_ref[0:192, :] = d_weight.astype(BF16)
    d_bias = jnp.concatenate([d_bias, jnp.zeros((1, D - 192), F32)], axis=1)
    row = lax.broadcasted_iota(jnp.int32, (64, D), 0)
    dw_ref[192:256, :] = jnp.where(row == 0, d_bias, 0.0).astype(BF16)


def attention_backward(head, info, grads, attended, saved, local_head, rows):
    one = lambda *shape: pl.BlockSpec((1,) + shape, lambda i, info: (local_head,) + (0,) * len(shape))
    in_specs = (
        [pl.BlockSpec((HEAD_DIM, SHORT), lambda i, info: (head, 0))] * 8
        + [one(1, SLOT), one(SLOT, 256), one(SLOT, 256), one(SLOT, 128)]
        + [pl.BlockSpec(memory_space=pl.ANY)] * 4
    )
    operands = [*grads, *attended, *saved, *rows]
    out_specs = [whole_spec(SLOT, 192), whole_spec(256, D)]
    out_shape = [jax.ShapeDtypeStruct((SLOT, 192), BF16), jax.ShapeDtypeStruct((256, D), BF16)]
    return pl.pallas_call(
        attention_backward_kernel,
        grid_spec=pltpu.PrefetchScalarGridSpec(
            num_scalar_prefetch=1,
            grid=(1,),
            in_specs=in_specs,
            out_specs=out_specs,
            scratch_shapes=[
                pltpu.VMEM((SLOT, HEAD_DIM), BF16),
                pltpu.VMEM((SLOT, 128), F32),
                pltpu.VMEM((1, SLOT), F32),
                pltpu.VMEM((SLOT, 192), BF16),
                pltpu.VMEM((4, SHORT, D), BF16),
                pltpu.SemaphoreType.DMA((4,)),
            ],
        ),
        out_shape=out_shape,
        compiler_params=pltpu.CompilerParams(
            dimension_semantics=("arbitrary",), vmem_limit_bytes=VMEM_LIMIT
        ),
        cost_estimate=pl.CostEstimate(
            flops=15_000_000_000, bytes_accessed=8_000_000, transcendentals=4_000_000
        ),
        name="attention_backward",
    )(info, *operands)


def input_part_kernel(heads, *refs):
    packed, (w_ref,), d_weights = refs[:heads], refs[heads : heads + 1], refs[heads + 1 : 2 * heads + 1]
    dx_keep, dx_send, gain_ref = refs[2 * heads + 1 :]
    for block in (1, 3, 2, 0):
        rows = pl.ds(block * SHORT, SHORT)
        term = nn(packed[0][rows, :], w_ref[0])
        for h in range(1, heads):
            term += nn(packed[h][rows, :], w_ref[h])
        out = dx_send if block % 2 else dx_keep
        out[block // 2] = term.astype(BF16)
    gain = jnp.zeros((1, D), F32)
    for h in range(heads):
        gain += jnp.sum(d_weights[h][0:192, :].astype(F32) * w_ref[h].astype(F32), axis=0, keepdims=True)
    gain_ref[...] = jnp.broadcast_to(gain, (8, D))


def input_part(packed, weights, d_weights):
    heads = len(packed)
    return pl.pallas_call(
        functools.partial(input_part_kernel, heads),
        out_shape=[jax.ShapeDtypeStruct((2, SHORT, D), BF16)] * 2 + [jax.ShapeDtypeStruct((8, D), F32)],
        compiler_params=pltpu.CompilerParams(vmem_limit_bytes=VMEM_LIMIT),
        cost_estimate=pl.CostEstimate(flops=6_000_000_000, bytes_accessed=8_000_000, transcendentals=0),
        name="input_part",
    )(*packed, weights, *d_weights)


def step_call(kernel, name, info, operands, outs, first_blocks=()):
    def spec(i, shape):
        if i in first_blocks:
            return pl.BlockSpec((1,) + shape[1:], lambda j, info: (info[7],) + (0,) * (len(shape) - 1))
        return pl.BlockSpec(shape, lambda j, info: (0,) * len(shape))

    return pl.pallas_call(
        kernel,
        grid_spec=pltpu.PrefetchScalarGridSpec(
            num_scalar_prefetch=1,
            grid=(1,),
            in_specs=[spec(i, v.shape) for i, v in enumerate(operands)],
            out_specs=[pl.BlockSpec(shape, lambda j, info, n=len(shape): (0,) * n) for shape, _ in outs],
        ),
        out_shape=[jax.ShapeDtypeStruct(shape, kind) for shape, kind in outs],
        name=name,
    )(info, *operands)


def opening_kernel(info, half_0, d_w1, bundle, cross_half, own_half, *refs):
    count, rows, _ = half_0.shape
    cross, own, outs = refs[: count - 1], refs[count - 1 : 2 * count - 2], refs[2 * count - 2 :]
    quarter, half_1, cross_total, own_total = outs[:4]
    near, far = info[6], info[7]
    total = half_0[far].astype(F32)
    for g in cross:
        total += g[0:rows, :].astype(F32)
    quarter[...] = total.astype(BF16)
    for m in range(count):
        value = d_w1[near * count + m].astype(F32) + bundle[m, bundle.shape[1] - rows :, :].astype(F32)
        half_1[m] = value.astype(BF16)
    for m in range(1, count):
        outs[3 + m][0:rows, :] = quarter[...]
        outs[3 + m][rows : 2 * rows, :] = half_1[far ^ m]
    total = cross_half[0]
    for g in cross:
        total += g[rows:, :].astype(F32)
    cross_total[...] = total.astype(BF16)
    total = own_half[0]
    for g in own:
        total += g[...].astype(F32)
    own_total[...] = total


def opening(info, half_0, d_w1, bundle, cross_half, own_half, cross, own):
    count, rows, _ = half_0.shape
    blocks = lambda v: v.reshape(2 * count, rows, D)
    part = cross_half.shape[1]
    outs = [((rows, D), BF16), (half_0.shape, BF16), ((part, D), BF16), ((part, D), F32)]
    outs += [((2 * rows, D), BF16)] * (count - 1)
    operands = [half_0, blocks(d_w1), bundle, cross_half, own_half, *cross, *own]
    return step_call(opening_kernel, "opening", info, operands, outs, (3, 4))


def middle_kernel(info, quarter_0, half_1, d_w2, near_got, *refs):
    count, rows, _ = half_1.shape
    got, (whole, quarter, half_2, *payload) = refs[: count - 1], refs[count - 1 :]
    near, far = info[6], info[7]
    whole[0] = quarter_0[...]
    total = half_1[far].astype(F32)
    for m, g in enumerate(got):
        whole[m + 1] = g[0:rows, :]
        total += g[rows : 2 * rows, :].astype(F32)
    quarter[...] = total.astype(BF16)
    for m in range(count):
        half_2[m] = (d_w2[near * count + m].astype(F32) + near_got[m].astype(F32)).astype(BF16)
    for m in range(1, count):
        payload[m - 1][0:rows, :] = quarter[...]
        payload[m - 1][rows : 2 * rows, :] = half_2[far ^ m]


def middle_step(info, quarter_0, half_1, d_w2, near_got, got):
    count, rows, _ = half_1.shape
    outs = [(half_1.shape, BF16), ((rows, D), BF16), (half_1.shape, BF16)] + [((2 * rows, D), BF16)] * (count - 1)
    operands = [quarter_0, half_1, d_w2.reshape(2 * count, rows, D), near_got, *got]
    return step_call(middle_kernel, "middle_step", info, operands, outs)


def in_two(values):
    high = values.astype(BF16).astype(F32)
    return jnp.concatenate([high[0:4], (values - high)[0:4]], axis=0)


def third_kernel(info, quarter_1, half_2, own_total, across, gain, *refs):
    count, rows, _ = half_2.shape
    got, (whole, third, project, vectors) = refs[: count - 1], refs[count - 1 :]
    far = info[7]
    whole[0] = quarter_1[...]
    total = half_2[far].astype(F32)
    for m, g in enumerate(got):
        whole[m + 1] = g[0:rows, :]
        total += g[rows : 2 * rows, :].astype(F32)
    part = own_total[...] + across[...].astype(F32)
    project[...] = part[0 : project.shape[0]]
    vectors[...] = part[part.shape[0] - 8 :]
    o_part = part[project.shape[0] : part.shape[0] - 8]
    third[...] = jnp.concatenate([total, o_part, in_two(gain[...])], axis=0).astype(BF16)


def third_step(info, quarter_1, half_2, own_total, across, gain, got, shard_rows):
    count, rows, _ = half_2.shape
    third_rows = rows + own_total.shape[0] - shard_rows
    outs = [(half_2.shape, BF16), ((third_rows, D), BF16), ((shard_rows, D), F32), ((8, D), F32)]
    return step_call(third_kernel, "third_step", info, [quarter_1, half_2, own_total, across, gain, *got], outs)


def last_kernel(info, third, *refs):
    got, out = refs[:-1], refs[-1]
    out[0] = third[...]
    value = third[...].astype(F32)
    total = value[value.shape[0] - 8 :]
    for m, g in enumerate(got):
        out[m + 1] = g[...]
        total += g[...].astype(F32)[g.shape[0] - 8 :]
    total = jnp.broadcast_to(total[0:1] + total[4:5], (8, D))
    out[0] = jnp.concatenate([value[: value.shape[0] - 8], in_two(total)], axis=0).astype(BF16)


def last_step(info, third, got):
    outs = [((len(got) + 1,) + third.shape, BF16)]
    return step_call(last_kernel, "last_step", info, [third, *got], outs)[0]


def finish_kernel(info, w0, n0, w1, n1, w2, n2, gain, q_out, k_out, v_out, q_bias, v_bias, o_out, gain_out, whole):
    near, far = info[6], info[7]
    for h, pair in enumerate(((w0, n0), (w1, n1), (w2, n2))):
        for n, half in enumerate(pair):
            count, rows, _ = w0.shape
            for m in range(count):
                start = ((near ^ n) * count + (far ^ m)) * rows
                whole[h, pl.ds(pl.multiple_of(start, rows), rows), :] = half[m, 0:rows, :]
    for kind, out in enumerate((q_out, k_out, v_out)):
        for h in range(3):
            part = whole[h, kind * HEAD_DIM : (kind + 1) * HEAD_DIM, :].astype(F32)
            out[h * HEAD_DIM : (h + 1) * HEAD_DIM, :] = part
    bias = [whole[h, 192:208, :].astype(F32)[0:1] for h in range(3)]
    for out, first in ((q_bias, 0), (v_bias, 128)):
        out[...] = jnp.concatenate([b[:, first : first + HEAD_DIM] for b in bias], axis=1)[0]
    count, rows, _ = w0.shape
    o_rows = w2.shape[1] - rows - 8
    total = jnp.zeros((1, D), F32)
    for n, half in enumerate((w2, n2)):
        for m in range(count):
            value = half[m, rows:, :].astype(F32)
            start = ((far ^ m) * 2 + (near ^ n)) * o_rows
            o_out[pl.ds(pl.multiple_of(start, o_rows), o_rows), :] = value[0:o_rows]
            if m == 0:
                total += value[o_rows : o_rows + 1] + value[o_rows + 4 : o_rows + 5]
    gain_out[...] = (total / gain[...].astype(F32))[0]


def finish(info, halves, gain):
    count, rows, _ = halves[0].shape
    o_rows = halves[-1].shape[1] - rows - 8
    outs = [((192, D), F32)] * 3 + [((192,), F32)] * 2 + [((2 * count * o_rows, D), F32), ((D,), F32)]
    fixed = lambda *shape: pl.BlockSpec(shape, lambda i, info: (0,) * len(shape))
    return pl.pallas_call(
        finish_kernel,
        grid_spec=pltpu.PrefetchScalarGridSpec(
            num_scalar_prefetch=1,
            grid=(1,),
            in_specs=[fixed(*v.shape) for v in (*halves, gain)],
            out_specs=[fixed(*shape) for shape, _ in outs],
            scratch_shapes=[pltpu.VMEM((3, 256, D), BF16)],
        ),
        out_shape=[jax.ShapeDtypeStruct(shape, kind) for shape, kind in outs],
        name="finish",
    )(info, *halves, gain)


def first_norm_kernel(x_ref, gain_ref, out_ref):
    unit, _ = rows_normed(x_ref[...].astype(F32))
    out_ref[...] = (unit * gain_ref[...].astype(F32)).astype(BF16)


def first_norm(inputs, gain):
    return pl.pallas_call(
        first_norm_kernel,
        out_shape=jax.ShapeDtypeStruct(inputs.shape, BF16),
        name="first_norm",
    )(inputs, gain)


def input_grad_kernel(x_ref, gain_ref, middle_ref, keep_ref, near_ref, got_ref, out_ref):
    unit, scaling = rows_normed(x_ref[...].astype(F32))
    grad = keep_ref[0].astype(F32) + near_ref[0].astype(F32) + got_ref[...].astype(F32)
    out_ref[...] = middle_ref[...] + rows_back(grad * gain_ref[...].astype(F32), unit, scaling)


def input_gradient(inputs, gain, d_middle, keep, near, got):
    fixed = lambda *shape: pl.BlockSpec(shape, lambda i: (0,) * len(shape))
    tokens = inputs.shape[0]
    first = pl.BlockSpec((1, tokens, D), lambda i: (0, 0, 0))
    return pl.pallas_call(
        input_grad_kernel,
        grid=(1,),
        in_specs=[fixed(tokens, D), fixed(1, D), fixed(tokens, D), first, first, fixed(tokens, D)],
        out_specs=fixed(tokens, D),
        out_shape=jax.ShapeDtypeStruct((tokens, D), F32),
        name="input_gradient",
    )(inputs, gain, d_middle, keep, near, got)


def rows_normed(values):
    centre = jnp.mean(values, axis=1, keepdims=True)
    spread = jnp.mean(values * values, axis=1, keepdims=True) - centre * centre
    scaling = lax.rsqrt(spread + epsilon)
    return (values - centre) * scaling, scaling


def rows_back(scaled, unit, scaling):
    first = jnp.mean(scaled, axis=1, keepdims=True)
    second = jnp.mean(scaled * unit, axis=1, keepdims=True)
    return scaling * (scaled - first - unit * second)


def lanes_folded(values):
    return sum(values[:, c : c + 128] for c in range(0, values.shape[1], 128))


def token_kernel(pieces, source_count, info, *refs):
    sources = refs[:source_count]
    a_refs = refs[source_count : source_count + 4]
    packs = refs[source_count + 4 : source_count + 8]
    x_ref, cot_ref, vec_ref = refs[source_count + 8 : source_count + 11]
    out_ref, middle_grad_ref, g0, g1, g2, g3, in_keep, in_send, out_keep, out_send = refs[
        source_count + 11 : source_count + 21
    ]
    (
        w_in, w_out, staged, sides, activated, slope, d_mixed, unit_c, middle, unit2, vec_out_ref, in_sems, out_sems,
        side_sems,
    ) = refs[source_count + 21 :]
    count, block_rows = staged.shape[1:3]
    tokens = x_ref.shape[0]
    ff_slice = w_in.shape[-1]
    ff = 4 * ff_slice
    inner_rows = a_refs[0].shape[0]

    loads = {}
    for which, target in ((0, w_in), (1, w_out)):
        for r in range(4):
            loads[which, r] = [
                pltpu.make_async_copy(source, target.at[r, pl.ds(start, source.shape[0])], in_sems.at[which, r, i])
                for i, (source, start) in enumerate(pieces(info, sources, which, r))
            ]
    for which in range(2):
        for r in range(4):
            for copy in loads[which, r]:
                copy.start()

    stores = {}

    def store(which, r, value):
        staged[r] = value.astype(BF16).reshape(count, block_rows, ff_slice)
        target = ((in_keep, in_send), (out_keep, out_send))[which][r % 2]
        target = target.at[r // 2, :, pl.ds(0, block_rows)]
        stores[r] = pltpu.make_async_copy(staged.at[r], target, out_sems.at[which, r])
        stores[r].start()

    values = jnp.concatenate([a_ref[...] for a_ref in a_refs], axis=0).astype(F32)
    centre = jnp.mean(values, axis=0, keepdims=True)
    spread = jnp.mean(values * values, axis=0, keepdims=True) - centre * centre
    scaling_c = lax.rsqrt(spread + epsilon)
    unit = (values - centre) * scaling_c
    unit_c[...] = unit
    gain_c = jnp.concatenate([p[0:inner_rows, D : D + 1] for p in packs], axis=0).astype(F32)
    context = (unit * gain_c).astype(BF16)
    weight_o = jnp.concatenate([p[0:inner_rows, 0:D] for p in packs], axis=0)
    total = x_ref[...].astype(F32) + (tn(context, weight_o) + vec_ref[0:1, :])
    middle[...] = total
    unit, scaling2 = rows_normed(total)
    unit2[...] = unit
    normed2 = (unit * vec_ref[1:2, :]).astype(BF16)
    flipped = normed2.T
    cot = cot_ref[...]
    cot_flipped = cot.T
    rows_below = [p[inner_rows : inner_rows + 16, 0:ff_slice].astype(F32) for p in packs]

    fold_a = jnp.zeros((tokens, 128), F32)
    fold_b = jnp.zeros((tokens, 128), F32)
    for r in range(4):
        for copy in loads[0, r]:
            copy.wait()
        hidden = nn(normed2, w_in[r]) + rows_below[r][0:1]
        density = jnp.exp(hidden * hidden * -0.5) * (1.0 / math.sqrt(2.0 * math.pi))
        share = 0.5 * (1.0 + lax.erf(hidden * math.sqrt(0.5)))
        value = hidden * share
        activated[r] = value
        slope[r] = share + hidden * density
        fold_a += lanes_folded(value)
        fold_b += lanes_folded(value * value)
    centre = jnp.sum(fold_a, axis=1, keepdims=True) * (1.0 / ff)
    spread = jnp.sum(fold_b, axis=1, keepdims=True) * (1.0 / ff) - centre * centre
    scaling = lax.rsqrt(spread + epsilon)

    fold_a = jnp.zeros((tokens, 128), F32)
    fold_b = jnp.zeros((tokens, 128), F32)
    projected = jnp.zeros((tokens, D), F32)
    for r in range(4):
        for copy in loads[1, r]:
            copy.wait()
        gain = rows_below[r][1:2]
        unit = (activated[r] - centre) * scaling
        activated[r] = unit
        mixed = (unit * gain).astype(BF16)
        projected += nt(mixed, w_out[r])
        store(1, r, nn(cot_flipped, mixed))
        grad = nn(cot, w_out[r])
        vec_out_ref[r, 0:1, :] = jnp.sum(grad * unit, axis=0, keepdims=True)
        scaled = grad * gain
        d_mixed[r] = scaled
        fold_a += lanes_folded(scaled)
        fold_b += lanes_folded(scaled * unit)
    first = jnp.sum(fold_a, axis=1, keepdims=True) * (1.0 / ff)
    second = jnp.sum(fold_b, axis=1, keepdims=True) * (1.0 / ff)
    out_ref[...] = (middle[...] + (projected + vec_ref[2:3, :])).astype(BF16)

    d_normed2 = jnp.zeros((tokens, D), F32)
    for r in range(4):
        grad = (slope[r] * (scaling * (d_mixed[r] - first - activated[r] * second))).astype(BF16)
        vec_out_ref[r, 1:2, :] = jnp.sum(grad.astype(F32), axis=0, keepdims=True)
        stores[r].wait()
        store(0, r, nn(flipped, grad))
        d_normed2 += nt(grad, w_in[r])

    cot = cot.astype(F32)
    unit = unit2[...]
    d_middle = cot + rows_back(d_normed2 * vec_ref[1:2, :], unit, scaling2)
    middle_grad_ref[...] = d_middle
    d_branch = d_middle.astype(BF16)
    norm2_part = jnp.sum(d_normed2 * unit, axis=0, keepdims=True)
    project_bias_part = jnp.sum(cot, axis=0, keepdims=True)
    output_bias_part = jnp.sum(d_branch.astype(F32), axis=0, keepdims=True)
    d_context = nt(weight_o, d_branch)
    o_grad = nn(context, d_branch)
    unit = unit_c[...]
    inner_part = jnp.sum(d_context * unit, axis=1, keepdims=True)
    inner_part = jnp.broadcast_to(inner_part, (D, 128)).T[0:1]
    scaled = d_context * gain_c
    first = jnp.mean(scaled, axis=0, keepdims=True)
    second = jnp.mean(scaled * unit, axis=0, keepdims=True)
    grad = (scaling_c * (scaled - first - unit * second)).astype(BF16)
    for i, g_ref in enumerate((g0, g1, g2, g3)):
        rows = slice(i * inner_rows, (i + 1) * inner_rows)
        g_ref[...] = grad[rows]
        vec_out_ref[i, 2:3, 0:inner_rows] = inner_part[:, rows]
        vec_out_ref[i, 2:3, inner_rows:D] = jnp.zeros((1, D - inner_rows), F32)
        vec_out_ref[i, 3:4, :] = norm2_part
        vec_out_ref[i, 4:5, :] = project_bias_part
        vec_out_ref[i, 5:6, :] = output_bias_part
        vec_out_ref[i, 6:8, :] = jnp.zeros((2, D), F32)
    o_rows = inner_rows // count
    side_stores = []
    for i in range(4):
        vectors = vec_out_ref[i]
        for d in range(count):
            start = i * inner_rows + d * o_rows
            block = jnp.concatenate([o_grad[start : start + o_rows], vectors], axis=0)
            sides[i, d] = block.astype(BF16)
        target = (out_keep, out_send)[i % 2].at[i // 2, :, pl.ds(block_rows, o_rows + 8)]
        side_stores.append(pltpu.make_async_copy(sides.at[i], target, side_sems.at[i]))
        side_stores[i].start()
    for copy in list(stores.values()) + side_stores:
        copy.wait()


def token_section(info, attended, packs, inputs, cotangent, vectors, sources, pieces, piece_count):
    tokens = inputs.shape[0]
    inner_rows = attended[0].shape[0]
    ff_slice = sources[0].shape[-1]
    fixed = lambda *shape: pl.BlockSpec(shape, lambda s, info: (0,) * len(shape))
    anywhere = pl.BlockSpec(memory_space=pl.ANY)
    grad_piece = jax.ShapeDtypeStruct((inner_rows, tokens), BF16)
    count = 8
    block_rows, side_rows = D // count, inner_rows // count + 8
    grad_pair = lambda rows: jax.ShapeDtypeStruct((2, count, rows, ff_slice), BF16)
    return pl.pallas_call(
        functools.partial(token_kernel, pieces, len(sources)),
        grid_spec=pltpu.PrefetchScalarGridSpec(
            num_scalar_prefetch=1,
            grid=(1,),
            in_specs=[anywhere] * len(sources)
            + [fixed(*a.shape) for a in attended]
            + [fixed(*p.shape) for p in packs]
            + [fixed(tokens, D), fixed(tokens, D), fixed(8, D)],
            out_specs=[fixed(tokens, D), fixed(tokens, D)]
            + [fixed(inner_rows, tokens)] * 4
            + [anywhere] * 4,
            scratch_shapes=[
                pltpu.VMEM((4, D, ff_slice), BF16),
                pltpu.VMEM((4, D, ff_slice), BF16),
                pltpu.VMEM((4, count, block_rows, ff_slice), BF16),
                pltpu.VMEM((4, count, side_rows, ff_slice), BF16),
                pltpu.VMEM((4, tokens, ff_slice), F32),
                pltpu.VMEM((4, tokens, ff_slice), F32),
                pltpu.VMEM((4, tokens, ff_slice), F32),
                pltpu.VMEM((D, tokens), F32),
                pltpu.VMEM((tokens, D), F32),
                pltpu.VMEM((tokens, D), F32),
                pltpu.VMEM((4, 8, D), F32),
                pltpu.SemaphoreType.DMA((2, 4, piece_count)),
                pltpu.SemaphoreType.DMA((2, 4)),
                pltpu.SemaphoreType.DMA((4,)),
            ],
        ),
        out_shape=[
            jax.ShapeDtypeStruct((tokens, D), BF16),
            jax.ShapeDtypeStruct((tokens, D), F32),
            *[grad_piece] * 4,
            *[grad_pair(block_rows)] * 2,
            *[grad_pair(block_rows + side_rows)] * 2,
        ],
        compiler_params=pltpu.CompilerParams(
            dimension_semantics=("arbitrary",), vmem_limit_bytes=60 << 20
        ),
        cost_estimate=pl.CostEstimate(
            flops=20_000_000_000, bytes_accessed=30_000_000, transcendentals=4_000_000
        ),
        name="token_section",
    )(info, *sources, *attended, *packs, inputs, cotangent, vectors)


def swap(values, distance):
    count = lax.axis_size("head")
    return lax.ppermute(values, "head", [(i, i ^ distance) for i in range(count)])


def dp_swap(values, distance):
    count = lax.axis_size("dp")
    return lax.ppermute(values, "dp", [(i, i ^ distance) for i in range(count)])


def pick(values, index, axis):
    return lax.dynamic_index_in_dim(values, index, axis, keepdims=False)


def wide(values):
    return values.astype(F32)


def swap_near(values, axis):
    near = lax.axis_index("dp") & 1
    return dp_swap(pick(values, 1 - near, axis).astype(BF16), 1)


def keep_near(values, axis):
    return pick(values, lax.axis_index("dp") & 1, axis)


def keep_far(values, axis):
    return pick(values, lax.axis_index("dp") >> 1, axis)


def far_of(values, m, axis):
    return pick(values, (lax.axis_index("dp") >> 1) ^ m, axis).astype(BF16)


def far_swaps(payload):
    count = lax.axis_size("dp") // 2
    return [dp_swap(payload(m), 2 * m) for m in range(1, count)]


def after(value, *others):
    return lax.optimization_barrier((value,) + others)[0]


def in_order_of(place, far_count):
    def in_order(own, neighbour):
        total = jnp.zeros((2, far_count) + own.shape[1:], own.dtype)
        for m in range(far_count):
            for n, part in enumerate((own, neighbour)):
                total = lax.dynamic_update_slice(
                    total, part[m][None, None], ((place & 1) ^ n, (place >> 1) ^ m, 0, 0)
                )
        return total

    return in_order


def plain_steps(place, in_order):
    near, far = place & 1, place >> 1

    def half_of(d_w, got):
        return (wide(pick(d_w.reshape((2,) + got.shape), near, 0)) + wide(got)).astype(BF16)

    def bundle_of(quarter, half):
        return [jnp.concatenate([quarter, pick(half, far ^ m, 0)], axis=0) for m in range(1, half.shape[0])]

    def quarter_of(half, parts):
        return (wide(pick(half, far, 0)) + sum(wide(p) for p in parts)).astype(BF16)

    def first(info, half_0, d_w1, bundle, cross_half, own_half, cross, own):
        rows = half_0.shape[1]
        quarter = quarter_of(half_0, [g[:rows] for g in cross])
        half_1 = half_of(d_w1, bundle[:, -rows:])
        cross_total = (pick(cross_half, far, 0) + sum(wide(g[rows:]) for g in cross)).astype(BF16)
        own_total = pick(own_half, far, 0) + sum(wide(g) for g in own)
        return quarter, half_1, cross_total, own_total, *bundle_of(quarter, half_1)

    def second(info, quarter_0, half_1, d_w2, near_got, got):
        rows = half_1.shape[1]
        whole = jnp.stack([quarter_0] + [g[:rows] for g in got])
        quarter = quarter_of(half_1, [g[rows:] for g in got])
        half_2 = half_of(d_w2, near_got)
        return whole, quarter, half_2, *bundle_of(quarter, half_2)

    def third(info, quarter_1, half_2, own_total, across, gain, got, shard_rows):
        rows = half_2.shape[1]
        whole = jnp.stack([quarter_1] + [g[:rows] for g in got])
        quarter = quarter_of(half_2, [g[rows:] for g in got])
        part = own_total + wide(across)
        sent = jnp.concatenate([quarter, part[shard_rows:-8].astype(BF16), in_two(gain).astype(BF16)], axis=0)
        return whole, sent, part[:shard_rows], part[-8:]

    def last(info, third, got):
        total = sum(wide(g[-8:]) for g in got) + wide(third[-8:])
        total = jnp.broadcast_to(total[0:1] + total[4:5], (8, D))
        own = jnp.concatenate([third[:-8], in_two(total).astype(BF16)], axis=0)
        return jnp.stack([own] + list(got))

    def close(info, halves, gain):
        rows = halves[0].shape[1]
        whole = [
            wide(in_order(halves[2 * h][:, :rows], halves[2 * h + 1][:, :rows]).reshape(-1, D)) for h in range(3)
        ]
        kinds = [jnp.concatenate([w[k * 64 : k * 64 + 64] for w in whole], axis=0) for k in range(3)]
        bias = [jnp.concatenate([w[192, k : k + 64] for w in whole]) for k in (0, 128)]
        o_total = in_order(halves[4][:, rows:-8], halves[5][:, rows:-8]).transpose(1, 0, 2, 3).reshape(-1, D)
        total = sum(wide(v[0, -8:-7]) + wide(v[0, -4:-3]) for v in halves[4:])
        return *kinds, *bias, wide(o_total), (total / wide(gain))[0]

    return first, second, third, last, close


def local(
    inputs,
    cotangent,
    lengths,
    norm1_gain,
    query_weight,
    query_bias,
    key_weight,
    value_weight,
    value_bias,
    inner_gain,
    output_weight,
    output_bias,
    norm2_gain,
    hidden_weight,
    hidden_bias,
    hidden_gain,
    project_weight,
    project_bias,
):
    dp_count = lax.axis_size("dp")
    far_count = dp_count // 2
    me = lax.axis_index("head")
    heads = query_weight.shape[1] // HEAD_DIM
    shard_rows = hidden_weight.shape[0]
    slice_cols = hidden_weight.shape[1]
    inner_rows = output_weight.shape[0]

    first_length = lengths[0, 0]
    limits = [
        jnp.where(first_length > SHORT, first_length - SHORT * (me ^ r), lengths[0, me ^ r])
        for r in range(4)
    ]
    place = lax.axis_index("dp")
    info = jnp.stack([first_length] + limits + [me, place & 1, place >> 1]).astype(jnp.int32)

    first_weight, second_weight = hidden_weight, project_weight.T
    straight = shard_rows % 16 == 0

    gain1 = wide(norm1_gain)
    normed1 = first_norm(inputs, norm1_gain[None])
    near = swap(normed1, 1)
    across = swap(normed1, 2)

    if straight:
        both = jnp.concatenate([first_weight, second_weight], axis=0)
        both_far = [both] + far_swaps(lambda m: both)

    pack = jnp.concatenate(
        [
            jnp.pad(jnp.concatenate([output_weight, inner_gain[:, None]], axis=1), ((0, 0), (0, 127))),
            jnp.pad(jnp.stack([hidden_bias, hidden_gain]), ((0, 14), (0, D + 128 - slice_cols))),
        ],
        axis=0,
    )
    pack_across = swap(pack, 2)
    pack_near = swap(pack, 1)

    def per_head(weight):
        return weight.T.reshape(heads, HEAD_DIM, D)

    zero_bias = jnp.zeros_like(query_bias)
    packed_weight = jnp.concatenate(
        [per_head(query_weight), per_head(key_weight), per_head(value_weight)], axis=1
    )
    packed_bias = wide(
        jnp.concatenate(
            [b.reshape(heads, 1, HEAD_DIM) for b in (query_bias, zero_bias, value_bias)], axis=2
        )
    )
    across, info, packed_weight, packed_bias, pack = lax.optimization_barrier(
        (across, info, packed_weight, packed_bias, pack)
    )
    far = swap(across, 1)
    rows = (normed1, near, across, far)
    waits = []
    if straight:
        first_own = jnp.stack([w[:shard_rows] for w in both_far])
        second_own = jnp.stack([w[shard_rows:] for w in both_far])
        first_own, second_own = lax.optimization_barrier((first_own, second_own))
        first_near = dp_swap(first_own, 1)
        second_across = swap(second_own, 2)
        waits = [first_own, second_own]
    early = attention_forward(after(info, *waits), rows, packed_weight, packed_bias, 0, 1, [])
    waits = []
    if straight:
        pack_across, first_near, second_across, early = lax.optimization_barrier(
            (pack_across, first_near, second_across, early)
        )
        first_block = jnp.stack([first_own, first_near])
        second_block = jnp.stack([second_own, second_across])
        first_across = swap(first_block, 2)
        second_near = dp_swap(second_block, 1)
        first_sides = [first_block, swap(first_block, 1), first_across]
        second_sides = [second_block, second_near, swap(second_block, 1)]
        waits = [first_block, second_block, first_sides[1], second_sides[2]]
    pack_far = swap(pack_across, 1)
    packs = (pack, pack_near, pack_across, pack_far)
    info_now = after(info, early[0], pack_far, pack_near, *waits)
    late = attention_forward(info_now, rows, packed_weight, packed_bias, 1, heads - 1, early[:4])
    attended_heads = late[:4]

    def exchange(pieces):
        return [pieces[0]] + [swap(pieces[r], r) for r in (1, 2, 3)]

    attended = exchange(attended_heads)
    vectors = jnp.concatenate(
        [wide(jnp.stack([output_bias, norm2_gain, project_bias])), jnp.zeros((5, D), F32)], axis=0
    )
    if straight:
        first_across, second_near = (after(v, late[0]) for v in (first_across, second_near))
        first_sides.append(swap(first_across, 1))
        second_sides.append(swap(second_near, 1))
        sources = first_sides + second_sides

        def pieces(info, refs, which, r):
            found = []
            for n in range(2):
                for m in range(far_count):
                    start = ((info[7] ^ m) * 2 + (info[6] ^ n)) * shard_rows
                    if which == 0:
                        source = refs[r].at[n, m]
                    else:
                        source = refs[4 + (r % 2) * 2 + n].at[r // 2, m]
                    found.append((source, pl.multiple_of(start, shard_rows)))
            return found

        piece_count = dp_count
    else:
        shards = jnp.concatenate([first_weight, second_weight], axis=0)
        gathered = lax.all_gather(shards, ("dp", "head"), axis=0, tiled=False)
        gathered = gathered.reshape(dp_count, 4, 2, shard_rows, slice_cols)
        sources = [gathered.transpose(1, 2, 0, 3, 4).reshape(4, 2, D, slice_cols)]
        pieces = lambda info, refs, which, r: [(refs[0].at[info[5] ^ r, which], 0)]
        piece_count = 1
    output, d_middle, *rest = token_section(
        info, attended, packs, inputs, cotangent, vectors, sources, pieces, piece_count
    )
    attended_grad, (in_keep, in_send, out_keep, out_send) = rest[:4], rest[4:]

    if out_keep.shape[1] != dp_count:
        def recut(v):
            o_rows = inner_rows // v.shape[1]
            end = v.shape[2] - 8
            weight = v[:, :, : end - o_rows].reshape(2, dp_count, -1, slice_cols)
            o_part = v[:, :, end - o_rows : end].reshape(2, dp_count, -1, slice_cols)
            vec_part = jnp.broadcast_to(v[:, 0:1, end:], (2, dp_count, 8, slice_cols))
            return jnp.concatenate([weight, o_part, vec_part], axis=2)

        out_keep, out_send = recut(out_keep), recut(out_send)
    grads = exchange(attended_grad)
    out_got, in_got = swap(out_send, 1), swap(in_send, 1)
    pairs = lambda v: v.reshape(2, far_count, 2, -1, slice_cols)
    out_keep, out_got, in_keep, in_got = pairs(out_keep), pairs(out_got), pairs(in_keep), pairs(in_got)
    mine = lambda v: pick(v, place & 1, 1)
    theirs = lambda v: pick(v, 1 - (place & 1), 1)
    out_part = lambda q, take: wide(take(out_keep[q])) + wide(take(out_got[q]))

    head_rows = 256 // dp_count
    by_place = lambda v: v.reshape(2, far_count, head_rows, D)
    other_half = lambda v: pick(by_place(v), 1 - (place & 1), 0)

    def half_sum(d_w, got):
        return (wide(keep_near(by_place(d_w), 0)) + wide(got)).astype(BF16)

    def head_step(h, info):
        saved, local_head = (early[4:], 0) if h == 0 else (late[4:], h - 1)
        return attention_backward(h, info, grads, attended_heads, saved, local_head, rows)

    lane_halves = (slice(0, slice_cols // 2), slice(slice_cols // 2, slice_cols))

    def across_part(lanes):
        return (wide(in_keep[1][..., lanes]) + wide(in_got[1][..., lanes])).astype(BF16)

    across_a = across_part(lane_halves[0])
    own_sent = out_part(0, theirs).astype(BF16)
    own_sent, across_a, grads = lax.optimization_barrier((own_sent, across_a, grads))
    across_got_a = swap(across_a, 2)
    own_near = dp_swap(own_sent, 1)
    packed_0, d_weight_0 = head_step(0, after(info, own_sent, across_a))

    packed_0, d_weight_0, own_near, across_got_a, in_keep, in_got = lax.optimization_barrier(
        (packed_0, d_weight_0, own_near, across_got_a, in_keep, in_got)
    )
    across_b = across_part(lane_halves[1])
    own_half = out_part(0, mine) + wide(own_near)
    own_payload = [far_of(own_half, m, 0) for m in range(1, far_count)]
    near_sent = jnp.concatenate([out_part(1, theirs).astype(BF16), other_half(d_weight_0)], axis=1)
    near_sent, across_b, *own_payload = lax.optimization_barrier((near_sent, across_b, *own_payload))
    across_got_b = swap(across_b, 2)
    near_got = dp_swap(near_sent, 1)
    own_far = [dp_swap(p, 2 * (m + 1)) for m, p in enumerate(own_payload)]
    packed_1, d_weight_1 = head_step(1, after(info, near_sent, across_b, *own_payload))

    packed_1, d_weight_1, near_got, across_got_b, *own_far = lax.optimization_barrier(
        (packed_1, d_weight_1, near_got, across_got_b, *own_far)
    )
    half_0 = half_sum(d_weight_0, near_got[:, -head_rows:])
    cross_half = out_part(1, mine) + wide(near_got[:, :-head_rows])
    cross_payload = [
        jnp.concatenate([far_of(half_0, m, 0), far_of(cross_half, m, 0)], axis=0) for m in range(1, far_count)
    ]
    across_got = jnp.concatenate([across_got_a, across_got_b], axis=-1)
    in_sum = wide(in_keep[0]) + wide(in_got[0]) + wide(across_got)
    near_sent = jnp.concatenate([theirs(in_sum).astype(BF16), other_half(d_weight_1)], axis=1)
    near_sent, *cross_payload = lax.optimization_barrier((near_sent, *cross_payload))
    near_got = dp_swap(near_sent, 1)
    cross_far = [dp_swap(p, 2 * (m + 1)) for m, p in enumerate(cross_payload)]
    packed_2, d_weight_2 = head_step(2, after(info, near_sent, *cross_payload))

    d_weight_2, packed_2, near_got, *cross_far = lax.optimization_barrier(
        (d_weight_2, packed_2, near_got, *cross_far)
    )
    hr = head_rows
    steps = opening, middle_step, third_step, last_step, finish
    if hr % 16:
        steps = plain_steps(place, in_order_of(place, far_count))
    step_a, step_b, step_c, step_d, step_e = steps
    sent_2 = other_half(d_weight_2)
    got_2 = dp_swap(sent_2, 1)
    quarter_0, half_1, cross_total, own_total, *payload = step_a(
        after(info, sent_2), half_0, d_weight_1, near_got, cross_half, own_half, cross_far, own_far
    )
    step_1 = [dp_swap(p, 2 * (m + 1)) for m, p in enumerate(payload)]
    out_across = swap(cross_total, 2)
    dx_keep, dx_send, gain_part = input_part(
        [packed_0, packed_1, after(packed_2, cross_total, *payload)], packed_weight, [d_weight_0, d_weight_1, d_weight_2]
    )
    d_weight_2, got_2, step_1, out_across, dx_send, gain_part = lax.optimization_barrier(
        (d_weight_2, got_2, step_1, out_across, dx_send, gain_part)
    )
    near_rows = swap(dx_send, 1)
    gain_across = swap(gain_part, 2)

    whole_0, quarter_1, half_2, *payload = step_b(info, quarter_0, half_1, d_weight_2, got_2, step_1)
    whole_0, near_rows, gain_across, *payload = lax.optimization_barrier(
        (whole_0, near_rows, gain_across, *payload)
    )
    step_2 = [dp_swap(p, 2 * (m + 1)) for m, p in enumerate(payload)]
    other_0 = dp_swap(whole_0, 1)
    gain_sum = gain_part + gain_across
    cross_sum = (wide(dx_keep[1]) + wide(near_rows[1])).astype(BF16)
    gain_sum, cross_sum = lax.optimization_barrier((gain_sum, cross_sum))
    gain_sum = gain_sum + swap(gain_sum, 1)
    cross_got = swap(cross_sum, 2)

    whole_1, third, project_grad, vec_total = step_c(
        after(info, other_0, cross_sum), quarter_1, half_2, own_total, out_across, gain_sum, step_2, shard_rows
    )
    step_3 = far_swaps(lambda m: third)
    other_1 = dp_swap(whole_1, 1)
    in_half = mine(in_sum) + wide(near_got[:, :-hr])

    last_own = step_d(after(info, other_1, cross_got), third, step_3)
    last_sent, in_half = lax.optimization_barrier((last_own, in_half))
    last_near = dp_swap(last_sent, 1)
    in_far = far_swaps(lambda m: far_of(in_half, m, 0))
    hidden_grad = keep_far(in_half, 0) + sum(wide(g) for g in in_far)
    input_grad = input_gradient(inputs, norm1_gain[None], d_middle, dx_keep, near_rows, cross_got)
    query_grad, key_grad, value_grad, query_bias_grad, value_bias_grad, o_total, norm1_total = step_e(
        after(info, input_grad), [whole_0, other_0, whole_1, other_1, last_own, last_near], norm1_gain[None]
    )
    return (
        output,
        input_grad,
        norm1_total,
        query_grad.T,
        query_bias_grad,
        key_grad.T,
        value_grad.T,
        value_bias_grad,
        vec_total[2, :inner_rows],
        o_total,
        vec_total[5],
        vec_total[3],
        hidden_grad,
        vec_total[1],
        vec_total[0],
        project_grad.T,
        vec_total[4],
    )


def solution(mesh):
    rows = P(("dp", "head"), None)
    columns = P(None, "head")
    head = P("head")
    return jax.shard_map(
        local,
        mesh=mesh,
        in_specs=(
            rows, rows, P("dp", None), P(), columns, head, columns, columns, head, head,
            P("head", None), P(), P(), P("dp", "head"), head, head, P("head", "dp"), P(),
        ),
        out_specs=(
            rows, rows, P(), columns, head, columns, columns, head, head, P("head", None),
            P(), P(), P("dp", "head"), head, head, P("head", "dp"), P(),
        ),
        check_vma=False,
    )
```

```python
import functools
import math

import jax
import jax.numpy as jnp
from jax import lax
from jax.experimental import pallas as pl
from jax.experimental.pallas import tpu as pltpu
from jax.sharding import PartitionSpec as P

D = 768
HEAD_DIM = 64
FF = 3072
SHORT = 512
SLOT = 4 * SHORT

BF16 = jnp.bfloat16
F32 = jnp.float32
epsilon = 1e-05
excluded = 1e30
SCALE = HEAD_DIM ** (-0.5)
LOG2_SCALE = SCALE * math.log2(math.e)
LN2 = math.log(2.0)
QUERY_ROWS = 512
KEY_ROWS = 256
VMEM_LIMIT = 56 << 20


def nt(left, right):
    return lax.dot_general(left, right, (((1,), (1,)), ((), ())), preferred_element_type=F32)


def nn(left, right):
    return lax.dot_general(left, right, (((1,), (0,)), ((), ())), preferred_element_type=F32)


def tn(left, right):
    return lax.dot_general(left, right, (((0,), (0,)), ((), ())), preferred_element_type=F32)


def attention_forward_kernel(before, info, *refs):
    x_refs, (w_ref, b_ref), earlier = refs[0:4], refs[4:6], refs[6 : 6 + 4 * (before > 0)]
    *o_refs, lse_ref, q_ref, k_ref, v_ref = refs[6 + len(earlier) :]
    head = pl.program_id(0)
    lane = lax.broadcasted_iota(jnp.int32, (SHORT, 128), 1)
    row = lax.broadcasted_iota(jnp.int32, (SHORT, 128), 0)
    for o_ref, early in zip(o_refs, earlier):

        @pl.when(head == 0)
        def _():
            o_ref[0 : before * HEAD_DIM, :] = early[...]

    for block, x_ref in enumerate(x_refs):
        rows = pl.ds(block * SHORT, SHORT)
        packed = (nt(x_ref[...], w_ref[0]) + b_ref[0]).astype(BF16)
        inside = jnp.where(row < info[1 + block], 1.0, 0.0).astype(F32)
        q_flags = jnp.where(lane == 0, inside, jnp.where(lane == 1, 1.0 - inside, 0.0))
        k_flags = jnp.where(
            lane == 0, (inside - 1.0) * excluded, jnp.where(lane == 1, inside * -excluded, 0.0)
        )
        q, k, v = packed[:, 0:64], packed[:, 64:128], packed[:, 128:192]
        scaled = k.astype(F32) * LOG2_SCALE
        high = scaled.astype(BF16)
        low = (scaled - high.astype(F32)).astype(BF16)
        q_ref[0, rows, :] = jnp.concatenate([q, q, q_flags.astype(BF16)], axis=1)
        k_ref[0, rows, :] = jnp.concatenate([high, low, k_flags.astype(BF16)], axis=1)
        v_ref[0, rows, :] = jnp.concatenate([v, jnp.ones((SHORT, 64), BF16)], axis=1)

    out_rows = pl.ds(pl.multiple_of((before + head) * HEAD_DIM, HEAD_DIM), HEAD_DIM)

    def block_of(start, keys):
        scores = nt(q_ref[0, pl.ds(start, QUERY_ROWS), :], k_ref[0, keys, :])
        top = jnp.max(scores, axis=1, keepdims=True)
        weights = jnp.exp2(scores - top).astype(BF16)
        out = nn(weights, v_ref[0, keys, :])
        out_lane = lax.broadcasted_iota(jnp.int32, (QUERY_ROWS, 128), 1)
        out = jnp.where(out_lane == 65, jnp.broadcast_to(top, (QUERY_ROWS, 128)), out).T
        total = out[64:65]
        o_refs[start // SHORT][out_rows, pl.ds(start % SHORT, QUERY_ROWS)] = (
            out[0:64] * (1.0 / total)
        ).astype(BF16)
        lse_ref[0, :, pl.ds(start, QUERY_ROWS)] = out[65:66] + jnp.log2(total)

    longer = info[0] > SHORT

    @pl.when(longer)
    def _():
        for start in range(0, SLOT, QUERY_ROWS):
            block_of(start, pl.ds(0, SLOT))

    @pl.when(jnp.logical_not(longer))
    def _():
        for start in range(0, SLOT, QUERY_ROWS):
            block_of(start, pl.ds(start // SHORT * SHORT, SHORT))


def head_spec(*shape):
    return pl.BlockSpec((1,) + shape, lambda h, info: (h,) + (0,) * len(shape))


def whole_spec(*shape):
    return pl.BlockSpec(shape, lambda h, info: (0,) * len(shape))


def attention_forward(info, rows, weights, biases, before, count, earlier):
    out_rows = (before + count) * HEAD_DIM
    later = lambda *shape: pl.BlockSpec((1,) + shape, lambda h, info: (before + h,) + (0,) * len(shape))
    return pl.pallas_call(
        functools.partial(attention_forward_kernel, before),
        grid_spec=pltpu.PrefetchScalarGridSpec(
            num_scalar_prefetch=1,
            grid=(count,),
            in_specs=[whole_spec(SHORT, D)] * 4
            + [later(192, D), later(1, 192)]
            + [whole_spec(before * HEAD_DIM, SHORT)] * len(earlier),
            out_specs=[whole_spec(out_rows, SHORT)] * 4
            + [head_spec(1, SLOT), head_spec(SLOT, 256), head_spec(SLOT, 256), head_spec(SLOT, 128)],
        ),
        out_shape=[jax.ShapeDtypeStruct((out_rows, SHORT), BF16)] * 4
        + [
            jax.ShapeDtypeStruct((count, 1, SLOT), F32),
            jax.ShapeDtypeStruct((count, SLOT, 256), BF16),
            jax.ShapeDtypeStruct((count, SLOT, 256), BF16),
            jax.ShapeDtypeStruct((count, SLOT, 128), BF16),
        ],
        compiler_params=pltpu.CompilerParams(
            dimension_semantics=("arbitrary",), vmem_limit_bytes=VMEM_LIMIT
        ),
        cost_estimate=pl.CostEstimate(
            flops=8_000_000_000 * count, bytes_accessed=4_000_000 * count, transcendentals=4_000_000 * count
        ),
        name="attention_forward",
    )(info, *rows, weights, biases, *earlier)


def attention_backward_kernel(*refs):
    info, *pieces = refs[:9]
    lse_ref, q_ref, k_ref, v_ref = refs[9:13]
    x_refs = refs[13:17]
    rest = list(refs[17:])
    packed_ref, dw_ref, grad, dq, delta, packed, x_all, sems = rest
    copies = [
        pltpu.make_async_copy(x_ref, x_all.at[block], sems.at[block]) for block, x_ref in enumerate(x_refs)
    ]
    for copy in copies:
        copy.start()
    for block, (g_ref, o_ref) in enumerate(zip(pieces[:4], pieces[4:])):
        g = g_ref[...].astype(F32)
        cols = pl.ds(block * SHORT, SHORT)
        delta[:, cols] = jnp.sum(g * o_ref[...].astype(F32), axis=0, keepdims=True)
        grad[cols, :] = g.T.astype(BF16)

    def block_of(start, queries, first):
        rows = pl.ds(start, KEY_ROWS)
        k = k_ref[0, rows, :]
        q = q_ref[0, queries, :]
        g = grad[queries, :]
        weights = jnp.exp2(nt(k, q) - lse_ref[0, :, queries])
        d_probs = nt(v_ref[0, rows, 0:64], g)
        d_scores = (weights * (d_probs - delta[:, queries])).astype(BF16)
        packed[rows, 128:192] = nn(weights.astype(BF16), g).astype(BF16)
        packed[rows, 64:128] = (nn(d_scores, q[:, 0:128])[:, 0:64] * SCALE).astype(BF16)
        term = tn(d_scores, k[:, 0:128])
        if first:
            dq[queries, :] = term
        else:
            dq[queries, :] += term

    longer = info[0] > SHORT

    @pl.when(longer)
    def _():
        for start in range(0, SLOT, KEY_ROWS):
            block_of(start, pl.ds(0, SLOT), start == 0)

    @pl.when(jnp.logical_not(longer))
    def _():
        for start in range(0, SLOT, KEY_ROWS):
            block_of(start, pl.ds(start // SHORT * SHORT, SHORT), start % SHORT == 0)

    total = dq[...]
    packed[:, 0:64] = ((total[:, 0:64] + total[:, 64:128]) * LN2).astype(BF16)
    packed_ref[...] = packed[...]
    for copy in copies:
        copy.wait()
    d_weight = jnp.zeros((192, D), F32)
    d_bias = jnp.zeros((1, 192), F32)
    for block in range(4):
        part = packed[pl.ds(block * SHORT, SHORT), :]
        d_weight += tn(part, x_all[block])
        d_bias += jnp.sum(part.astype(F32), axis=0, keepdims=True)
    dw_ref[0:192, :] = d_weight.astype(BF16)
    d_bias = jnp.concatenate([d_bias, jnp.zeros((1, D - 192), F32)], axis=1)
    row = lax.broadcasted_iota(jnp.int32, (64, D), 0)
    dw_ref[192:256, :] = jnp.where(row == 0, d_bias, 0.0).astype(BF16)


def attention_backward(head, info, grads, attended, saved, local_head, rows):
    one = lambda *shape: pl.BlockSpec((1,) + shape, lambda i, info: (local_head,) + (0,) * len(shape))
    in_specs = (
        [pl.BlockSpec((HEAD_DIM, SHORT), lambda i, info: (head, 0))] * 8
        + [one(1, SLOT), one(SLOT, 256), one(SLOT, 256), one(SLOT, 128)]
        + [pl.BlockSpec(memory_space=pl.ANY)] * 4
    )
    operands = [*grads, *attended, *saved, *rows]
    out_specs = [whole_spec(SLOT, 192), whole_spec(256, D)]
    out_shape = [jax.ShapeDtypeStruct((SLOT, 192), BF16), jax.ShapeDtypeStruct((256, D), BF16)]
    return pl.pallas_call(
        attention_backward_kernel,
        grid_spec=pltpu.PrefetchScalarGridSpec(
            num_scalar_prefetch=1,
            grid=(1,),
            in_specs=in_specs,
            out_specs=out_specs,
            scratch_shapes=[
                pltpu.VMEM((SLOT, HEAD_DIM), BF16),
                pltpu.VMEM((SLOT, 128), F32),
                pltpu.VMEM((1, SLOT), F32),
                pltpu.VMEM((SLOT, 192), BF16),
                pltpu.VMEM((4, SHORT, D), BF16),
                pltpu.SemaphoreType.DMA((4,)),
            ],
        ),
        out_shape=out_shape,
        compiler_params=pltpu.CompilerParams(
            dimension_semantics=("arbitrary",), vmem_limit_bytes=VMEM_LIMIT
        ),
        cost_estimate=pl.CostEstimate(
            flops=15_000_000_000, bytes_accessed=8_000_000, transcendentals=4_000_000
        ),
        name="attention_backward",
    )(info, *operands)


def input_part_kernel(heads, *refs):
    packed, (w_ref,), d_weights = refs[:heads], refs[heads : heads + 1], refs[heads + 1 : 2 * heads + 1]
    dx_keep, dx_send, gain_ref = refs[2 * heads + 1 :]
    for block in (1, 3, 2, 0):
        rows = pl.ds(block * SHORT, SHORT)
        term = nn(packed[0][rows, :], w_ref[0])
        for h in range(1, heads):
            term += nn(packed[h][rows, :], w_ref[h])
        out = dx_send if block % 2 else dx_keep
        out[block // 2] = term.astype(BF16)
    gain = jnp.zeros((1, D), F32)
    for h in range(heads):
        gain += jnp.sum(d_weights[h][0:192, :].astype(F32) * w_ref[h].astype(F32), axis=0, keepdims=True)
    gain_ref[...] = jnp.broadcast_to(gain, (8, D))


def input_part(packed, weights, d_weights):
    heads = len(packed)
    return pl.pallas_call(
        functools.partial(input_part_kernel, heads),
        out_shape=[jax.ShapeDtypeStruct((2, SHORT, D), BF16)] * 2 + [jax.ShapeDtypeStruct((8, D), F32)],
        compiler_params=pltpu.CompilerParams(vmem_limit_bytes=VMEM_LIMIT),
        cost_estimate=pl.CostEstimate(flops=6_000_000_000, bytes_accessed=8_000_000, transcendentals=0),
        name="input_part",
    )(*packed, weights, *d_weights)


def step_call(kernel, name, info, operands, outs, first_blocks=()):
    def spec(i, shape):
        if i in first_blocks:
            return pl.BlockSpec((1,) + shape[1:], lambda j, info: (info[7],) + (0,) * (len(shape) - 1))
        return pl.BlockSpec(shape, lambda j, info: (0,) * len(shape))

    return pl.pallas_call(
        kernel,
        grid_spec=pltpu.PrefetchScalarGridSpec(
            num_scalar_prefetch=1,
            grid=(1,),
            in_specs=[spec(i, v.shape) for i, v in enumerate(operands)],
            out_specs=[pl.BlockSpec(shape, lambda j, info, n=len(shape): (0,) * n) for shape, _ in outs],
        ),
        out_shape=[jax.ShapeDtypeStruct(shape, kind) for shape, kind in outs],
        name=name,
    )(info, *operands)


def opening_kernel(info, half_0, d_w1, bundle, cross_half, own_half, *refs):
    count, rows, _ = half_0.shape
    cross, own, outs = refs[: count - 1], refs[count - 1 : 2 * count - 2], refs[2 * count - 2 :]
    quarter, half_1, cross_total, own_total = outs[:4]
    near, far = info[6], info[7]
    total = half_0[far].astype(F32)
    for g in cross:
        total += g[0:rows, :].astype(F32)
    quarter[...] = total.astype(BF16)
    for m in range(count):
        value = d_w1[near * count + m].astype(F32) + bundle[m, bundle.shape[1] - rows :, :].astype(F32)
        half_1[m] = value.astype(BF16)
    for m in range(1, count):
        outs[3 + m][0:rows, :] = quarter[...]
        outs[3 + m][rows : 2 * rows, :] = half_1[far ^ m]
    total = cross_half[0]
    for g in cross:
        total += g[rows:, :].astype(F32)
    cross_total[...] = total.astype(BF16)
    total = own_half[0]
    for g in own:
        total += g[...].astype(F32)
    own_total[...] = total


def opening(info, half_0, d_w1, bundle, cross_half, own_half, cross, own):
    count, rows, _ = half_0.shape
    blocks = lambda v: v.reshape(2 * count, rows, D)
    part = cross_half.shape[1]
    outs = [((rows, D), BF16), (half_0.shape, BF16), ((part, D), BF16), ((part, D), F32)]
    outs += [((2 * rows, D), BF16)] * (count - 1)
    operands = [half_0, blocks(d_w1), bundle, cross_half, own_half, *cross, *own]
    return step_call(opening_kernel, "opening", info, operands, outs, (3, 4))


def middle_kernel(info, quarter_0, half_1, d_w2, near_got, *refs):
    count, rows, _ = half_1.shape
    got, (whole, quarter, half_2, *payload) = refs[: count - 1], refs[count - 1 :]
    near, far = info[6], info[7]
    whole[0] = quarter_0[...]
    total = half_1[far].astype(F32)
    for m, g in enumerate(got):
        whole[m + 1] = g[0:rows, :]
        total += g[rows : 2 * rows, :].astype(F32)
    quarter[...] = total.astype(BF16)
    for m in range(count):
        half_2[m] = (d_w2[near * count + m].astype(F32) + near_got[m].astype(F32)).astype(BF16)
    for m in range(1, count):
        payload[m - 1][0:rows, :] = quarter[...]
        payload[m - 1][rows : 2 * rows, :] = half_2[far ^ m]


def middle_step(info, quarter_0, half_1, d_w2, near_got, got):
    count, rows, _ = half_1.shape
    outs = [(half_1.shape, BF16), ((rows, D), BF16), (half_1.shape, BF16)] + [((2 * rows, D), BF16)] * (count - 1)
    operands = [quarter_0, half_1, d_w2.reshape(2 * count, rows, D), near_got, *got]
    return step_call(middle_kernel, "middle_step", info, operands, outs)


def in_two(values):
    high = values.astype(BF16).astype(F32)
    return jnp.concatenate([high[0:4], (values - high)[0:4]], axis=0)


def third_kernel(info, quarter_1, half_2, own_total, across, *refs):
    count, rows, _ = half_2.shape
    gain = sum(ref[...] for ref in refs[:4])
    refs = refs[4:]
    got, (whole, third, project, vectors) = refs[: count - 1], refs[count - 1 :]
    far = info[7]
    whole[0] = quarter_1[...]
    total = half_2[far].astype(F32)
    for m, g in enumerate(got):
        whole[m + 1] = g[0:rows, :]
        total += g[rows : 2 * rows, :].astype(F32)
    part = own_total[...] + across[...].astype(F32)
    project[...] = part[0 : project.shape[0]]
    vectors[...] = part[part.shape[0] - 8 :]
    o_part = part[project.shape[0] : part.shape[0] - 8]
    third[...] = jnp.concatenate([total, o_part, in_two(gain)], axis=0).astype(BF16)


def third_step(info, quarter_1, half_2, own_total, across, gains, got, shard_rows):
    count, rows, _ = half_2.shape
    third_rows = rows + own_total.shape[0] - shard_rows
    outs = [(half_2.shape, BF16), ((third_rows, D), BF16), ((shard_rows, D), F32), ((8, D), F32)]
    return step_call(third_kernel, "third_step", info, [quarter_1, half_2, own_total, across, *gains, *got], outs)


def last_kernel(info, third, whole_1, *refs):
    got, out = refs[:-1], refs[-1]
    rows = third.shape[0]
    value = third[...].astype(F32)
    total = value[rows - 8 :]
    for m, g in enumerate(got):
        out[m + 1, 0:rows, :] = g[...]
        total += g[...].astype(F32)[rows - 8 :]
    total = jnp.broadcast_to(total[0:1] + total[4:5], (8, D))
    out[0, 0:rows, :] = jnp.concatenate([value[: rows - 8], in_two(total)], axis=0).astype(BF16)
    for m in range(whole_1.shape[0]):
        out[m, rows:, :] = whole_1[m]


def last_step(info, third, whole_1, got):
    rows = third.shape[0] + whole_1.shape[1]
    return step_call(last_kernel, "last_step", info, [third, whole_1, *got], [((len(got) + 1, rows, D), BF16)])[0]


def finish_kernel(info, w0, n0, w1, w2, n2, gain, q_out, k_out, v_out, q_bias, v_bias, o_out, gain_out, whole):
    near, far = info[6], info[7]
    count, rows, _ = w0.shape
    third_rows = w2.shape[1] - rows
    below = n2.at[:, pl.ds(third_rows, rows), :]
    for h, pair in enumerate(((w0, n0), (w1, below), (w2, n2))):
        for n, half in enumerate(pair):
            for m in range(count):
                start = ((near ^ n) * count + (far ^ m)) * rows
                whole[h, pl.ds(pl.multiple_of(start, rows), rows), :] = half[m, 0:rows, :]
    for kind, out in enumerate((q_out, k_out, v_out)):
        for h in range(3):
            part = whole[h, kind * HEAD_DIM : (kind + 1) * HEAD_DIM, :].astype(F32)
            out[h * HEAD_DIM : (h + 1) * HEAD_DIM, :] = part
    bias = [whole[h, 192:208, :].astype(F32)[0:1] for h in range(3)]
    for out, first in ((q_bias, 0), (v_bias, 128)):
        out[...] = jnp.concatenate([b[:, first : first + HEAD_DIM] for b in bias], axis=1)[0]
    o_rows = third_rows - rows - 8
    total = jnp.zeros((1, D), F32)
    for n, half in enumerate((w2, n2)):
        for m in range(count):
            value = half[m, rows:third_rows, :].astype(F32)
            start = ((far ^ m) * 2 + (near ^ n)) * o_rows
            o_out[pl.ds(pl.multiple_of(start, o_rows), o_rows), :] = value[0:o_rows]
            if m == 0:
                total += value[o_rows : o_rows + 1] + value[o_rows + 4 : o_rows + 5]
    gain_out[...] = total[0] / gain[...].astype(F32)


def finish(info, halves, gain):
    count, rows, _ = halves[0].shape
    o_rows = halves[-1].shape[1] - 2 * rows - 8
    outs = [((192, D), F32)] * 3 + [((192,), F32)] * 2 + [((2 * count * o_rows, D), F32), ((D,), F32)]
    fixed = lambda *shape: pl.BlockSpec(shape, lambda i, info: (0,) * len(shape))
    return pl.pallas_call(
        finish_kernel,
        grid_spec=pltpu.PrefetchScalarGridSpec(
            num_scalar_prefetch=1,
            grid=(1,),
            in_specs=[fixed(*v.shape) for v in (*halves, gain)],
            out_specs=[fixed(*shape) for shape, _ in outs],
            scratch_shapes=[pltpu.VMEM((3, 256, D), BF16)],
        ),
        out_shape=[jax.ShapeDtypeStruct(shape, kind) for shape, kind in outs],
        name="finish",
    )(info, *halves, gain)


def first_norm_kernel(x_ref, gain_ref, out_ref):
    unit, _ = rows_normed(x_ref[...].astype(F32))
    out_ref[...] = (unit * gain_ref[...].astype(F32)[None]).astype(BF16)


def first_norm(inputs, gain):
    return pl.pallas_call(
        first_norm_kernel,
        out_shape=jax.ShapeDtypeStruct(inputs.shape, BF16),
        name="first_norm",
    )(inputs, gain)


def input_grad_kernel(x_ref, gain_ref, middle_ref, keep_ref, near_ref, got_ref, out_ref):
    unit, scaling = rows_normed(x_ref[...].astype(F32))
    grad = keep_ref[0].astype(F32) + near_ref[0].astype(F32) + got_ref[...].astype(F32)
    out_ref[...] = middle_ref[...] + rows_back(grad * gain_ref[...].astype(F32)[None], unit, scaling)


def input_gradient(inputs, gain, d_middle, keep, near, got):
    fixed = lambda *shape: pl.BlockSpec(shape, lambda i: (0,) * len(shape))
    tokens = inputs.shape[0]
    first = pl.BlockSpec((1, tokens, D), lambda i: (0, 0, 0))
    return pl.pallas_call(
        input_grad_kernel,
        grid=(1,),
        in_specs=[fixed(tokens, D), fixed(D), fixed(tokens, D), first, first, fixed(tokens, D)],
        out_specs=fixed(tokens, D),
        out_shape=jax.ShapeDtypeStruct((tokens, D), F32),
        name="input_gradient",
    )(inputs, gain, d_middle, keep, near, got)


def rows_normed(values):
    centre = jnp.mean(values, axis=1, keepdims=True)
    spread = jnp.mean(values * values, axis=1, keepdims=True) - centre * centre
    scaling = lax.rsqrt(spread + epsilon)
    return (values - centre) * scaling, scaling


def rows_back(scaled, unit, scaling):
    first = jnp.mean(scaled, axis=1, keepdims=True)
    second = jnp.mean(scaled * unit, axis=1, keepdims=True)
    return scaling * (scaled - first - unit * second)


def lanes_folded(values):
    return sum(values[:, c : c + 128] for c in range(0, values.shape[1], 128))


def token_kernel(pieces, source_count, info, *refs):
    sources = refs[:source_count]
    a_refs = refs[source_count : source_count + 4]
    packs = refs[source_count + 4 : source_count + 8]
    x_ref, cot_ref, vec_ref = refs[source_count + 8 : source_count + 11]
    out_ref, middle_grad_ref, g0, g1, g2, g3, in_keep, in_send, out_keep, out_send = refs[
        source_count + 11 : source_count + 21
    ]
    (
        w_in, w_out, staged, sides, activated, slope, d_mixed, unit_c, middle, unit2, vec_out_ref, in_sems, out_sems,
        side_sems,
    ) = refs[source_count + 21 :]
    count, block_rows = staged.shape[1:3]
    tokens = x_ref.shape[0]
    ff_slice = w_in.shape[-1]
    ff = 4 * ff_slice
    inner_rows = a_refs[0].shape[0]

    loads = {}
    for which, target in ((0, w_in), (1, w_out)):
        for r in range(4):
            loads[which, r] = [
                pltpu.make_async_copy(source, target.at[r, pl.ds(start, source.shape[0])], in_sems.at[which, r, i])
                for i, (source, start) in enumerate(pieces(info, sources, which, r))
            ]
    for which in range(2):
        for r in range(4):
            for copy in loads[which, r]:
                copy.start()

    stores = {}

    def store(which, r, value):
        staged[r] = value.astype(BF16).reshape(count, block_rows, ff_slice)
        target = ((in_keep, in_send), (out_keep, out_send))[which][r % 2]
        target = target.at[r // 2, :, pl.ds(0, block_rows)]
        stores[r] = pltpu.make_async_copy(staged.at[r], target, out_sems.at[which, r])
        stores[r].start()

    values = jnp.concatenate([a_ref[...] for a_ref in a_refs], axis=0).astype(F32)
    centre = jnp.mean(values, axis=0, keepdims=True)
    spread = jnp.mean(values * values, axis=0, keepdims=True) - centre * centre
    scaling_c = lax.rsqrt(spread + epsilon)
    unit = (values - centre) * scaling_c
    unit_c[...] = unit
    gain_c = jnp.concatenate([p[0:inner_rows, D : D + 1] for p in packs], axis=0).astype(F32)
    context = (unit * gain_c).astype(BF16)
    weight_o = jnp.concatenate([p[0:inner_rows, 0:D] for p in packs], axis=0)
    total = x_ref[...].astype(F32) + (tn(context, weight_o) + vec_ref[0:1, :])
    middle[...] = total
    unit, scaling2 = rows_normed(total)
    unit2[...] = unit
    normed2 = (unit * vec_ref[1:2, :]).astype(BF16)
    flipped = normed2.T
    cot = cot_ref[...]
    cot_flipped = cot.T
    rows_below = [p[inner_rows : inner_rows + 16, 0:ff_slice].astype(F32) for p in packs]

    fold_a = jnp.zeros((tokens, 128), F32)
    fold_b = jnp.zeros((tokens, 128), F32)
    for r in range(4):
        for copy in loads[0, r]:
            copy.wait()
        hidden = nn(normed2, w_in[r]) + rows_below[r][0:1]
        density = jnp.exp(hidden * hidden * -0.5) * (1.0 / math.sqrt(2.0 * math.pi))
        share = 0.5 * (1.0 + lax.erf(hidden * math.sqrt(0.5)))
        value = hidden * share
        activated[r] = value
        slope[r] = share + hidden * density
        fold_a += lanes_folded(value)
        fold_b += lanes_folded(value * value)
    centre = jnp.sum(fold_a, axis=1, keepdims=True) * (1.0 / ff)
    spread = jnp.sum(fold_b, axis=1, keepdims=True) * (1.0 / ff) - centre * centre
    scaling = lax.rsqrt(spread + epsilon)

    fold_a = jnp.zeros((tokens, 128), F32)
    fold_b = jnp.zeros((tokens, 128), F32)
    projected = jnp.zeros((tokens, D), F32)
    for r in range(4):
        for copy in loads[1, r]:
            copy.wait()
        gain = rows_below[r][1:2]
        unit = (activated[r] - centre) * scaling
        activated[r] = unit
        mixed = (unit * gain).astype(BF16)
        projected += nt(mixed, w_out[r])
        store(1, r, nn(cot_flipped, mixed))
        grad = nn(cot, w_out[r])
        vec_out_ref[r, 0:1, :] = jnp.sum(grad * unit, axis=0, keepdims=True)
        scaled = grad * gain
        d_mixed[r] = scaled
        fold_a += lanes_folded(scaled)
        fold_b += lanes_folded(scaled * unit)
    first = jnp.sum(fold_a, axis=1, keepdims=True) * (1.0 / ff)
    second = jnp.sum(fold_b, axis=1, keepdims=True) * (1.0 / ff)
    out_ref[...] = (middle[...] + (projected + vec_ref[2:3, :])).astype(BF16)

    d_normed2 = jnp.zeros((tokens, D), F32)
    for r in range(4):
        grad = (slope[r] * (scaling * (d_mixed[r] - first - activated[r] * second))).astype(BF16)
        vec_out_ref[r, 1:2, :] = jnp.sum(grad.astype(F32), axis=0, keepdims=True)
        stores[r].wait()
        store(0, r, nn(flipped, grad))
        d_normed2 += nt(grad, w_in[r])

    cot = cot.astype(F32)
    unit = unit2[...]
    d_middle = cot + rows_back(d_normed2 * vec_ref[1:2, :], unit, scaling2)
    middle_grad_ref[...] = d_middle
    d_branch = d_middle.astype(BF16)
    norm2_part = jnp.sum(d_normed2 * unit, axis=0, keepdims=True)
    project_bias_part = jnp.sum(cot, axis=0, keepdims=True)
    output_bias_part = jnp.sum(d_branch.astype(F32), axis=0, keepdims=True)
    d_context = nt(weight_o, d_branch)
    o_grad = nn(context, d_branch)
    unit = unit_c[...]
    inner_part = jnp.sum(d_context * unit, axis=1, keepdims=True)
    inner_part = jnp.broadcast_to(inner_part, (D, 128)).T[0:1]
    scaled = d_context * gain_c
    first = jnp.mean(scaled, axis=0, keepdims=True)
    second = jnp.mean(scaled * unit, axis=0, keepdims=True)
    grad = (scaling_c * (scaled - first - unit * second)).astype(BF16)
    for i, g_ref in enumerate((g0, g1, g2, g3)):
        rows = slice(i * inner_rows, (i + 1) * inner_rows)
        g_ref[...] = grad[rows]
        vec_out_ref[i, 2:3, 0:inner_rows] = inner_part[:, rows]
        vec_out_ref[i, 2:3, inner_rows:D] = jnp.zeros((1, D - inner_rows), F32)
        vec_out_ref[i, 3:4, :] = norm2_part
        vec_out_ref[i, 4:5, :] = project_bias_part
        vec_out_ref[i, 5:6, :] = output_bias_part
        vec_out_ref[i, 6:8, :] = jnp.zeros((2, D), F32)
    o_rows = inner_rows // count
    side_stores = []
    for i in range(4):
        vectors = vec_out_ref[i]
        for d in range(count):
            start = i * inner_rows + d * o_rows
            block = jnp.concatenate([o_grad[start : start + o_rows], vectors], axis=0)
            sides[i, d] = block.astype(BF16)
        target = (out_keep, out_send)[i % 2].at[i // 2, :, pl.ds(block_rows, o_rows + 8)]
        side_stores.append(pltpu.make_async_copy(sides.at[i], target, side_sems.at[i]))
        side_stores[i].start()
    for copy in list(stores.values()) + side_stores:
        copy.wait()


def token_section(info, attended, packs, inputs, cotangent, vectors, sources, pieces, piece_count):
    tokens = inputs.shape[0]
    inner_rows = attended[0].shape[0]
    ff_slice = sources[0].shape[-1]
    fixed = lambda *shape: pl.BlockSpec(shape, lambda s, info: (0,) * len(shape))
    anywhere = pl.BlockSpec(memory_space=pl.ANY)
    grad_piece = jax.ShapeDtypeStruct((inner_rows, tokens), BF16)
    count = 8
    block_rows, side_rows = D // count, inner_rows // count + 8
    grad_pair = lambda rows: jax.ShapeDtypeStruct((2, count, rows, ff_slice), BF16)
    return pl.pallas_call(
        functools.partial(token_kernel, pieces, len(sources)),
        grid_spec=pltpu.PrefetchScalarGridSpec(
            num_scalar_prefetch=1,
            grid=(1,),
            in_specs=[anywhere] * len(sources)
            + [fixed(*a.shape) for a in attended]
            + [fixed(*p.shape) for p in packs]
            + [fixed(tokens, D), fixed(tokens, D), fixed(8, D)],
            out_specs=[fixed(tokens, D), fixed(tokens, D)]
            + [fixed(inner_rows, tokens)] * 4
            + [anywhere] * 4,
            scratch_shapes=[
                pltpu.VMEM((4, D, ff_slice), BF16),
                pltpu.VMEM((4, D, ff_slice), BF16),
                pltpu.VMEM((4, count, block_rows, ff_slice), BF16),
                pltpu.VMEM((4, count, side_rows, ff_slice), BF16),
                pltpu.VMEM((4, tokens, ff_slice), F32),
                pltpu.VMEM((4, tokens, ff_slice), F32),
                pltpu.VMEM((4, tokens, ff_slice), F32),
                pltpu.VMEM((D, tokens), F32),
                pltpu.VMEM((tokens, D), F32),
                pltpu.VMEM((tokens, D), F32),
                pltpu.VMEM((4, 8, D), F32),
                pltpu.SemaphoreType.DMA((2, 4, piece_count)),
                pltpu.SemaphoreType.DMA((2, 4)),
                pltpu.SemaphoreType.DMA((4,)),
            ],
        ),
        out_shape=[
            jax.ShapeDtypeStruct((tokens, D), BF16),
            jax.ShapeDtypeStruct((tokens, D), F32),
            *[grad_piece] * 4,
            *[grad_pair(block_rows)] * 2,
            *[grad_pair(block_rows + side_rows)] * 2,
        ],
        compiler_params=pltpu.CompilerParams(
            dimension_semantics=("arbitrary",), vmem_limit_bytes=60 << 20
        ),
        cost_estimate=pl.CostEstimate(
            flops=20_000_000_000, bytes_accessed=30_000_000, transcendentals=4_000_000
        ),
        name="token_section",
    )(info, *sources, *attended, *packs, inputs, cotangent, vectors)


def swap(values, distance):
    count = lax.axis_size("head")
    return lax.ppermute(values, "head", [(i, i ^ distance) for i in range(count)])


def dp_swap(values, distance):
    count = lax.axis_size("dp")
    return lax.ppermute(values, "dp", [(i, i ^ distance) for i in range(count)])


def pick(values, index, axis):
    return lax.dynamic_index_in_dim(values, index, axis, keepdims=False)


def wide(values):
    return values.astype(F32)


def swap_near(values, axis):
    near = lax.axis_index("dp") & 1
    return dp_swap(pick(values, 1 - near, axis).astype(BF16), 1)


def keep_near(values, axis):
    return pick(values, lax.axis_index("dp") & 1, axis)


def keep_far(values, axis):
    return pick(values, lax.axis_index("dp") >> 1, axis)


def far_of(values, m, axis):
    return pick(values, (lax.axis_index("dp") >> 1) ^ m, axis).astype(BF16)


def far_swaps(payload):
    count = lax.axis_size("dp") // 2
    return [dp_swap(payload(m), 2 * m) for m in range(1, count)]


def after(value, *others):
    return lax.optimization_barrier((value,) + others)[0]


def in_order_of(place, far_count):
    def in_order(own, neighbour):
        total = jnp.zeros((2, far_count) + own.shape[1:], own.dtype)
        for m in range(far_count):
            for n, part in enumerate((own, neighbour)):
                total = lax.dynamic_update_slice(
                    total, part[m][None, None], ((place & 1) ^ n, (place >> 1) ^ m, 0, 0)
                )
        return total

    return in_order


def plain_steps(place, in_order):
    near, far = place & 1, place >> 1

    def half_of(d_w, got):
        return (wide(pick(d_w.reshape((2,) + got.shape), near, 0)) + wide(got)).astype(BF16)

    def bundle_of(quarter, half):
        return [jnp.concatenate([quarter, pick(half, far ^ m, 0)], axis=0) for m in range(1, half.shape[0])]

    def quarter_of(half, parts):
        return (wide(pick(half, far, 0)) + sum(wide(p) for p in parts)).astype(BF16)

    def first(info, half_0, d_w1, bundle, cross_half, own_half, cross, own):
        rows = half_0.shape[1]
        quarter = quarter_of(half_0, [g[:rows] for g in cross])
        half_1 = half_of(d_w1, bundle[:, -rows:])
        cross_total = (pick(cross_half, far, 0) + sum(wide(g[rows:]) for g in cross)).astype(BF16)
        own_total = pick(own_half, far, 0) + sum(wide(g) for g in own)
        return quarter, half_1, cross_total, own_total, *bundle_of(quarter, half_1)

    def second(info, quarter_0, half_1, d_w2, near_got, got):
        rows = half_1.shape[1]
        whole = jnp.stack([quarter_0] + [g[:rows] for g in got])
        quarter = quarter_of(half_1, [g[rows:] for g in got])
        half_2 = half_of(d_w2, near_got)
        return whole, quarter, half_2, *bundle_of(quarter, half_2)

    def third(info, quarter_1, half_2, own_total, across, gains, got, shard_rows):
        gain = sum(gains)
        rows = half_2.shape[1]
        whole = jnp.stack([quarter_1] + [g[:rows] for g in got])
        quarter = quarter_of(half_2, [g[rows:] for g in got])
        part = own_total + wide(across)
        sent = jnp.concatenate([quarter, part[shard_rows:-8].astype(BF16), in_two(gain).astype(BF16)], axis=0)
        return whole, sent, part[:shard_rows], part[-8:]

    def last(info, third, whole_1, got):
        total = sum(wide(g[-8:]) for g in got) + wide(third[-8:])
        total = jnp.broadcast_to(total[0:1] + total[4:5], (8, D))
        own = jnp.concatenate([third[:-8], in_two(total).astype(BF16)], axis=0)
        return jnp.concatenate([jnp.stack([own] + list(got)), whole_1], axis=1)

    def close(info, halves, gain):
        rows = halves[0].shape[1]
        *halves, last_own, last_got = halves
        halves = [*halves, last_got[:, -rows:], last_own[:, :-rows], last_got[:, :-rows]]
        whole = [
            wide(in_order(halves[2 * h][:, :rows], halves[2 * h + 1][:, :rows]).reshape(-1, D)) for h in range(3)
        ]
        kinds = [jnp.concatenate([w[k * 64 : k * 64 + 64] for w in whole], axis=0) for k in range(3)]
        bias = [jnp.concatenate([w[192, k : k + 64] for w in whole]) for k in (0, 128)]
        o_total = in_order(halves[4][:, rows:-8], halves[5][:, rows:-8]).transpose(1, 0, 2, 3).reshape(-1, D)
        total = sum(wide(v[0, -8:-7]) + wide(v[0, -4:-3]) for v in halves[4:])
        return *kinds, *bias, wide(o_total), (total / wide(gain))[0]

    return first, second, third, last, close


def local(
    inputs,
    cotangent,
    lengths,
    norm1_gain,
    query_weight,
    query_bias,
    key_weight,
    value_weight,
    value_bias,
    inner_gain,
    output_weight,
    output_bias,
    norm2_gain,
    hidden_weight,
    hidden_bias,
    hidden_gain,
    project_weight,
    project_bias,
):
    dp_count = lax.axis_size("dp")
    far_count = dp_count // 2
    me = lax.axis_index("head")
    heads = query_weight.shape[1] // HEAD_DIM
    shard_rows = hidden_weight.shape[0]
    slice_cols = hidden_weight.shape[1]
    inner_rows = output_weight.shape[0]

    first_length = lengths[0, 0]
    limits = [
        jnp.where(first_length > SHORT, first_length - SHORT * (me ^ r), lengths[0, me ^ r])
        for r in range(4)
    ]
    place = lax.axis_index("dp")
    info = jnp.stack([first_length] + limits + [me, place & 1, place >> 1]).astype(jnp.int32)

    first_weight, second_weight = hidden_weight, project_weight.T
    straight = shard_rows % 16 == 0

    pack = jnp.concatenate(
        [
            jnp.pad(jnp.concatenate([output_weight, inner_gain[:, None]], axis=1), ((0, 0), (0, 127))),
            jnp.pad(jnp.stack([hidden_bias, hidden_gain]), ((0, 14), (0, D + 128 - slice_cols))),
        ],
        axis=0,
    )
    normed1 = first_norm(inputs, norm1_gain)
    near = swap(normed1, 1)
    across = swap(normed1, 2)

    if straight:
        both = jnp.concatenate([first_weight, second_weight], axis=0)
        both_far = [both] + far_swaps(lambda m: both)

    pack_across = swap(pack, 2)
    pack_near = swap(pack, 1)

    def per_head(weight):
        return weight.T.reshape(heads, HEAD_DIM, D)

    zero_bias = jnp.zeros_like(query_bias)
    packed_weight = jnp.concatenate(
        [per_head(query_weight), per_head(key_weight), per_head(value_weight)], axis=1
    )
    packed_bias = wide(
        jnp.concatenate(
            [b.reshape(heads, 1, HEAD_DIM) for b in (query_bias, zero_bias, value_bias)], axis=2
        )
    )
    across, info, packed_weight, packed_bias, pack = lax.optimization_barrier(
        (across, info, packed_weight, packed_bias, pack)
    )
    far = swap(across, 1)
    rows = (normed1, near, across, far)
    waits = []
    if straight:
        first_own = jnp.stack([w[:shard_rows] for w in both_far])
        second_own = jnp.stack([w[shard_rows:] for w in both_far])
        first_own, second_own = lax.optimization_barrier((first_own, second_own))
        first_near = dp_swap(first_own, 1)
        second_across = swap(second_own, 2)
        waits = [first_own, second_own]
    early = attention_forward(after(info, *waits), rows, packed_weight, packed_bias, 0, 1, [])
    waits = []
    if straight:
        pack_across, first_near, second_across, early = lax.optimization_barrier(
            (pack_across, first_near, second_across, early)
        )
        first_block = jnp.stack([first_own, first_near])
        second_block = jnp.stack([second_own, second_across])
        first_across = swap(first_block, 2)
        second_near = dp_swap(second_block, 1)
        first_sides = [first_block, swap(first_block, 1), first_across]
        second_sides = [second_block, second_near, swap(second_block, 1)]
        waits = [first_block, second_block, first_sides[1], second_sides[2]]
    pack_far = swap(pack_across, 1)
    packs = (pack, pack_near, pack_across, pack_far)
    info_now = after(info, early[0], pack_far, pack_near, *waits)
    late = attention_forward(info_now, rows, packed_weight, packed_bias, 1, heads - 1, early[:4])
    attended_heads = late[:4]

    def exchange(pieces):
        return [pieces[0]] + [swap(pieces[r], r) for r in (1, 2, 3)]

    attended = exchange(attended_heads)
    vectors = jnp.concatenate(
        [wide(jnp.stack([output_bias, norm2_gain, project_bias])), jnp.zeros((5, D), F32)], axis=0
    )
    if straight:
        first_across, second_near = (after(v, late[0]) for v in (first_across, second_near))
        first_sides.append(swap(first_across, 1))
        second_sides.append(swap(second_near, 1))
        sources = first_sides + second_sides

        def pieces(info, refs, which, r):
            found = []
            for n in range(2):
                for m in range(far_count):
                    start = ((info[7] ^ m) * 2 + (info[6] ^ n)) * shard_rows
                    if which == 0:
                        source = refs[r].at[n, m]
                    else:
                        source = refs[4 + (r % 2) * 2 + n].at[r // 2, m]
                    found.append((source, pl.multiple_of(start, shard_rows)))
            return found

        piece_count = dp_count
    else:
        shards = jnp.concatenate([first_weight, second_weight], axis=0)
        gathered = lax.all_gather(shards, ("dp", "head"), axis=0, tiled=False)
        gathered = gathered.reshape(dp_count, 4, 2, shard_rows, slice_cols)
        sources = [gathered.transpose(1, 2, 0, 3, 4).reshape(4, 2, D, slice_cols)]
        pieces = lambda info, refs, which, r: [(refs[0].at[info[5] ^ r, which], 0)]
        piece_count = 1
    output, d_middle, *rest = token_section(
        info, attended, packs, inputs, cotangent, vectors, sources, pieces, piece_count
    )
    attended_grad, (in_keep, in_send, out_keep, out_send) = rest[:4], rest[4:]

    if out_keep.shape[1] != dp_count:
        def recut(v):
            o_rows = inner_rows // v.shape[1]
            end = v.shape[2] - 8
            weight = v[:, :, : end - o_rows].reshape(2, dp_count, -1, slice_cols)
            o_part = v[:, :, end - o_rows : end].reshape(2, dp_count, -1, slice_cols)
            vec_part = jnp.broadcast_to(v[:, 0:1, end:], (2, dp_count, 8, slice_cols))
            return jnp.concatenate([weight, o_part, vec_part], axis=2)

        out_keep, out_send = recut(out_keep), recut(out_send)
    grads = exchange(attended_grad)
    out_got, in_got = swap(out_send, 1), swap(in_send, 1)
    pairs = lambda v: v.reshape(2, far_count, 2, -1, slice_cols)
    out_keep, out_got, in_keep, in_got = pairs(out_keep), pairs(out_got), pairs(in_keep), pairs(in_got)
    mine = lambda v: pick(v, place & 1, 1)
    theirs = lambda v: pick(v, 1 - (place & 1), 1)
    out_part = lambda q, take: wide(take(out_keep[q])) + wide(take(out_got[q]))

    head_rows = 256 // dp_count
    by_place = lambda v: v.reshape(2, far_count, head_rows, D)
    other_half = lambda v: pick(by_place(v), 1 - (place & 1), 0)

    def half_sum(d_w, got):
        return (wide(keep_near(by_place(d_w), 0)) + wide(got)).astype(BF16)

    def head_step(h, info):
        saved, local_head = (early[4:], 0) if h == 0 else (late[4:], h - 1)
        return attention_backward(h, info, grads, attended_heads, saved, local_head, rows)

    lane_halves = (slice(0, slice_cols // 2), slice(slice_cols // 2, slice_cols))

    def across_part(lanes):
        return (wide(in_keep[1][..., lanes]) + wide(in_got[1][..., lanes])).astype(BF16)

    across_a = across_part(lane_halves[0])
    own_sent = out_part(0, theirs).astype(BF16)
    own_sent, across_a, grads = lax.optimization_barrier((own_sent, across_a, grads))
    across_got_a = swap(across_a, 2)
    own_near = dp_swap(own_sent, 1)
    packed_0, d_weight_0 = head_step(0, after(info, own_sent, across_a))

    packed_0, d_weight_0, own_near, across_got_a, in_keep, in_got = lax.optimization_barrier(
        (packed_0, d_weight_0, own_near, across_got_a, in_keep, in_got)
    )
    across_b = across_part(lane_halves[1])
    own_half = out_part(0, mine) + wide(own_near)
    own_payload = [far_of(own_half, m, 0) for m in range(1, far_count)]
    near_sent = jnp.concatenate([out_part(1, theirs).astype(BF16), other_half(d_weight_0)], axis=1)
    near_sent, across_b, *own_payload = lax.optimization_barrier((near_sent, across_b, *own_payload))
    across_got_b = swap(across_b, 2)
    near_got = dp_swap(near_sent, 1)
    own_far = [dp_swap(p, 2 * (m + 1)) for m, p in enumerate(own_payload)]
    packed_1, d_weight_1 = head_step(1, after(info, near_sent, across_b, *own_payload))

    packed_1, d_weight_1, near_got, across_got_b, *own_far = lax.optimization_barrier(
        (packed_1, d_weight_1, near_got, across_got_b, *own_far)
    )
    half_0 = half_sum(d_weight_0, near_got[:, -head_rows:])
    cross_half = out_part(1, mine) + wide(near_got[:, :-head_rows])
    cross_payload = [
        jnp.concatenate([far_of(half_0, m, 0), far_of(cross_half, m, 0)], axis=0) for m in range(1, far_count)
    ]
    across_got = jnp.concatenate([across_got_a, across_got_b], axis=-1)
    in_sum = wide(in_keep[0]) + wide(in_got[0]) + wide(across_got)
    near_sent = jnp.concatenate([theirs(in_sum).astype(BF16), other_half(d_weight_1)], axis=1)
    near_sent, *cross_payload = lax.optimization_barrier((near_sent, *cross_payload))
    near_got = dp_swap(near_sent, 1)
    cross_far = [dp_swap(p, 2 * (m + 1)) for m, p in enumerate(cross_payload)]
    packed_2, d_weight_2 = head_step(2, after(info, near_sent, *cross_payload))

    d_weight_2, packed_2, near_got, *cross_far = lax.optimization_barrier(
        (d_weight_2, packed_2, near_got, *cross_far)
    )
    hr = head_rows
    steps = opening, middle_step, third_step, last_step, finish
    if hr % 16:
        steps = plain_steps(place, in_order_of(place, far_count))
    step_a, step_b, step_c, step_d, step_e = steps
    sent_2 = other_half(d_weight_2)
    got_2 = dp_swap(sent_2, 1)
    quarter_0, half_1, cross_total, own_total, *payload = step_a(
        after(info, sent_2), half_0, d_weight_1, near_got, cross_half, own_half, cross_far, own_far
    )
    step_1 = [dp_swap(p, 2 * (m + 1)) for m, p in enumerate(payload)]
    out_across = swap(cross_total, 2)
    dx_keep, dx_send, gain_part = input_part(
        [packed_0, packed_1, after(packed_2, cross_total, *payload)], packed_weight, [d_weight_0, d_weight_1, d_weight_2]
    )
    d_weight_2, got_2, step_1, out_across, dx_send, gain_part = lax.optimization_barrier(
        (d_weight_2, got_2, step_1, out_across, dx_send, gain_part)
    )
    near_rows = swap(dx_send, 1)
    gains = [gain_part] + [swap(gain_part, r) for r in (1, 2, 3)]

    whole_0, quarter_1, half_2, *payload = step_b(info, quarter_0, half_1, d_weight_2, got_2, step_1)
    whole_0, near_rows, *payload = lax.optimization_barrier((whole_0, near_rows, *payload))
    step_2 = [dp_swap(p, 2 * (m + 1)) for m, p in enumerate(payload)]
    other_0 = dp_swap(whole_0, 1)
    cross_sum = (wide(dx_keep[1]) + wide(after(near_rows[1], *step_2))).astype(BF16)
    cross_got = swap(cross_sum, 2)

    whole_1, third, project_grad, vec_total = step_c(
        after(info, cross_sum), quarter_1, half_2, own_total, out_across, gains, step_2, shard_rows
    )
    step_3 = far_swaps(lambda m: third)
    in_half = mine(in_sum) + wide(near_got[:, :-hr])

    last_own = step_d(after(info, other_0), third, whole_1, step_3)
    last_sent, in_half = lax.optimization_barrier((last_own, in_half))
    last_near = dp_swap(last_sent, 1)
    in_far = far_swaps(lambda m: far_of(in_half, m, 0))
    input_grad = input_gradient(inputs, norm1_gain, d_middle, dx_keep, near_rows, cross_got)
    query_grad, key_grad, value_grad, query_bias_grad, value_bias_grad, o_total, norm1_total = step_e(
        after(info, input_grad), [whole_0, other_0, whole_1, last_own, last_near], norm1_gain
    )
    *in_far, norm1_total = lax.optimization_barrier((*in_far, norm1_total))
    hidden_grad = keep_far(in_half, 0) + sum(wide(g) for g in in_far)
    return (
        output,
        input_grad,
        norm1_total,
        query_grad.T,
        query_bias_grad,
        key_grad.T,
        value_grad.T,
        value_bias_grad,
        vec_total[2, :inner_rows],
        o_total,
        vec_total[5],
        vec_total[3],
        hidden_grad,
        vec_total[1],
        vec_total[0],
        project_grad.T,
        vec_total[4],
    )


def solution(mesh):
    rows = P(("dp", "head"), None)
    columns = P(None, "head")
    head = P("head")
    return jax.shard_map(
        local,
        mesh=mesh,
        in_specs=(
            rows, rows, P("dp", None), P(), columns, head, columns, columns, head, head,
            P("head", None), P(), P(), P("dp", "head"), head, head, P("head", "dp"), P(),
        ),
        out_specs=(
            rows, rows, P(), columns, head, columns, columns, head, head, P("head", None),
            P(), P(), P("dp", "head"), head, head, P("head", "dp"), P(),
        ),
        check_vma=False,
    )
```

```python
import functools
import math

import jax
import jax.numpy as jnp
from jax import lax
from jax.experimental import pallas as pl
from jax.experimental.pallas import tpu as pltpu
from jax.sharding import PartitionSpec as P

D = 768
HEAD_DIM = 64
FF = 3072
SHORT = 512
SLOT = 4 * SHORT

BF16 = jnp.bfloat16
F32 = jnp.float32
epsilon = 1e-05
excluded = 1e30
SCALE = HEAD_DIM ** (-0.5)
LOG2_SCALE = SCALE * math.log2(math.e)
LN2 = math.log(2.0)
QUERY_ROWS = 512
KEY_ROWS = 512
VMEM_LIMIT = 56 << 20


def nt(left, right):
    return lax.dot_general(left, right, (((1,), (1,)), ((), ())), preferred_element_type=F32)


def nn(left, right):
    return lax.dot_general(left, right, (((1,), (0,)), ((), ())), preferred_element_type=F32)


def tn(left, right):
    return lax.dot_general(left, right, (((0,), (0,)), ((), ())), preferred_element_type=F32)


def attention_forward_kernel(before, info, *refs):
    x_refs, (w_ref, b_ref), earlier = refs[0:4], refs[4:6], refs[6 : 6 + 4 * (before > 0)]
    *o_refs, lse_ref, q_ref, k_ref, v_ref = refs[6 + len(earlier) :]
    head = pl.program_id(0)
    lane = lax.broadcasted_iota(jnp.int32, (SHORT, 128), 1)
    row = lax.broadcasted_iota(jnp.int32, (SHORT, 128), 0)
    for o_ref, early in zip(o_refs, earlier):

        @pl.when(head == 0)
        def _():
            o_ref[0 : before * HEAD_DIM, :] = early[...]

    for block, x_ref in enumerate(x_refs):
        rows = pl.ds(block * SHORT, SHORT)
        packed = (nt(x_ref[...], w_ref[0]) + b_ref[0]).astype(BF16)
        inside = jnp.where(row < info[1 + block], 1.0, 0.0).astype(F32)
        q_flags = jnp.where(lane == 0, inside, jnp.where(lane == 1, 1.0 - inside, 0.0))
        k_flags = jnp.where(
            lane == 0, (inside - 1.0) * excluded, jnp.where(lane == 1, inside * -excluded, 0.0)
        )
        q, k, v = packed[:, 0:64], packed[:, 64:128], packed[:, 128:192]
        scaled = k.astype(F32) * LOG2_SCALE
        high = scaled.astype(BF16)
        low = (scaled - high.astype(F32)).astype(BF16)
        q_ref[0, rows, :] = jnp.concatenate([q, q, q_flags.astype(BF16)], axis=1)
        k_ref[0, rows, :] = jnp.concatenate([high, low, k_flags.astype(BF16)], axis=1)
        v_ref[0, rows, :] = jnp.concatenate([v, jnp.ones((SHORT, 64), BF16)], axis=1)

    out_rows = pl.ds(pl.multiple_of((before + head) * HEAD_DIM, HEAD_DIM), HEAD_DIM)

    def block_of(start, keys):
        scores = nt(q_ref[0, pl.ds(start, QUERY_ROWS), :], k_ref[0, keys, :])
        top = jnp.max(scores, axis=1, keepdims=True)
        weights = jnp.exp2(scores - top).astype(BF16)
        out = nn(weights, v_ref[0, keys, :])
        out_lane = lax.broadcasted_iota(jnp.int32, (QUERY_ROWS, 128), 1)
        out = jnp.where(out_lane == 65, jnp.broadcast_to(top, (QUERY_ROWS, 128)), out).T
        total = out[64:65]
        o_refs[start // SHORT][out_rows, pl.ds(start % SHORT, QUERY_ROWS)] = (
            out[0:64] * (1.0 / total)
        ).astype(BF16)
        lse_ref[0, :, pl.ds(start, QUERY_ROWS)] = out[65:66] + jnp.log2(total)

    longer = info[0] > SHORT

    @pl.when(longer)
    def _():
        for start in range(0, SLOT, QUERY_ROWS):
            block_of(start, pl.ds(0, SLOT))

    @pl.when(jnp.logical_not(longer))
    def _():
        for start in range(0, SLOT, QUERY_ROWS):
            block_of(start, pl.ds(start // SHORT * SHORT, SHORT))


def head_spec(*shape):
    return pl.BlockSpec((1,) + shape, lambda h, info: (h,) + (0,) * len(shape))


def whole_spec(*shape):
    return pl.BlockSpec(shape, lambda h, info: (0,) * len(shape))


def attention_forward(info, rows, weights, biases, before, count, earlier):
    out_rows = (before + count) * HEAD_DIM
    later = lambda *shape: pl.BlockSpec((1,) + shape, lambda h, info: (before + h,) + (0,) * len(shape))
    return pl.pallas_call(
        functools.partial(attention_forward_kernel, before),
        grid_spec=pltpu.PrefetchScalarGridSpec(
            num_scalar_prefetch=1,
            grid=(count,),
            in_specs=[whole_spec(SHORT, D)] * 4
            + [later(192, D), later(1, 192)]
            + [whole_spec(before * HEAD_DIM, SHORT)] * len(earlier),
            out_specs=[whole_spec(out_rows, SHORT)] * 4
            + [head_spec(1, SLOT), head_spec(SLOT, 256), head_spec(SLOT, 256), head_spec(SLOT, 128)],
        ),
        out_shape=[jax.ShapeDtypeStruct((out_rows, SHORT), BF16)] * 4
        + [
            jax.ShapeDtypeStruct((count, 1, SLOT), F32),
            jax.ShapeDtypeStruct((count, SLOT, 256), BF16),
            jax.ShapeDtypeStruct((count, SLOT, 256), BF16),
            jax.ShapeDtypeStruct((count, SLOT, 128), BF16),
        ],
        compiler_params=pltpu.CompilerParams(
            dimension_semantics=("arbitrary",), vmem_limit_bytes=VMEM_LIMIT
        ),
        cost_estimate=pl.CostEstimate(
            flops=8_000_000_000 * count, bytes_accessed=4_000_000 * count, transcendentals=4_000_000 * count
        ),
        name="attention_forward",
    )(info, *rows, weights, biases, *earlier)


def attention_backward_kernel(*refs):
    info, *pieces = refs[:9]
    lse_ref, q_ref, k_ref, v_ref = refs[9:13]
    x_refs = refs[13:17]
    rest = list(refs[17:])
    packed_ref, dw_ref, grad, dq, delta, packed, x_all, sems = rest
    copies = [
        pltpu.make_async_copy(x_ref, x_all.at[block], sems.at[block]) for block, x_ref in enumerate(x_refs)
    ]
    for copy in copies:
        copy.start()
    for block, (g_ref, o_ref) in enumerate(zip(pieces[:4], pieces[4:])):
        g = g_ref[...].astype(F32)
        cols = pl.ds(block * SHORT, SHORT)
        delta[:, cols] = jnp.sum(g * o_ref[...].astype(F32), axis=0, keepdims=True)
        grad[cols, :] = g.T.astype(BF16)

    def block_of(start, queries, first):
        rows = pl.ds(start, KEY_ROWS)
        k = k_ref[0, rows, :]
        q = q_ref[0, queries, :]
        g = grad[queries, :]
        weights = jnp.exp2(nt(k, q) - lse_ref[0, :, queries])
        d_probs = nt(v_ref[0, rows, 0:64], g)
        d_scores = (weights * (d_probs - delta[:, queries])).astype(BF16)
        packed[rows, 128:192] = nn(weights.astype(BF16), g).astype(BF16)
        packed[rows, 64:128] = (nn(d_scores, q[:, 0:128])[:, 0:64] * SCALE).astype(BF16)
        term = tn(k[:, 0:128], d_scores)
        if first:
            dq[:, queries] = term
        else:
            dq[:, queries] += term

    longer = info[0] > SHORT

    @pl.when(longer)
    def _():
        for start in range(0, SLOT, KEY_ROWS):
            block_of(start, pl.ds(0, SLOT), start == 0)

    @pl.when(jnp.logical_not(longer))
    def _():
        for start in range(0, SLOT, KEY_ROWS):
            block_of(start, pl.ds(start // SHORT * SHORT, SHORT), start % SHORT == 0)

    total = dq[...].T
    packed[:, 0:64] = ((total[:, 0:64] + total[:, 64:128]) * LN2).astype(BF16)
    packed_ref[...] = packed[...]
    for copy in copies:
        copy.wait()
    d_weight = jnp.zeros((192, D), F32)
    d_bias = jnp.zeros((1, 192), F32)
    for block in range(4):
        part = packed[pl.ds(block * SHORT, SHORT), :]
        d_weight += tn(part, x_all[block])
        d_bias += jnp.sum(part.astype(F32), axis=0, keepdims=True)
    dw_ref[0:192, :] = d_weight.astype(BF16)
    d_bias = jnp.concatenate([d_bias, jnp.zeros((1, D - 192), F32)], axis=1)
    row = lax.broadcasted_iota(jnp.int32, (64, D), 0)
    dw_ref[192:256, :] = jnp.where(row == 0, d_bias, 0.0).astype(BF16)


def attention_backward(head, info, grads, attended, saved, local_head, rows):
    one = lambda *shape: pl.BlockSpec((1,) + shape, lambda i, info: (local_head,) + (0,) * len(shape))
    in_specs = (
        [pl.BlockSpec((HEAD_DIM, SHORT), lambda i, info: (head, 0))] * 8
        + [one(1, SLOT), one(SLOT, 256), one(SLOT, 256), one(SLOT, 128)]
        + [pl.BlockSpec(memory_space=pl.ANY)] * 4
    )
    operands = [*grads, *attended, *saved, *rows]
    out_specs = [whole_spec(SLOT, 192), whole_spec(256, D)]
    out_shape = [jax.ShapeDtypeStruct((SLOT, 192), BF16), jax.ShapeDtypeStruct((256, D), BF16)]
    return pl.pallas_call(
        attention_backward_kernel,
        grid_spec=pltpu.PrefetchScalarGridSpec(
            num_scalar_prefetch=1,
            grid=(1,),
            in_specs=in_specs,
            out_specs=out_specs,
            scratch_shapes=[
                pltpu.VMEM((SLOT, HEAD_DIM), BF16),
                pltpu.VMEM((128, SLOT), F32),
                pltpu.VMEM((1, SLOT), F32),
                pltpu.VMEM((SLOT, 192), BF16),
                pltpu.VMEM((4, SHORT, D), BF16),
                pltpu.SemaphoreType.DMA((4,)),
            ],
        ),
        out_shape=out_shape,
        compiler_params=pltpu.CompilerParams(
            dimension_semantics=("arbitrary",), vmem_limit_bytes=VMEM_LIMIT
        ),
        cost_estimate=pl.CostEstimate(
            flops=15_000_000_000, bytes_accessed=8_000_000, transcendentals=4_000_000
        ),
        name="attention_backward",
    )(info, *operands)


def input_part_kernel(heads, *refs):
    packed, (w_ref,), d_weights = refs[:heads], refs[heads : heads + 1], refs[heads + 1 : 2 * heads + 1]
    dx_keep, dx_send, gain_ref = refs[2 * heads + 1 :]
    for block in (1, 3, 2, 0):
        rows = pl.ds(block * SHORT, SHORT)
        term = nn(packed[0][rows, :], w_ref[0])
        for h in range(1, heads):
            term += nn(packed[h][rows, :], w_ref[h])
        out = dx_send if block % 2 else dx_keep
        out[block // 2] = term.astype(BF16)
    gain = jnp.zeros((1, D), F32)
    for h in range(heads):
        gain += jnp.sum(d_weights[h][0:192, :].astype(F32) * w_ref[h].astype(F32), axis=0, keepdims=True)
    gain_ref[...] = jnp.broadcast_to(gain, (8, D))


def input_part(packed, weights, d_weights):
    heads = len(packed)
    return pl.pallas_call(
        functools.partial(input_part_kernel, heads),
        out_shape=[jax.ShapeDtypeStruct((2, SHORT, D), BF16)] * 2 + [jax.ShapeDtypeStruct((8, D), F32)],
        compiler_params=pltpu.CompilerParams(vmem_limit_bytes=VMEM_LIMIT),
        cost_estimate=pl.CostEstimate(flops=6_000_000_000, bytes_accessed=8_000_000, transcendentals=0),
        name="input_part",
    )(*packed, weights, *d_weights)


def step_call(kernel, name, info, operands, outs, first_blocks=()):
    def spec(i, shape):
        if i in first_blocks:
            return pl.BlockSpec((1,) + shape[1:], lambda j, info: (info[7],) + (0,) * (len(shape) - 1))
        return pl.BlockSpec(shape, lambda j, info: (0,) * len(shape))

    return pl.pallas_call(
        kernel,
        grid_spec=pltpu.PrefetchScalarGridSpec(
            num_scalar_prefetch=1,
            grid=(1,),
            in_specs=[spec(i, v.shape) for i, v in enumerate(operands)],
            out_specs=[pl.BlockSpec(shape, lambda j, info, n=len(shape): (0,) * n) for shape, _ in outs],
        ),
        out_shape=[jax.ShapeDtypeStruct(shape, kind) for shape, kind in outs],
        name=name,
    )(info, *operands)


def opening_kernel(info, half_0, d_w1, bundle, cross_half, own_half, *refs):
    count, rows, _ = half_0.shape
    cross, own, outs = refs[: count - 1], refs[count - 1 : 2 * count - 2], refs[2 * count - 2 :]
    quarter, half_1, cross_total, own_total = outs[:4]
    near, far = info[6], info[7]
    total = half_0[far].astype(F32)
    for g in cross:
        total += g[0:rows, :].astype(F32)
    quarter[...] = total.astype(BF16)
    for m in range(count):
        value = d_w1[near * count + m].astype(F32) + bundle[m, bundle.shape[1] - rows :, :].astype(F32)
        half_1[m] = value.astype(BF16)
    for m in range(1, count):
        outs[3 + m][0:rows, :] = quarter[...]
        outs[3 + m][rows : 2 * rows, :] = half_1[far ^ m]
    total = cross_half[0]
    for g in cross:
        total += g[rows:, :].astype(F32)
    cross_total[...] = total.astype(BF16)
    total = own_half[0]
    for g in own:
        total += g[...].astype(F32)
    own_total[...] = total


def opening(info, half_0, d_w1, bundle, cross_half, own_half, cross, own):
    count, rows, _ = half_0.shape
    blocks = lambda v: v.reshape(2 * count, rows, D)
    part = cross_half.shape[1]
    outs = [((rows, D), BF16), (half_0.shape, BF16), ((part, D), BF16), ((part, D), F32)]
    outs += [((2 * rows, D), BF16)] * (count - 1)
    operands = [half_0, blocks(d_w1), bundle, cross_half, own_half, *cross, *own]
    return step_call(opening_kernel, "opening", info, operands, outs, (3, 4))


def middle_kernel(info, quarter_0, half_1, d_w2, near_got, *refs):
    count, rows, _ = half_1.shape
    got, (whole, quarter, half_2, *payload) = refs[: count - 1], refs[count - 1 :]
    near, far = info[6], info[7]
    whole[0] = quarter_0[...]
    total = half_1[far].astype(F32)
    for m, g in enumerate(got):
        whole[m + 1] = g[0:rows, :]
        total += g[rows : 2 * rows, :].astype(F32)
    quarter[...] = total.astype(BF16)
    for m in range(count):
        half_2[m] = (d_w2[near * count + m].astype(F32) + near_got[m].astype(F32)).astype(BF16)
    for m in range(1, count):
        payload[m - 1][0:rows, :] = quarter[...]
        payload[m - 1][rows : 2 * rows, :] = half_2[far ^ m]


def middle_step(info, quarter_0, half_1, d_w2, near_got, got):
    count, rows, _ = half_1.shape
    outs = [(half_1.shape, BF16), ((rows, D), BF16), (half_1.shape, BF16)] + [((2 * rows, D), BF16)] * (count - 1)
    operands = [quarter_0, half_1, d_w2.reshape(2 * count, rows, D), near_got, *got]
    return step_call(middle_kernel, "middle_step", info, operands, outs)


def in_two(values):
    high = values.astype(BF16).astype(F32)
    return jnp.concatenate([high[0:4], (values - high)[0:4]], axis=0)


def third_kernel(info, quarter_1, half_2, own_total, across, *refs):
    count, rows, _ = half_2.shape
    gain = sum(ref[...] for ref in refs[:4])
    refs = refs[4:]
    got, (whole, third, project, vectors) = refs[: count - 1], refs[count - 1 :]
    far = info[7]
    whole[0] = quarter_1[...]
    total = half_2[far].astype(F32)
    for m, g in enumerate(got):
        whole[m + 1] = g[0:rows, :]
        total += g[rows : 2 * rows, :].astype(F32)
    part = own_total[...] + across[...].astype(F32)
    project[...] = part[0 : project.shape[0]]
    vectors[...] = part[part.shape[0] - 8 :]
    o_part = part[project.shape[0] : part.shape[0] - 8]
    third[...] = jnp.concatenate([total, o_part, in_two(gain)], axis=0).astype(BF16)


def third_step(info, quarter_1, half_2, own_total, across, gains, got, shard_rows):
    count, rows, _ = half_2.shape
    third_rows = rows + own_total.shape[0] - shard_rows
    outs = [(half_2.shape, BF16), ((third_rows, D), BF16), ((shard_rows, D), F32), ((8, D), F32)]
    return step_call(third_kernel, "third_step", info, [quarter_1, half_2, own_total, across, *gains, *got], outs)


def last_kernel(info, third, whole_1, *refs):
    got, out = refs[:-1], refs[-1]
    rows = third.shape[0]
    value = third[...].astype(F32)
    total = value[rows - 8 :]
    for m, g in enumerate(got):
        out[m + 1, 0:rows, :] = g[...]
        total += g[...].astype(F32)[rows - 8 :]
    total = jnp.broadcast_to(total[0:1] + total[4:5], (8, D))
    out[0, 0:rows, :] = jnp.concatenate([value[: rows - 8], in_two(total)], axis=0).astype(BF16)
    for m in range(whole_1.shape[0]):
        out[m, rows:, :] = whole_1[m]


def last_step(info, third, whole_1, got):
    rows = third.shape[0] + whole_1.shape[1]
    return step_call(last_kernel, "last_step", info, [third, whole_1, *got], [((len(got) + 1, rows, D), BF16)])[0]


def finish_kernel(info, w0, n0, w1, w2, n2, gain, q_out, k_out, v_out, q_bias, v_bias, o_out, gain_out, whole):
    near, far = info[6], info[7]
    count, rows, _ = w0.shape
    third_rows = w2.shape[1] - rows
    below = n2.at[:, pl.ds(third_rows, rows), :]
    for h, pair in enumerate(((w0, n0), (w1, below), (w2, n2))):
        for n, half in enumerate(pair):
            for m in range(count):
                start = ((near ^ n) * count + (far ^ m)) * rows
                whole[h, pl.ds(pl.multiple_of(start, rows), rows), :] = half[m, 0:rows, :]
    for kind, out in enumerate((q_out, k_out, v_out)):
        for h in range(3):
            part = whole[h, kind * HEAD_DIM : (kind + 1) * HEAD_DIM, :].astype(F32)
            out[h * HEAD_DIM : (h + 1) * HEAD_DIM, :] = part
    bias = [whole[h, 192:208, :].astype(F32)[0:1] for h in range(3)]
    for out, first in ((q_bias, 0), (v_bias, 128)):
        out[...] = jnp.concatenate([b[:, first : first + HEAD_DIM] for b in bias], axis=1)[0]
    o_rows = third_rows - rows - 8
    total = jnp.zeros((1, D), F32)
    for n, half in enumerate((w2, n2)):
        for m in range(count):
            value = half[m, rows:third_rows, :].astype(F32)
            start = ((far ^ m) * 2 + (near ^ n)) * o_rows
            o_out[pl.ds(pl.multiple_of(start, o_rows), o_rows), :] = value[0:o_rows]
            if m == 0:
                total += value[o_rows : o_rows + 1] + value[o_rows + 4 : o_rows + 5]
    gain_out[...] = total[0] / gain[...].astype(F32)


def finish(info, halves, gain):
    count, rows, _ = halves[0].shape
    o_rows = halves[-1].shape[1] - 2 * rows - 8
    outs = [((192, D), F32)] * 3 + [((192,), F32)] * 2 + [((2 * count * o_rows, D), F32), ((D,), F32)]
    fixed = lambda *shape: pl.BlockSpec(shape, lambda i, info: (0,) * len(shape))
    return pl.pallas_call(
        finish_kernel,
        grid_spec=pltpu.PrefetchScalarGridSpec(
            num_scalar_prefetch=1,
            grid=(1,),
            in_specs=[fixed(*v.shape) for v in (*halves, gain)],
            out_specs=[fixed(*shape) for shape, _ in outs],
            scratch_shapes=[pltpu.VMEM((3, 256, D), BF16)],
        ),
        out_shape=[jax.ShapeDtypeStruct(shape, kind) for shape, kind in outs],
        name="finish",
    )(info, *halves, gain)


def first_norm_kernel(x_ref, gain_ref, out_ref):
    unit, _ = rows_normed(x_ref[...].astype(F32))
    out_ref[...] = (unit * gain_ref[...].astype(F32)[None]).astype(BF16)


def first_norm(inputs, gain):
    return pl.pallas_call(
        first_norm_kernel,
        out_shape=jax.ShapeDtypeStruct(inputs.shape, BF16),
        name="first_norm",
    )(inputs, gain)


def input_grad_kernel(x_ref, gain_ref, middle_ref, keep_ref, near_ref, got_ref, out_ref):
    unit, scaling = rows_normed(x_ref[...].astype(F32))
    grad = keep_ref[0].astype(F32) + near_ref[0].astype(F32) + got_ref[...].astype(F32)
    out_ref[...] = middle_ref[...] + rows_back(grad * gain_ref[...].astype(F32)[None], unit, scaling)


def input_gradient(inputs, gain, d_middle, keep, near, got):
    fixed = lambda *shape: pl.BlockSpec(shape, lambda i: (0,) * len(shape))
    tokens = inputs.shape[0]
    first = pl.BlockSpec((1, tokens, D), lambda i: (0, 0, 0))
    return pl.pallas_call(
        input_grad_kernel,
        grid=(1,),
        in_specs=[fixed(tokens, D), fixed(D), fixed(tokens, D), first, first, fixed(tokens, D)],
        out_specs=fixed(tokens, D),
        out_shape=jax.ShapeDtypeStruct((tokens, D), F32),
        name="input_gradient",
    )(inputs, gain, d_middle, keep, near, got)


def rows_normed(values):
    centre = jnp.mean(values, axis=1, keepdims=True)
    spread = jnp.mean(values * values, axis=1, keepdims=True) - centre * centre
    scaling = lax.rsqrt(spread + epsilon)
    return (values - centre) * scaling, scaling


def rows_back(scaled, unit, scaling):
    first = jnp.mean(scaled, axis=1, keepdims=True)
    second = jnp.mean(scaled * unit, axis=1, keepdims=True)
    return scaling * (scaled - first - unit * second)


def lanes_folded(values):
    return sum(values[:, c : c + 128] for c in range(0, values.shape[1], 128))


def token_kernel(pieces, source_count, info, *refs):
    sources = refs[:source_count]
    a_refs = refs[source_count : source_count + 4]
    packs = refs[source_count + 4 : source_count + 8]
    x_ref, cot_ref, vec_ref = refs[source_count + 8 : source_count + 11]
    out_ref, middle_grad_ref, g0, g1, g2, g3, in_keep, in_send, out_keep, out_send = refs[
        source_count + 11 : source_count + 21
    ]
    (
        w_in, w_out, staged, sides, activated, slope, d_mixed, unit_c, middle, unit2, vec_out_ref, in_sems, out_sems,
        side_sems,
    ) = refs[source_count + 21 :]
    count, block_rows = staged.shape[1:3]
    tokens = x_ref.shape[0]
    ff_slice = w_in.shape[-1]
    ff = 4 * ff_slice
    inner_rows = a_refs[0].shape[0]

    loads = {}
    for which, target in ((0, w_in), (1, w_out)):
        for r in range(4):
            loads[which, r] = [
                pltpu.make_async_copy(source, target.at[r, pl.ds(start, source.shape[0])], in_sems.at[which, r, i])
                for i, (source, start) in enumerate(pieces(info, sources, which, r))
            ]
    for which in range(2):
        for r in range(4):
            for copy in loads[which, r]:
                copy.start()

    stores = {}

    def store(which, r, value):
        staged[r] = value.astype(BF16).reshape(count, block_rows, ff_slice)
        target = ((in_keep, in_send), (out_keep, out_send))[which][r % 2]
        target = target.at[r // 2, :, pl.ds(0, block_rows)]
        stores[r] = pltpu.make_async_copy(staged.at[r], target, out_sems.at[which, r])
        stores[r].start()

    values = jnp.concatenate([a_ref[...] for a_ref in a_refs], axis=0).astype(F32)
    centre = jnp.mean(values, axis=0, keepdims=True)
    spread = jnp.mean(values * values, axis=0, keepdims=True) - centre * centre
    scaling_c = lax.rsqrt(spread + epsilon)
    unit = (values - centre) * scaling_c
    unit_c[...] = unit
    rows_below = [p[inner_rows : inner_rows + 16, 0:ff_slice].astype(F32) for p in packs]
    gain_rows = [jnp.broadcast_to(p[2:3, 0:inner_rows], (128, inner_rows)).T[:, 0:1] for p in rows_below]
    gain_c = jnp.concatenate(gain_rows, axis=0)
    context = (unit * gain_c).astype(BF16)
    weight_o = jnp.concatenate([p[0:inner_rows, 0:D] for p in packs], axis=0)
    total = x_ref[...].astype(F32) + (tn(context, weight_o) + vec_ref[0:1, :])
    middle[...] = total
    unit, scaling2 = rows_normed(total)
    unit2[...] = unit
    normed2 = (unit * vec_ref[1:2, :]).astype(BF16)
    flipped = normed2.T
    cot = cot_ref[...]
    cot_flipped = cot.T

    fold_a = jnp.zeros((tokens, 128), F32)
    fold_b = jnp.zeros((tokens, 128), F32)
    for r in range(4):
        for copy in loads[0, r]:
            copy.wait()
        hidden = nn(normed2, w_in[r]) + rows_below[r][0:1]
        density = jnp.exp(hidden * hidden * -0.5) * (1.0 / math.sqrt(2.0 * math.pi))
        share = 0.5 * (1.0 + lax.erf(hidden * math.sqrt(0.5)))
        value = hidden * share
        activated[r] = value
        slope[r] = share + hidden * density
        fold_a += lanes_folded(value)
        fold_b += lanes_folded(value * value)
    centre = jnp.sum(fold_a, axis=1, keepdims=True) * (1.0 / ff)
    spread = jnp.sum(fold_b, axis=1, keepdims=True) * (1.0 / ff) - centre * centre
    scaling = lax.rsqrt(spread + epsilon)

    fold_a = jnp.zeros((tokens, 128), F32)
    fold_b = jnp.zeros((tokens, 128), F32)
    projected = jnp.zeros((tokens, D), F32)
    for r in range(4):
        for copy in loads[1, r]:
            copy.wait()
        gain = rows_below[r][1:2]
        unit = (activated[r] - centre) * scaling
        activated[r] = unit
        mixed = (unit * gain).astype(BF16)
        projected += nt(mixed, w_out[r])
        store(1, r, nn(cot_flipped, mixed))
        grad = nn(cot, w_out[r])
        vec_out_ref[r, 0:1, :] = jnp.sum(grad * unit, axis=0, keepdims=True)
        scaled = grad * gain
        d_mixed[r] = scaled
        fold_a += lanes_folded(scaled)
        fold_b += lanes_folded(scaled * unit)
    first = jnp.sum(fold_a, axis=1, keepdims=True) * (1.0 / ff)
    second = jnp.sum(fold_b, axis=1, keepdims=True) * (1.0 / ff)
    out_ref[...] = (middle[...] + (projected + vec_ref[2:3, :])).astype(BF16)

    d_normed2 = jnp.zeros((tokens, D), F32)
    for r in range(4):
        grad = (slope[r] * (scaling * (d_mixed[r] - first - activated[r] * second))).astype(BF16)
        vec_out_ref[r, 1:2, :] = jnp.sum(grad.astype(F32), axis=0, keepdims=True)
        stores[r].wait()
        store(0, r, nn(flipped, grad))
        d_normed2 += nt(grad, w_in[r])

    cot = cot.astype(F32)
    unit = unit2[...]
    d_middle = cot + rows_back(d_normed2 * vec_ref[1:2, :], unit, scaling2)
    middle_grad_ref[...] = d_middle
    d_branch = d_middle.astype(BF16)
    norm2_part = jnp.sum(d_normed2 * unit, axis=0, keepdims=True)
    project_bias_part = jnp.sum(cot, axis=0, keepdims=True)
    output_bias_part = jnp.sum(d_branch.astype(F32), axis=0, keepdims=True)
    d_context = nt(weight_o, d_branch)
    o_grad = nn(context, d_branch)
    unit = unit_c[...]
    inner_part = jnp.sum(d_context * unit, axis=1, keepdims=True)
    inner_part = jnp.broadcast_to(inner_part, (D, 128)).T[0:1]
    scaled = d_context * gain_c
    first = jnp.mean(scaled, axis=0, keepdims=True)
    second = jnp.mean(scaled * unit, axis=0, keepdims=True)
    grad = (scaling_c * (scaled - first - unit * second)).astype(BF16)
    for i, g_ref in enumerate((g0, g1, g2, g3)):
        rows = slice(i * inner_rows, (i + 1) * inner_rows)
        g_ref[...] = grad[rows]
        vec_out_ref[i, 2:3, 0:inner_rows] = inner_part[:, rows]
        vec_out_ref[i, 2:3, inner_rows:D] = jnp.zeros((1, D - inner_rows), F32)
        vec_out_ref[i, 3:4, :] = norm2_part
        vec_out_ref[i, 4:5, :] = project_bias_part
        vec_out_ref[i, 5:6, :] = output_bias_part
        vec_out_ref[i, 6:8, :] = jnp.zeros((2, D), F32)
    o_rows = inner_rows // count
    side_stores = []
    for i in range(4):
        vectors = vec_out_ref[i]
        for d in range(count):
            start = i * inner_rows + d * o_rows
            block = jnp.concatenate([o_grad[start : start + o_rows], vectors], axis=0)
            sides[i, d] = block.astype(BF16)
        target = (out_keep, out_send)[i % 2].at[i // 2, :, pl.ds(block_rows, o_rows + 8)]
        side_stores.append(pltpu.make_async_copy(sides.at[i], target, side_sems.at[i]))
        side_stores[i].start()
    for copy in list(stores.values()) + side_stores:
        copy.wait()


def token_section(info, attended, packs, inputs, cotangent, vectors, sources, pieces, piece_count):
    tokens = inputs.shape[0]
    inner_rows = attended[0].shape[0]
    ff_slice = sources[0].shape[-1]
    fixed = lambda *shape: pl.BlockSpec(shape, lambda s, info: (0,) * len(shape))
    anywhere = pl.BlockSpec(memory_space=pl.ANY)
    grad_piece = jax.ShapeDtypeStruct((inner_rows, tokens), BF16)
    count = 8
    block_rows, side_rows = D // count, inner_rows // count + 8
    grad_pair = lambda rows: jax.ShapeDtypeStruct((2, count, rows, ff_slice), BF16)
    return pl.pallas_call(
        functools.partial(token_kernel, pieces, len(sources)),
        grid_spec=pltpu.PrefetchScalarGridSpec(
            num_scalar_prefetch=1,
            grid=(1,),
            in_specs=[anywhere] * len(sources)
            + [fixed(*a.shape) for a in attended]
            + [fixed(*p.shape) for p in packs]
            + [fixed(tokens, D), fixed(tokens, D), fixed(8, D)],
            out_specs=[fixed(tokens, D), fixed(tokens, D)]
            + [fixed(inner_rows, tokens)] * 4
            + [anywhere] * 4,
            scratch_shapes=[
                pltpu.VMEM((4, D, ff_slice), BF16),
                pltpu.VMEM((4, D, ff_slice), BF16),
                pltpu.VMEM((4, count, block_rows, ff_slice), BF16),
                pltpu.VMEM((4, count, side_rows, ff_slice), BF16),
                pltpu.VMEM((4, tokens, ff_slice), F32),
                pltpu.VMEM((4, tokens, ff_slice), F32),
                pltpu.VMEM((4, tokens, ff_slice), F32),
                pltpu.VMEM((D, tokens), F32),
                pltpu.VMEM((tokens, D), F32),
                pltpu.VMEM((tokens, D), F32),
                pltpu.VMEM((4, 8, D), F32),
                pltpu.SemaphoreType.DMA((2, 4, piece_count)),
                pltpu.SemaphoreType.DMA((2, 4)),
                pltpu.SemaphoreType.DMA((4,)),
            ],
        ),
        out_shape=[
            jax.ShapeDtypeStruct((tokens, D), BF16),
            jax.ShapeDtypeStruct((tokens, D), F32),
            *[grad_piece] * 4,
            *[grad_pair(block_rows)] * 2,
            *[grad_pair(block_rows + side_rows)] * 2,
        ],
        compiler_params=pltpu.CompilerParams(
            dimension_semantics=("arbitrary",), vmem_limit_bytes=60 << 20
        ),
        cost_estimate=pl.CostEstimate(
            flops=20_000_000_000, bytes_accessed=30_000_000, transcendentals=4_000_000
        ),
        name="token_section",
    )(info, *sources, *attended, *packs, inputs, cotangent, vectors)


def swap(values, distance):
    count = lax.axis_size("head")
    return lax.ppermute(values, "head", [(i, i ^ distance) for i in range(count)])


def dp_swap(values, distance):
    count = lax.axis_size("dp")
    return lax.ppermute(values, "dp", [(i, i ^ distance) for i in range(count)])


def pick(values, index, axis):
    return lax.dynamic_index_in_dim(values, index, axis, keepdims=False)


def wide(values):
    return values.astype(F32)


def swap_near(values, axis):
    near = lax.axis_index("dp") & 1
    return dp_swap(pick(values, 1 - near, axis).astype(BF16), 1)


def keep_near(values, axis):
    return pick(values, lax.axis_index("dp") & 1, axis)


def keep_far(values, axis):
    return pick(values, lax.axis_index("dp") >> 1, axis)


def far_of(values, m, axis):
    return pick(values, (lax.axis_index("dp") >> 1) ^ m, axis).astype(BF16)


def far_swaps(payload):
    count = lax.axis_size("dp") // 2
    return [dp_swap(payload(m), 2 * m) for m in range(1, count)]


def after(value, *others):
    return lax.optimization_barrier((value,) + others)[0]


def in_order_of(place, far_count):
    def in_order(own, neighbour):
        total = jnp.zeros((2, far_count) + own.shape[1:], own.dtype)
        for m in range(far_count):
            for n, part in enumerate((own, neighbour)):
                total = lax.dynamic_update_slice(
                    total, part[m][None, None], ((place & 1) ^ n, (place >> 1) ^ m, 0, 0)
                )
        return total

    return in_order


def plain_steps(place, in_order):
    near, far = place & 1, place >> 1

    def half_of(d_w, got):
        return (wide(pick(d_w.reshape((2,) + got.shape), near, 0)) + wide(got)).astype(BF16)

    def bundle_of(quarter, half):
        return [jnp.concatenate([quarter, pick(half, far ^ m, 0)], axis=0) for m in range(1, half.shape[0])]

    def quarter_of(half, parts):
        return (wide(pick(half, far, 0)) + sum(wide(p) for p in parts)).astype(BF16)

    def first(info, half_0, d_w1, bundle, cross_half, own_half, cross, own):
        rows = half_0.shape[1]
        quarter = quarter_of(half_0, [g[:rows] for g in cross])
        half_1 = half_of(d_w1, bundle[:, -rows:])
        cross_total = (pick(cross_half, far, 0) + sum(wide(g[rows:]) for g in cross)).astype(BF16)
        own_total = pick(own_half, far, 0) + sum(wide(g) for g in own)
        return quarter, half_1, cross_total, own_total, *bundle_of(quarter, half_1)

    def second(info, quarter_0, half_1, d_w2, near_got, got):
        rows = half_1.shape[1]
        whole = jnp.stack([quarter_0] + [g[:rows] for g in got])
        quarter = quarter_of(half_1, [g[rows:] for g in got])
        half_2 = half_of(d_w2, near_got)
        return whole, quarter, half_2, *bundle_of(quarter, half_2)

    def third(info, quarter_1, half_2, own_total, across, gains, got, shard_rows):
        gain = sum(gains)
        rows = half_2.shape[1]
        whole = jnp.stack([quarter_1] + [g[:rows] for g in got])
        quarter = quarter_of(half_2, [g[rows:] for g in got])
        part = own_total + wide(across)
        sent = jnp.concatenate([quarter, part[shard_rows:-8].astype(BF16), in_two(gain).astype(BF16)], axis=0)
        return whole, sent, part[:shard_rows], part[-8:]

    def last(info, third, whole_1, got):
        total = sum(wide(g[-8:]) for g in got) + wide(third[-8:])
        total = jnp.broadcast_to(total[0:1] + total[4:5], (8, D))
        own = jnp.concatenate([third[:-8], in_two(total).astype(BF16)], axis=0)
        return jnp.concatenate([jnp.stack([own] + list(got)), whole_1], axis=1)

    def close(info, halves, gain):
        rows = halves[0].shape[1]
        *halves, last_own, last_got = halves
        halves = [*halves, last_got[:, -rows:], last_own[:, :-rows], last_got[:, :-rows]]
        whole = [
            wide(in_order(halves[2 * h][:, :rows], halves[2 * h + 1][:, :rows]).reshape(-1, D)) for h in range(3)
        ]
        kinds = [jnp.concatenate([w[k * 64 : k * 64 + 64] for w in whole], axis=0) for k in range(3)]
        bias = [jnp.concatenate([w[192, k : k + 64] for w in whole]) for k in (0, 128)]
        o_total = in_order(halves[4][:, rows:-8], halves[5][:, rows:-8]).transpose(1, 0, 2, 3).reshape(-1, D)
        total = sum(wide(v[0, -8:-7]) + wide(v[0, -4:-3]) for v in halves[4:])
        return *kinds, *bias, wide(o_total), (total / wide(gain))[0]

    return first, second, third, last, close


def local(
    inputs,
    cotangent,
    lengths,
    norm1_gain,
    query_weight,
    query_bias,
    key_weight,
    value_weight,
    value_bias,
    inner_gain,
    output_weight,
    output_bias,
    norm2_gain,
    hidden_weight,
    hidden_bias,
    hidden_gain,
    project_weight,
    project_bias,
):
    dp_count = lax.axis_size("dp")
    far_count = dp_count // 2
    me = lax.axis_index("head")
    heads = query_weight.shape[1] // HEAD_DIM
    shard_rows = hidden_weight.shape[0]
    slice_cols = hidden_weight.shape[1]
    inner_rows = output_weight.shape[0]

    first_length = lengths[0, 0]
    limits = [
        jnp.where(first_length > SHORT, first_length - SHORT * (me ^ r), lengths[0, me ^ r])
        for r in range(4)
    ]
    place = lax.axis_index("dp")
    info = jnp.stack([first_length] + limits + [me, place & 1, place >> 1]).astype(jnp.int32)

    first_weight, second_weight = hidden_weight, project_weight.T
    straight = shard_rows % 16 == 0

    below = jnp.zeros((16, D), BF16)
    below = below.at[0, :slice_cols].set(hidden_bias).at[1, :slice_cols].set(hidden_gain)
    pack = jnp.concatenate([output_weight, below.at[2, :inner_rows].set(inner_gain)], axis=0)
    normed1 = first_norm(inputs, norm1_gain)
    near = swap(normed1, 1)
    across = swap(normed1, 2)

    if straight:
        both = jnp.concatenate([first_weight, second_weight], axis=0)
        both_far = [both] + far_swaps(lambda m: both)

    pack_across = swap(pack, 2)
    pack_near = swap(pack, 1)

    def per_head(weight):
        return weight.T.reshape(heads, HEAD_DIM, D)

    zero_bias = jnp.zeros_like(query_bias)
    packed_weight = jnp.concatenate(
        [per_head(query_weight), per_head(key_weight), per_head(value_weight)], axis=1
    )
    packed_bias = wide(
        jnp.concatenate(
            [b.reshape(heads, 1, HEAD_DIM) for b in (query_bias, zero_bias, value_bias)], axis=2
        )
    )
    across, info, packed_weight, packed_bias, pack = lax.optimization_barrier(
        (across, info, packed_weight, packed_bias, pack)
    )
    far = swap(across, 1)
    rows = (normed1, near, across, far)
    waits = []
    if straight:
        first_own = jnp.stack([w[:shard_rows] for w in both_far])
        second_own = jnp.stack([w[shard_rows:] for w in both_far])
        first_own, second_own = lax.optimization_barrier((first_own, second_own))
        first_near = dp_swap(first_own, 1)
        second_across = swap(second_own, 2)
        waits = [first_own, second_own]
    early = attention_forward(after(info, *waits), rows, packed_weight, packed_bias, 0, 1, [])
    waits = []
    if straight:
        pack_across, first_near, second_across, early = lax.optimization_barrier(
            (pack_across, first_near, second_across, early)
        )
        first_block = jnp.stack([first_own, first_near])
        second_block = jnp.stack([second_own, second_across])
        first_across = swap(first_block, 2)
        second_near = dp_swap(second_block, 1)
        first_sides = [first_block, swap(first_block, 1), first_across]
        second_sides = [second_block, second_near, swap(second_block, 1)]
        waits = [first_block, second_block, first_sides[1], second_sides[2]]
    pack_far = swap(pack_across, 1)
    packs = (pack, pack_near, pack_across, pack_far)
    info_now = after(info, early[0], pack_far, pack_near, *waits)
    late = attention_forward(info_now, rows, packed_weight, packed_bias, 1, heads - 1, early[:4])
    attended_heads = late[:4]

    def exchange(pieces):
        return [pieces[0]] + [swap(pieces[r], r) for r in (1, 2, 3)]

    attended = exchange(attended_heads)
    vectors = jnp.concatenate(
        [wide(jnp.stack([output_bias, norm2_gain, project_bias])), jnp.zeros((5, D), F32)], axis=0
    )
    if straight:
        first_across, second_near = (after(v, late[0]) for v in (first_across, second_near))
        first_sides.append(swap(first_across, 1))
        second_sides.append(swap(second_near, 1))
        sources = first_sides + second_sides

        def pieces(info, refs, which, r):
            found = []
            for n in range(2):
                for m in range(far_count):
                    start = ((info[7] ^ m) * 2 + (info[6] ^ n)) * shard_rows
                    if which == 0:
                        source = refs[r].at[n, m]
                    else:
                        source = refs[4 + (r % 2) * 2 + n].at[r // 2, m]
                    found.append((source, pl.multiple_of(start, shard_rows)))
            return found

        piece_count = dp_count
    else:
        shards = jnp.concatenate([first_weight, second_weight], axis=0)
        gathered = lax.all_gather(shards, ("dp", "head"), axis=0, tiled=False)
        gathered = gathered.reshape(dp_count, 4, 2, shard_rows, slice_cols)
        sources = [gathered.transpose(1, 2, 0, 3, 4).reshape(4, 2, D, slice_cols)]
        pieces = lambda info, refs, which, r: [(refs[0].at[info[5] ^ r, which], 0)]
        piece_count = 1
    output, d_middle, *rest = token_section(
        info, attended, packs, inputs, cotangent, vectors, sources, pieces, piece_count
    )
    attended_grad, (in_keep, in_send, out_keep, out_send) = rest[:4], rest[4:]

    if out_keep.shape[1] != dp_count:
        def recut(v):
            o_rows = inner_rows // v.shape[1]
            end = v.shape[2] - 8
            weight = v[:, :, : end - o_rows].reshape(2, dp_count, -1, slice_cols)
            o_part = v[:, :, end - o_rows : end].reshape(2, dp_count, -1, slice_cols)
            vec_part = jnp.broadcast_to(v[:, 0:1, end:], (2, dp_count, 8, slice_cols))
            return jnp.concatenate([weight, o_part, vec_part], axis=2)

        out_keep, out_send = recut(out_keep), recut(out_send)
    grads = exchange(attended_grad)
    out_got, in_got = swap(out_send, 1), swap(in_send, 1)
    pairs = lambda v: v.reshape(2, far_count, 2, -1, slice_cols)
    out_keep, out_got, in_keep, in_got = pairs(out_keep), pairs(out_got), pairs(in_keep), pairs(in_got)
    mine = lambda v: pick(v, place & 1, 1)
    theirs = lambda v: pick(v, 1 - (place & 1), 1)
    out_part = lambda q, take: wide(take(out_keep[q])) + wide(take(out_got[q]))

    head_rows = 256 // dp_count
    by_place = lambda v: v.reshape(2, far_count, head_rows, D)
    other_half = lambda v: pick(by_place(v), 1 - (place & 1), 0)

    def half_sum(d_w, got):
        return (wide(keep_near(by_place(d_w), 0)) + wide(got)).astype(BF16)

    def head_step(h, info):
        saved, local_head = (early[4:], 0) if h == 0 else (late[4:], h - 1)
        return attention_backward(h, info, grads, attended_heads, saved, local_head, rows)

    lane_halves = (slice(0, slice_cols // 2), slice(slice_cols // 2, slice_cols))

    def across_part(lanes):
        return (wide(in_keep[1][..., lanes]) + wide(in_got[1][..., lanes])).astype(BF16)

    across_a = across_part(lane_halves[0])
    own_sent = out_part(0, theirs).astype(BF16)
    own_sent, across_a, grads = lax.optimization_barrier((own_sent, across_a, grads))
    across_got_a = swap(across_a, 2)
    own_near = dp_swap(own_sent, 1)
    packed_0, d_weight_0 = head_step(0, after(info, own_sent, across_a))

    packed_0, d_weight_0, own_near, across_got_a, in_keep, in_got = lax.optimization_barrier(
        (packed_0, d_weight_0, own_near, across_got_a, in_keep, in_got)
    )
    across_b = across_part(lane_halves[1])
    own_half = out_part(0, mine) + wide(own_near)
    own_payload = [far_of(own_half, m, 0) for m in range(1, far_count)]
    near_sent = jnp.concatenate([out_part(1, theirs).astype(BF16), other_half(d_weight_0)], axis=1)
    near_sent, across_b, *own_payload = lax.optimization_barrier((near_sent, across_b, *own_payload))
    across_got_b = swap(across_b, 2)
    near_got = dp_swap(near_sent, 1)
    own_far = [dp_swap(p, 2 * (m + 1)) for m, p in enumerate(own_payload)]
    packed_1, d_weight_1 = head_step(1, after(info, near_sent, across_b, *own_payload))

    packed_1, d_weight_1, near_got, across_got_b, *own_far = lax.optimization_barrier(
        (packed_1, d_weight_1, near_got, across_got_b, *own_far)
    )
    half_0 = half_sum(d_weight_0, near_got[:, -head_rows:])
    cross_half = out_part(1, mine) + wide(near_got[:, :-head_rows])
    cross_payload = [
        jnp.concatenate([far_of(half_0, m, 0), far_of(cross_half, m, 0)], axis=0) for m in range(1, far_count)
    ]
    across_got = jnp.concatenate([across_got_a, across_got_b], axis=-1)
    in_sum = wide(in_keep[0]) + wide(in_got[0]) + wide(across_got)
    near_sent = jnp.concatenate([theirs(in_sum).astype(BF16), other_half(d_weight_1)], axis=1)
    near_sent, *cross_payload = lax.optimization_barrier((near_sent, *cross_payload))
    near_got = dp_swap(near_sent, 1)
    cross_far = [dp_swap(p, 2 * (m + 1)) for m, p in enumerate(cross_payload)]
    packed_2, d_weight_2 = head_step(2, after(info, near_sent, *cross_payload))

    d_weight_2, packed_2, near_got, *cross_far = lax.optimization_barrier(
        (d_weight_2, packed_2, near_got, *cross_far)
    )
    hr = head_rows
    steps = opening, middle_step, third_step, last_step, finish
    if hr % 16:
        steps = plain_steps(place, in_order_of(place, far_count))
    step_a, step_b, step_c, step_d, step_e = steps
    sent_2 = other_half(d_weight_2)
    got_2 = dp_swap(sent_2, 1)
    quarter_0, half_1, cross_total, own_total, *payload = step_a(
        after(info, sent_2), half_0, d_weight_1, near_got, cross_half, own_half, cross_far, own_far
    )
    step_1 = [dp_swap(p, 2 * (m + 1)) for m, p in enumerate(payload)]
    out_across = swap(cross_total, 2)
    dx_keep, dx_send, gain_part = input_part(
        [packed_0, packed_1, after(packed_2, cross_total, *payload)], packed_weight, [d_weight_0, d_weight_1, d_weight_2]
    )
    d_weight_2, got_2, step_1, out_across, dx_send, gain_part = lax.optimization_barrier(
        (d_weight_2, got_2, step_1, out_across, dx_send, gain_part)
    )
    near_rows = swap(dx_send, 1)
    gains = [gain_part] + [swap(gain_part, r) for r in (1, 2, 3)]

    whole_0, quarter_1, half_2, *payload = step_b(info, quarter_0, half_1, d_weight_2, got_2, step_1)
    whole_0, near_rows, *payload = lax.optimization_barrier((whole_0, near_rows, *payload))
    step_2 = [dp_swap(p, 2 * (m + 1)) for m, p in enumerate(payload)]
    other_0 = dp_swap(whole_0, 1)
    cross_sum = (wide(dx_keep[1]) + wide(after(near_rows[1], *step_2))).astype(BF16)
    cross_got = swap(cross_sum, 2)

    whole_1, third, project_grad, vec_total = step_c(
        after(info, cross_sum), quarter_1, half_2, own_total, out_across, gains, step_2, shard_rows
    )
    step_3 = far_swaps(lambda m: third)
    in_half = mine(in_sum) + wide(near_got[:, :-hr])

    last_own = step_d(after(info, other_0), third, whole_1, step_3)
    last_sent, in_half = lax.optimization_barrier((last_own, in_half))
    last_near = dp_swap(last_sent, 1)
    in_far = far_swaps(lambda m: far_of(in_half, m, 0))
    input_grad = input_gradient(inputs, norm1_gain, d_middle, dx_keep, near_rows, cross_got)
    query_grad, key_grad, value_grad, query_bias_grad, value_bias_grad, o_total, norm1_total = step_e(
        after(info, input_grad), [whole_0, other_0, whole_1, last_own, last_near], norm1_gain
    )
    *in_far, norm1_total = lax.optimization_barrier((*in_far, norm1_total))
    hidden_grad = keep_far(in_half, 0) + sum(wide(g) for g in in_far)
    return (
        output,
        input_grad,
        norm1_total,
        query_grad.T,
        query_bias_grad,
        key_grad.T,
        value_grad.T,
        value_bias_grad,
        vec_total[2, :inner_rows],
        o_total,
        vec_total[5],
        vec_total[3],
        hidden_grad,
        vec_total[1],
        vec_total[0],
        project_grad.T,
        vec_total[4],
    )


def solution(mesh):
    rows = P(("dp", "head"), None)
    columns = P(None, "head")
    head = P("head")
    return jax.shard_map(
        local,
        mesh=mesh,
        in_specs=(
            rows, rows, P("dp", None), P(), columns, head, columns, columns, head, head,
            P("head", None), P(), P(), P("dp", "head"), head, head, P("head", "dp"), P(),
        ),
        out_specs=(
            rows, rows, P(), columns, head, columns, columns, head, head, P("head", None),
            P(), P(), P("dp", "head"), head, head, P("head", "dp"), P(),
        ),
        check_vma=False,
    )
```

```python
import functools
import math

import jax
import jax.numpy as jnp
from jax import lax
from jax.experimental import pallas as pl
from jax.experimental.pallas import tpu as pltpu
from jax.sharding import PartitionSpec as P

D = 768
HEAD_DIM = 64
FF = 3072
SHORT = 512
SLOT = 4 * SHORT

BF16 = jnp.bfloat16
F32 = jnp.float32
epsilon = 1e-05
excluded = 1e30
SCALE = HEAD_DIM ** (-0.5)
LOG2_SCALE = SCALE * math.log2(math.e)
LN2 = math.log(2.0)
QUERY_ROWS = 512
KEY_ROWS = 512
VMEM_LIMIT = 56 << 20


def nt(left, right):
    return lax.dot_general(left, right, (((1,), (1,)), ((), ())), preferred_element_type=F32)


def nn(left, right):
    return lax.dot_general(left, right, (((1,), (0,)), ((), ())), preferred_element_type=F32)


def tn(left, right):
    return lax.dot_general(left, right, (((0,), (0,)), ((), ())), preferred_element_type=F32)


def attention_forward_kernel(before, info, *refs):
    x_refs, (w_ref, b_ref), earlier = refs[0:4], refs[4:6], refs[6 : 6 + 4 * (before > 0)]
    *o_refs, lse_ref, q_ref, k_ref, v_ref = refs[6 + len(earlier) :]
    head = pl.program_id(0)
    lane = lax.broadcasted_iota(jnp.int32, (SHORT, 128), 1)
    row = lax.broadcasted_iota(jnp.int32, (SHORT, 128), 0)
    for o_ref, early in zip(o_refs, earlier):

        @pl.when(head == 0)
        def _():
            o_ref[0 : before * HEAD_DIM, :] = early[...]

    for block, x_ref in enumerate(x_refs):
        rows = pl.ds(block * SHORT, SHORT)
        packed = (nt(x_ref[...], w_ref[0]) + b_ref[0]).astype(BF16)
        inside = jnp.where(row < info[1 + block], 1.0, 0.0).astype(F32)
        q_flags = jnp.where(lane == 0, inside, jnp.where(lane == 1, 1.0 - inside, 0.0))
        k_flags = jnp.where(
            lane == 0, (inside - 1.0) * excluded, jnp.where(lane == 1, inside * -excluded, 0.0)
        )
        q, k, v = packed[:, 0:64], packed[:, 64:128], packed[:, 128:192]
        scaled = k.astype(F32) * LOG2_SCALE
        high = scaled.astype(BF16)
        low = (scaled - high.astype(F32)).astype(BF16)
        q_ref[0, rows, :] = jnp.concatenate([q, q, q_flags.astype(BF16)], axis=1)
        k_ref[0, rows, :] = jnp.concatenate([high, low, k_flags.astype(BF16)], axis=1)
        v_ref[0, rows, :] = jnp.concatenate([v, jnp.ones((SHORT, 64), BF16)], axis=1)

    out_rows = pl.ds(pl.multiple_of((before + head) * HEAD_DIM, HEAD_DIM), HEAD_DIM)

    def block_of(start, keys):
        scores = nt(q_ref[0, pl.ds(start, QUERY_ROWS), :], k_ref[0, keys, :])
        top = jnp.max(scores, axis=1, keepdims=True)
        weights = jnp.exp2(scores - top).astype(BF16)
        out = nn(weights, v_ref[0, keys, :])
        out_lane = lax.broadcasted_iota(jnp.int32, (QUERY_ROWS, 128), 1)
        out = jnp.where(out_lane == 65, jnp.broadcast_to(top, (QUERY_ROWS, 128)), out).T
        total = out[64:65]
        o_refs[start // SHORT][out_rows, pl.ds(start % SHORT, QUERY_ROWS)] = (
            out[0:64] * (1.0 / total)
        ).astype(BF16)
        lse_ref[0, :, pl.ds(start, QUERY_ROWS)] = out[65:66] + jnp.log2(total)

    longer = info[0] > SHORT

    @pl.when(longer)
    def _():
        for start in range(0, SLOT, QUERY_ROWS):
            block_of(start, pl.ds(0, SLOT))

    @pl.when(jnp.logical_not(longer))
    def _():
        for start in range(0, SLOT, QUERY_ROWS):
            block_of(start, pl.ds(start // SHORT * SHORT, SHORT))


def head_spec(*shape):
    return pl.BlockSpec((1,) + shape, lambda h, info: (h,) + (0,) * len(shape))


def whole_spec(*shape):
    return pl.BlockSpec(shape, lambda h, info: (0,) * len(shape))


def attention_forward(info, rows, weights, biases, before, count, earlier):
    out_rows = (before + count) * HEAD_DIM
    later = lambda *shape: pl.BlockSpec((1,) + shape, lambda h, info: (before + h,) + (0,) * len(shape))
    return pl.pallas_call(
        functools.partial(attention_forward_kernel, before),
        grid_spec=pltpu.PrefetchScalarGridSpec(
            num_scalar_prefetch=1,
            grid=(count,),
            in_specs=[whole_spec(SHORT, D)] * 4
            + [later(192, D), later(1, 192)]
            + [whole_spec(before * HEAD_DIM, SHORT)] * len(earlier),
            out_specs=[whole_spec(out_rows, SHORT)] * 4
            + [head_spec(1, SLOT), head_spec(SLOT, 256), head_spec(SLOT, 256), head_spec(SLOT, 128)],
        ),
        out_shape=[jax.ShapeDtypeStruct((out_rows, SHORT), BF16)] * 4
        + [
            jax.ShapeDtypeStruct((count, 1, SLOT), F32),
            jax.ShapeDtypeStruct((count, SLOT, 256), BF16),
            jax.ShapeDtypeStruct((count, SLOT, 256), BF16),
            jax.ShapeDtypeStruct((count, SLOT, 128), BF16),
        ],
        compiler_params=pltpu.CompilerParams(
            dimension_semantics=("arbitrary",), vmem_limit_bytes=VMEM_LIMIT
        ),
        cost_estimate=pl.CostEstimate(
            flops=8_000_000_000 * count, bytes_accessed=4_000_000 * count, transcendentals=4_000_000 * count
        ),
        name="attention_forward",
    )(info, *rows, weights, biases, *earlier)


def attention_backward_kernel(*refs):
    info, *pieces = refs[:9]
    lse_ref, q_ref, k_ref, v_ref = refs[9:13]
    x_refs = refs[13:17]
    rest = list(refs[17:])
    packed_ref, dw_ref, grad, dq, delta, packed, x_all, sems = rest
    copies = [
        pltpu.make_async_copy(x_ref, x_all.at[block], sems.at[block]) for block, x_ref in enumerate(x_refs)
    ]
    for copy in copies:
        copy.start()
    for block, (g_ref, o_ref) in enumerate(zip(pieces[:4], pieces[4:])):
        g = g_ref[...].astype(F32)
        cols = pl.ds(block * SHORT, SHORT)
        delta[:, cols] = jnp.sum(g * o_ref[...].astype(F32), axis=0, keepdims=True)
        grad[cols, :] = g.T.astype(BF16)

    def block_of(start, queries, first):
        rows = pl.ds(start, KEY_ROWS)
        k = k_ref[0, rows, :]
        q = q_ref[0, queries, :]
        g = grad[queries, :]
        weights = jnp.exp2(nt(k, q) - lse_ref[0, :, queries])
        d_probs = nt(v_ref[0, rows, 0:64], g)
        d_scores = (weights * (d_probs - delta[:, queries])).astype(BF16)
        packed[rows, 128:192] = nn(weights.astype(BF16), g).astype(BF16)
        packed[rows, 64:128] = (nn(d_scores, q[:, 0:128])[:, 0:64] * SCALE).astype(BF16)
        term = tn(k[:, 0:128], d_scores)
        if first:
            dq[:, queries] = term
        else:
            dq[:, queries] += term

    longer = info[0] > SHORT

    @pl.when(longer)
    def _():
        for start in range(0, SLOT, KEY_ROWS):
            block_of(start, pl.ds(0, SLOT), start == 0)

    @pl.when(jnp.logical_not(longer))
    def _():
        for start in range(0, SLOT, KEY_ROWS):
            block_of(start, pl.ds(start // SHORT * SHORT, SHORT), start % SHORT == 0)

    total = dq[...].T
    packed[:, 0:64] = ((total[:, 0:64] + total[:, 64:128]) * LN2).astype(BF16)
    packed_ref[...] = packed[...]
    for copy in copies:
        copy.wait()
    d_weight = jnp.zeros((192, D), F32)
    d_bias = jnp.zeros((1, 192), F32)
    for block in range(4):
        part = packed[pl.ds(block * SHORT, SHORT), :]
        d_weight += tn(part, x_all[block])
        d_bias += jnp.sum(part.astype(F32), axis=0, keepdims=True)
    dw_ref[0:192, :] = d_weight.astype(BF16)
    d_bias = jnp.concatenate([d_bias, jnp.zeros((1, D - 192), F32)], axis=1)
    row = lax.broadcasted_iota(jnp.int32, (64, D), 0)
    dw_ref[192:256, :] = jnp.where(row == 0, d_bias, 0.0).astype(BF16)


def attention_backward(head, info, grads, attended, saved, local_head, rows):
    one = lambda *shape: pl.BlockSpec((1,) + shape, lambda i, info: (local_head,) + (0,) * len(shape))
    in_specs = (
        [pl.BlockSpec((HEAD_DIM, SHORT), lambda i, info: (head, 0))] * 8
        + [one(1, SLOT), one(SLOT, 256), one(SLOT, 256), one(SLOT, 128)]
        + [pl.BlockSpec(memory_space=pl.ANY)] * 4
    )
    operands = [*grads, *attended, *saved, *rows]
    out_specs = [whole_spec(SLOT, 192), whole_spec(256, D)]
    out_shape = [jax.ShapeDtypeStruct((SLOT, 192), BF16), jax.ShapeDtypeStruct((256, D), BF16)]
    return pl.pallas_call(
        attention_backward_kernel,
        grid_spec=pltpu.PrefetchScalarGridSpec(
            num_scalar_prefetch=1,
            grid=(1,),
            in_specs=in_specs,
            out_specs=out_specs,
            scratch_shapes=[
                pltpu.VMEM((SLOT, HEAD_DIM), BF16),
                pltpu.VMEM((128, SLOT), F32),
                pltpu.VMEM((1, SLOT), F32),
                pltpu.VMEM((SLOT, 192), BF16),
                pltpu.VMEM((4, SHORT, D), BF16),
                pltpu.SemaphoreType.DMA((4,)),
            ],
        ),
        out_shape=out_shape,
        compiler_params=pltpu.CompilerParams(
            dimension_semantics=("arbitrary",), vmem_limit_bytes=VMEM_LIMIT
        ),
        cost_estimate=pl.CostEstimate(
            flops=15_000_000_000, bytes_accessed=8_000_000, transcendentals=4_000_000
        ),
        name="attention_backward",
    )(info, *operands)


def input_part_kernel(heads, *refs):
    packed, (w_ref,), d_weights = refs[:heads], refs[heads : heads + 1], refs[heads + 1 : 2 * heads + 1]
    dx_keep, dx_send, gain_ref = refs[2 * heads + 1 :]
    for block in (1, 3, 2, 0):
        rows = pl.ds(block * SHORT, SHORT)
        term = nn(packed[0][rows, :], w_ref[0])
        for h in range(1, heads):
            term += nn(packed[h][rows, :], w_ref[h])
        out = dx_send if block % 2 else dx_keep
        out[block // 2] = term.astype(BF16)
    gain = jnp.zeros((1, D), F32)
    for h in range(heads):
        gain += jnp.sum(d_weights[h][0:192, :].astype(F32) * w_ref[h].astype(F32), axis=0, keepdims=True)
    gain_ref[...] = jnp.broadcast_to(gain, (8, D))


def input_part(packed, weights, d_weights):
    heads = len(packed)
    return pl.pallas_call(
        functools.partial(input_part_kernel, heads),
        out_shape=[jax.ShapeDtypeStruct((2, SHORT, D), BF16)] * 2 + [jax.ShapeDtypeStruct((8, D), F32)],
        compiler_params=pltpu.CompilerParams(vmem_limit_bytes=VMEM_LIMIT),
        cost_estimate=pl.CostEstimate(flops=6_000_000_000, bytes_accessed=8_000_000, transcendentals=0),
        name="input_part",
    )(*packed, weights, *d_weights)


def step_call(kernel, name, info, operands, outs, first_blocks=()):
    def spec(i, shape):
        if i in first_blocks:
            return pl.BlockSpec((1,) + shape[1:], lambda j, info: (info[7],) + (0,) * (len(shape) - 1))
        return pl.BlockSpec(shape, lambda j, info: (0,) * len(shape))

    return pl.pallas_call(
        kernel,
        grid_spec=pltpu.PrefetchScalarGridSpec(
            num_scalar_prefetch=1,
            grid=(1,),
            in_specs=[spec(i, v.shape) for i, v in enumerate(operands)],
            out_specs=[pl.BlockSpec(shape, lambda j, info, n=len(shape): (0,) * n) for shape, _ in outs],
        ),
        out_shape=[jax.ShapeDtypeStruct(shape, kind) for shape, kind in outs],
        name=name,
    )(info, *operands)


def opening_kernel(info, half_0, d_w1, bundle, cross_half, own_half, *refs):
    count, rows, _ = half_0.shape
    cross, own, outs = refs[: count - 1], refs[count - 1 : 2 * count - 2], refs[2 * count - 2 :]
    quarter, half_1, cross_total, own_total = outs[:4]
    near, far = info[6], info[7]
    total = half_0[far].astype(F32)
    for g in cross:
        total += g[0:rows, :].astype(F32)
    quarter[...] = total.astype(BF16)
    for m in range(count):
        value = d_w1[near * count + m].astype(F32) + bundle[m, bundle.shape[1] - rows :, :].astype(F32)
        half_1[m] = value.astype(BF16)
    for m in range(1, count):
        outs[3 + m][0:rows, :] = quarter[...]
        outs[3 + m][rows : 2 * rows, :] = half_1[far ^ m]
    total = cross_half[0]
    for g in cross:
        total += g[rows:, :].astype(F32)
    cross_total[...] = total.astype(BF16)
    total = own_half[0]
    for g in own:
        total += g[...].astype(F32)
    own_total[...] = total


def opening(info, half_0, d_w1, bundle, cross_half, own_half, cross, own):
    count, rows, _ = half_0.shape
    blocks = lambda v: v.reshape(2 * count, rows, D)
    part = cross_half.shape[1]
    outs = [((rows, D), BF16), (half_0.shape, BF16), ((part, D), BF16), ((part, D), F32)]
    outs += [((2 * rows, D), BF16)] * (count - 1)
    operands = [half_0, blocks(d_w1), bundle, cross_half, own_half, *cross, *own]
    return step_call(opening_kernel, "opening", info, operands, outs, (3, 4))


def middle_kernel(info, quarter_0, half_1, d_w2, near_got, *refs):
    count, rows, _ = half_1.shape
    got, (whole, quarter, half_2, *payload) = refs[: count - 1], refs[count - 1 :]
    near, far = info[6], info[7]
    whole[0] = quarter_0[...]
    total = half_1[far].astype(F32)
    for m, g in enumerate(got):
        whole[m + 1] = g[0:rows, :]
        total += g[rows : 2 * rows, :].astype(F32)
    quarter[...] = total.astype(BF16)
    for m in range(count):
        half_2[m] = (d_w2[near * count + m].astype(F32) + near_got[m].astype(F32)).astype(BF16)
    for m in range(1, count):
        payload[m - 1][0:rows, :] = quarter[...]
        payload[m - 1][rows : 2 * rows, :] = half_2[far ^ m]


def middle_step(info, quarter_0, half_1, d_w2, near_got, got):
    count, rows, _ = half_1.shape
    outs = [(half_1.shape, BF16), ((rows, D), BF16), (half_1.shape, BF16)] + [((2 * rows, D), BF16)] * (count - 1)
    operands = [quarter_0, half_1, d_w2.reshape(2 * count, rows, D), near_got, *got]
    return step_call(middle_kernel, "middle_step", info, operands, outs)


def in_two(values):
    high = values.astype(BF16).astype(F32)
    return jnp.concatenate([high[0:4], (values - high)[0:4]], axis=0)


def third_kernel(info, quarter_1, half_2, own_total, across, *refs):
    count, rows, _ = half_2.shape
    gain = sum(ref[...] for ref in refs[:4])
    refs = refs[4:]
    got, (whole, third, project, vectors) = refs[: count - 1], refs[count - 1 :]
    far = info[7]
    whole[0] = quarter_1[...]
    total = half_2[far].astype(F32)
    for m, g in enumerate(got):
        whole[m + 1] = g[0:rows, :]
        total += g[rows : 2 * rows, :].astype(F32)
    part = own_total[...] + across[...].astype(F32)
    project[...] = part[0 : project.shape[0]]
    vectors[...] = part[part.shape[0] - 8 :]
    o_part = part[project.shape[0] : part.shape[0] - 8]
    third[...] = jnp.concatenate([total, o_part, in_two(gain)], axis=0).astype(BF16)


def third_step(info, quarter_1, half_2, own_total, across, gains, got, shard_rows):
    count, rows, _ = half_2.shape
    third_rows = rows + own_total.shape[0] - shard_rows
    outs = [(half_2.shape, BF16), ((third_rows, D), BF16), ((shard_rows, D), F32), ((8, D), F32)]
    return step_call(third_kernel, "third_step", info, [quarter_1, half_2, own_total, across, *gains, *got], outs)


def last_kernel(info, third, whole_1, *refs):
    got, out = refs[:-1], refs[-1]
    rows = third.shape[0]
    value = third[...].astype(F32)
    total = value[rows - 8 :]
    for m, g in enumerate(got):
        out[m + 1, 0:rows, :] = g[...]
        total += g[...].astype(F32)[rows - 8 :]
    total = jnp.broadcast_to(total[0:1] + total[4:5], (8, D))
    out[0, 0:rows, :] = jnp.concatenate([value[: rows - 8], in_two(total)], axis=0).astype(BF16)
    for m in range(whole_1.shape[0]):
        out[m, rows:, :] = whole_1[m]


def last_step(info, third, whole_1, got):
    rows = third.shape[0] + whole_1.shape[1]
    return step_call(last_kernel, "last_step", info, [third, whole_1, *got], [((len(got) + 1, rows, D), BF16)])[0]


def finish_kernel(info, w0, n0, w1, w2, n2, gain, q_out, k_out, v_out, q_bias, v_bias, o_out, gain_out, whole):
    near, far = info[6], info[7]
    count, rows, _ = w0.shape
    third_rows = w2.shape[1] - rows
    below = n2.at[:, pl.ds(third_rows, rows), :]
    for h, pair in enumerate(((w0, n0), (w1, below), (w2, n2))):
        for n, half in enumerate(pair):
            for m in range(count):
                start = ((near ^ n) * count + (far ^ m)) * rows
                whole[h, pl.ds(pl.multiple_of(start, rows), rows), :] = half[m, 0:rows, :]
    for kind, out in enumerate((q_out, k_out, v_out)):
        for h in range(3):
            part = whole[h, kind * HEAD_DIM : (kind + 1) * HEAD_DIM, :].astype(F32)
            out[h * HEAD_DIM : (h + 1) * HEAD_DIM, :] = part
    bias = [whole[h, 192:208, :].astype(F32)[0:1] for h in range(3)]
    for out, first in ((q_bias, 0), (v_bias, 128)):
        out[...] = jnp.concatenate([b[:, first : first + HEAD_DIM] for b in bias], axis=1)[0]
    o_rows = third_rows - rows - 8
    total = jnp.zeros((1, D), F32)
    for n, half in enumerate((w2, n2)):
        for m in range(count):
            value = half[m, rows:third_rows, :].astype(F32)
            start = ((far ^ m) * 2 + (near ^ n)) * o_rows
            o_out[pl.ds(pl.multiple_of(start, o_rows), o_rows), :] = value[0:o_rows]
            if m == 0:
                total += value[o_rows : o_rows + 1] + value[o_rows + 4 : o_rows + 5]
    gain_out[...] = total[0] / gain[...].astype(F32)


def finish(info, halves, gain):
    count, rows, _ = halves[0].shape
    o_rows = halves[-1].shape[1] - 2 * rows - 8
    outs = [((192, D), F32)] * 3 + [((192,), F32)] * 2 + [((2 * count * o_rows, D), F32), ((D,), F32)]
    fixed = lambda *shape: pl.BlockSpec(shape, lambda i, info: (0,) * len(shape))
    return pl.pallas_call(
        finish_kernel,
        grid_spec=pltpu.PrefetchScalarGridSpec(
            num_scalar_prefetch=1,
            grid=(1,),
            in_specs=[fixed(*v.shape) for v in (*halves, gain)],
            out_specs=[fixed(*shape) for shape, _ in outs],
            scratch_shapes=[pltpu.VMEM((3, 256, D), BF16)],
        ),
        out_shape=[jax.ShapeDtypeStruct(shape, kind) for shape, kind in outs],
        name="finish",
    )(info, *halves, gain)


def first_norm_kernel(x_ref, gain_ref, out_ref):
    unit, _ = rows_normed(x_ref[...].astype(F32))
    out_ref[...] = (unit * gain_ref[...].astype(F32)[None]).astype(BF16)


def first_norm(inputs, gain):
    return pl.pallas_call(
        first_norm_kernel,
        out_shape=jax.ShapeDtypeStruct(inputs.shape, BF16),
        name="first_norm",
    )(inputs, gain)


def input_grad_kernel(x_ref, gain_ref, middle_ref, keep_ref, near_ref, got_ref, out_ref):
    unit, scaling = rows_normed(x_ref[...].astype(F32))
    grad = keep_ref[0].astype(F32) + near_ref[0].astype(F32) + got_ref[...].astype(F32)
    out_ref[...] = middle_ref[...] + rows_back(grad * gain_ref[...].astype(F32)[None], unit, scaling)


def input_gradient(inputs, gain, d_middle, keep, near, got):
    fixed = lambda *shape: pl.BlockSpec(shape, lambda i: (0,) * len(shape))
    tokens = inputs.shape[0]
    first = pl.BlockSpec((1, tokens, D), lambda i: (0, 0, 0))
    return pl.pallas_call(
        input_grad_kernel,
        grid=(1,),
        in_specs=[fixed(tokens, D), fixed(D), fixed(tokens, D), first, first, fixed(tokens, D)],
        out_specs=fixed(tokens, D),
        out_shape=jax.ShapeDtypeStruct((tokens, D), F32),
        name="input_gradient",
    )(inputs, gain, d_middle, keep, near, got)


def rows_normed(values):
    centre = jnp.mean(values, axis=1, keepdims=True)
    spread = jnp.mean(values * values, axis=1, keepdims=True) - centre * centre
    scaling = lax.rsqrt(spread + epsilon)
    return (values - centre) * scaling, scaling


def rows_back(scaled, unit, scaling):
    first = jnp.mean(scaled, axis=1, keepdims=True)
    second = jnp.mean(scaled * unit, axis=1, keepdims=True)
    return scaling * (scaled - first - unit * second)


def lanes_folded(values):
    return sum(values[:, c : c + 128] for c in range(0, values.shape[1], 128))


def token_kernel(pieces, source_count, info, *refs):
    sources = refs[:source_count]
    a_refs = refs[source_count : source_count + 4]
    packs = refs[source_count + 4 : source_count + 8]
    x_ref, cot_ref, vec_ref = refs[source_count + 8 : source_count + 11]
    out_ref, middle_grad_ref, g0, g1, g2, g3, in_keep, in_send, out_keep, out_send = refs[
        source_count + 11 : source_count + 21
    ]
    (
        w_in, w_out, staged, sides, activated, slope, d_mixed, unit_c, middle, unit2, vec_out_ref, in_sems, out_sems,
        side_sems,
    ) = refs[source_count + 21 :]
    count, block_rows = staged.shape[1:3]
    tokens = x_ref.shape[0]
    ff_slice = w_in.shape[-1]
    ff = 4 * ff_slice
    inner_rows = a_refs[0].shape[0]

    loads = {}
    for which, target in ((0, w_in), (1, w_out)):
        for r in range(4):
            loads[which, r] = [
                pltpu.make_async_copy(source, target.at[r, pl.ds(start, source.shape[0])], in_sems.at[which, r, i])
                for i, (source, start) in enumerate(pieces(info, sources, which, r))
            ]
    for which in range(2):
        for r in range(4):
            for copy in loads[which, r]:
                copy.start()

    stores = {}

    def store(which, r, value):
        staged[r] = value.astype(BF16).reshape(count, block_rows, ff_slice)
        target = ((in_keep, in_send), (out_keep, out_send))[which][r % 2]
        target = target.at[r // 2, :, pl.ds(0, block_rows)]
        stores[r] = pltpu.make_async_copy(staged.at[r], target, out_sems.at[which, r])
        stores[r].start()

    values = jnp.concatenate([a_ref[...] for a_ref in a_refs], axis=0).astype(F32)
    centre = jnp.mean(values, axis=0, keepdims=True)
    spread = jnp.mean(values * values, axis=0, keepdims=True) - centre * centre
    scaling_c = lax.rsqrt(spread + epsilon)
    unit = (values - centre) * scaling_c
    unit_c[...] = unit
    rows_below = [p[inner_rows : inner_rows + 16, 0:ff_slice].astype(F32) for p in packs]
    gain_rows = [jnp.broadcast_to(p[2:3, 0:inner_rows], (128, inner_rows)).T[:, 0:1] for p in rows_below]
    gain_c = jnp.concatenate(gain_rows, axis=0)
    context = (unit * gain_c).astype(BF16)
    weight_o = jnp.concatenate([p[0:inner_rows, 0:D] for p in packs], axis=0)
    total = x_ref[...].astype(F32) + (tn(context, weight_o) + vec_ref[0:1, :])
    middle[...] = total
    unit, scaling2 = rows_normed(total)
    unit2[...] = unit
    normed2 = (unit * vec_ref[1:2, :]).astype(BF16)
    flipped = normed2.T
    cot = cot_ref[...]
    cot_flipped = cot.T

    fold_a = jnp.zeros((tokens, 128), F32)
    fold_b = jnp.zeros((tokens, 128), F32)
    for r in range(4):
        for copy in loads[0, r]:
            copy.wait()
        hidden = nn(normed2, w_in[r]) + rows_below[r][0:1]
        density = jnp.exp(hidden * hidden * -0.5) * (1.0 / math.sqrt(2.0 * math.pi))
        share = 0.5 * (1.0 + lax.erf(hidden * math.sqrt(0.5)))
        value = hidden * share
        activated[r] = value
        slope[r] = share + hidden * density
        fold_a += lanes_folded(value)
        fold_b += lanes_folded(value * value)
    centre = jnp.sum(fold_a, axis=1, keepdims=True) * (1.0 / ff)
    spread = jnp.sum(fold_b, axis=1, keepdims=True) * (1.0 / ff) - centre * centre
    scaling = lax.rsqrt(spread + epsilon)

    fold_a = jnp.zeros((tokens, 128), F32)
    fold_b = jnp.zeros((tokens, 128), F32)
    projected = jnp.zeros((tokens, D), F32)
    for r in range(4):
        for copy in loads[1, r]:
            copy.wait()
        gain = rows_below[r][1:2]
        unit = (activated[r] - centre) * scaling
        activated[r] = unit
        mixed = (unit * gain).astype(BF16)
        projected += nt(mixed, w_out[r])
        store(1, r, nn(cot_flipped, mixed))
        grad = nn(cot, w_out[r])
        vec_out_ref[r, 0:1, :] = jnp.sum(grad * unit, axis=0, keepdims=True)
        scaled = grad * gain
        d_mixed[r] = scaled
        fold_a += lanes_folded(scaled)
        fold_b += lanes_folded(scaled * unit)
    first = jnp.sum(fold_a, axis=1, keepdims=True) * (1.0 / ff)
    second = jnp.sum(fold_b, axis=1, keepdims=True) * (1.0 / ff)
    out_ref[...] = (middle[...] + (projected + vec_ref[2:3, :])).astype(BF16)

    d_normed2 = jnp.zeros((tokens, D), F32)
    for r in range(4):
        grad = (slope[r] * (scaling * (d_mixed[r] - first - activated[r] * second))).astype(BF16)
        vec_out_ref[r, 1:2, :] = jnp.sum(grad.astype(F32), axis=0, keepdims=True)
        stores[r].wait()
        store(0, r, nn(flipped, grad))
        d_normed2 += nt(grad, w_in[r])

    cot = cot.astype(F32)
    unit = unit2[...]
    d_middle = cot + rows_back(d_normed2 * vec_ref[1:2, :], unit, scaling2)
    middle_grad_ref[...] = d_middle
    d_branch = d_middle.astype(BF16)
    norm2_part = jnp.sum(d_normed2 * unit, axis=0, keepdims=True)
    project_bias_part = jnp.sum(cot, axis=0, keepdims=True)
    output_bias_part = jnp.sum(d_branch.astype(F32), axis=0, keepdims=True)
    d_context = nt(weight_o, d_branch)
    o_grad = nn(context, d_branch)
    unit = unit_c[...]
    inner_part = jnp.sum(d_context * unit, axis=1, keepdims=True)
    inner_part = jnp.broadcast_to(inner_part, (D, 128)).T[0:1]
    scaled = d_context * gain_c
    first = jnp.mean(scaled, axis=0, keepdims=True)
    second = jnp.mean(scaled * unit, axis=0, keepdims=True)
    grad = (scaling_c * (scaled - first - unit * second)).astype(BF16)
    for i, g_ref in enumerate((g0, g1, g2, g3)):
        rows = slice(i * inner_rows, (i + 1) * inner_rows)
        g_ref[...] = grad[rows]
        vec_out_ref[i, 2:3, 0:inner_rows] = inner_part[:, rows]
        vec_out_ref[i, 2:3, inner_rows:D] = jnp.zeros((1, D - inner_rows), F32)
        vec_out_ref[i, 3:4, :] = norm2_part
        vec_out_ref[i, 4:5, :] = project_bias_part
        vec_out_ref[i, 5:6, :] = output_bias_part
        vec_out_ref[i, 6:8, :] = jnp.zeros((2, D), F32)
    o_rows = inner_rows // count
    side_stores = []
    for i in range(4):
        vectors = vec_out_ref[i]
        for d in range(count):
            start = i * inner_rows + d * o_rows
            block = jnp.concatenate([o_grad[start : start + o_rows], vectors], axis=0)
            sides[i, d] = block.astype(BF16)
        target = (out_keep, out_send)[i % 2].at[i // 2, :, pl.ds(block_rows, o_rows + 8)]
        side_stores.append(pltpu.make_async_copy(sides.at[i], target, side_sems.at[i]))
        side_stores[i].start()
    for copy in list(stores.values()) + side_stores:
        copy.wait()


def token_section(info, attended, packs, inputs, cotangent, vectors, sources, pieces, piece_count):
    tokens = inputs.shape[0]
    inner_rows = attended[0].shape[0]
    ff_slice = sources[0].shape[-1]
    fixed = lambda *shape: pl.BlockSpec(shape, lambda s, info: (0,) * len(shape))
    anywhere = pl.BlockSpec(memory_space=pl.ANY)
    grad_piece = jax.ShapeDtypeStruct((inner_rows, tokens), BF16)
    count = 8
    block_rows, side_rows = D // count, inner_rows // count + 8
    grad_pair = lambda rows: jax.ShapeDtypeStruct((2, count, rows, ff_slice), BF16)
    return pl.pallas_call(
        functools.partial(token_kernel, pieces, len(sources)),
        grid_spec=pltpu.PrefetchScalarGridSpec(
            num_scalar_prefetch=1,
            grid=(1,),
            in_specs=[anywhere] * len(sources)
            + [fixed(*a.shape) for a in attended]
            + [fixed(*p.shape) for p in packs]
            + [fixed(tokens, D), fixed(tokens, D), fixed(8, D)],
            out_specs=[fixed(tokens, D), fixed(tokens, D)]
            + [fixed(inner_rows, tokens)] * 4
            + [anywhere] * 4,
            scratch_shapes=[
                pltpu.VMEM((4, D, ff_slice), BF16),
                pltpu.VMEM((4, D, ff_slice), BF16),
                pltpu.VMEM((4, count, block_rows, ff_slice), BF16),
                pltpu.VMEM((4, count, side_rows, ff_slice), BF16),
                pltpu.VMEM((4, tokens, ff_slice), F32),
                pltpu.VMEM((4, tokens, ff_slice), F32),
                pltpu.VMEM((4, tokens, ff_slice), F32),
                pltpu.VMEM((D, tokens), F32),
                pltpu.VMEM((tokens, D), F32),
                pltpu.VMEM((tokens, D), F32),
                pltpu.VMEM((4, 8, D), F32),
                pltpu.SemaphoreType.DMA((2, 4, piece_count)),
                pltpu.SemaphoreType.DMA((2, 4)),
                pltpu.SemaphoreType.DMA((4,)),
            ],
        ),
        out_shape=[
            jax.ShapeDtypeStruct((tokens, D), BF16),
            jax.ShapeDtypeStruct((tokens, D), F32),
            *[grad_piece] * 4,
            *[grad_pair(block_rows)] * 2,
            *[grad_pair(block_rows + side_rows)] * 2,
        ],
        compiler_params=pltpu.CompilerParams(
            dimension_semantics=("arbitrary",), vmem_limit_bytes=60 << 20
        ),
        cost_estimate=pl.CostEstimate(
            flops=20_000_000_000, bytes_accessed=30_000_000, transcendentals=4_000_000
        ),
        name="token_section",
    )(info, *sources, *attended, *packs, inputs, cotangent, vectors)


def swap(values, distance):
    count = lax.axis_size("head")
    return lax.ppermute(values, "head", [(i, i ^ distance) for i in range(count)])


def dp_swap(values, distance):
    count = lax.axis_size("dp")
    return lax.ppermute(values, "dp", [(i, i ^ distance) for i in range(count)])


def pick(values, index, axis):
    return lax.dynamic_index_in_dim(values, index, axis, keepdims=False)


def wide(values):
    return values.astype(F32)


def swap_near(values, axis):
    near = lax.axis_index("dp") & 1
    return dp_swap(pick(values, 1 - near, axis).astype(BF16), 1)


def keep_near(values, axis):
    return pick(values, lax.axis_index("dp") & 1, axis)


def keep_far(values, axis):
    return pick(values, lax.axis_index("dp") >> 1, axis)


def far_of(values, m, axis):
    return pick(values, (lax.axis_index("dp") >> 1) ^ m, axis).astype(BF16)


def far_swaps(payload):
    count = lax.axis_size("dp") // 2
    return [dp_swap(payload(m), 2 * m) for m in range(1, count)]


def after(value, *others):
    return lax.optimization_barrier((value,) + others)[0]


def in_order_of(place, far_count):
    def in_order(own, neighbour):
        total = jnp.zeros((2, far_count) + own.shape[1:], own.dtype)
        for m in range(far_count):
            for n, part in enumerate((own, neighbour)):
                total = lax.dynamic_update_slice(
                    total, part[m][None, None], ((place & 1) ^ n, (place >> 1) ^ m, 0, 0)
                )
        return total

    return in_order


def plain_steps(place, in_order):
    near, far = place & 1, place >> 1

    def half_of(d_w, got):
        return (wide(pick(d_w.reshape((2,) + got.shape), near, 0)) + wide(got)).astype(BF16)

    def bundle_of(quarter, half):
        return [jnp.concatenate([quarter, pick(half, far ^ m, 0)], axis=0) for m in range(1, half.shape[0])]

    def quarter_of(half, parts):
        return (wide(pick(half, far, 0)) + sum(wide(p) for p in parts)).astype(BF16)

    def first(info, half_0, d_w1, bundle, cross_half, own_half, cross, own):
        rows = half_0.shape[1]
        quarter = quarter_of(half_0, [g[:rows] for g in cross])
        half_1 = half_of(d_w1, bundle[:, -rows:])
        cross_total = (pick(cross_half, far, 0) + sum(wide(g[rows:]) for g in cross)).astype(BF16)
        own_total = pick(own_half, far, 0) + sum(wide(g) for g in own)
        return quarter, half_1, cross_total, own_total, *bundle_of(quarter, half_1)

    def second(info, quarter_0, half_1, d_w2, near_got, got):
        rows = half_1.shape[1]
        whole = jnp.stack([quarter_0] + [g[:rows] for g in got])
        quarter = quarter_of(half_1, [g[rows:] for g in got])
        half_2 = half_of(d_w2, near_got)
        return whole, quarter, half_2, *bundle_of(quarter, half_2)

    def third(info, quarter_1, half_2, own_total, across, gains, got, shard_rows):
        gain = sum(gains)
        rows = half_2.shape[1]
        whole = jnp.stack([quarter_1] + [g[:rows] for g in got])
        quarter = quarter_of(half_2, [g[rows:] for g in got])
        part = own_total + wide(across)
        sent = jnp.concatenate([quarter, part[shard_rows:-8].astype(BF16), in_two(gain).astype(BF16)], axis=0)
        return whole, sent, part[:shard_rows], part[-8:]

    def last(info, third, whole_1, got):
        total = sum(wide(g[-8:]) for g in got) + wide(third[-8:])
        total = jnp.broadcast_to(total[0:1] + total[4:5], (8, D))
        own = jnp.concatenate([third[:-8], in_two(total).astype(BF16)], axis=0)
        return jnp.concatenate([jnp.stack([own] + list(got)), whole_1], axis=1)

    def close(info, halves, gain):
        rows = halves[0].shape[1]
        *halves, last_own, last_got = halves
        halves = [*halves, last_got[:, -rows:], last_own[:, :-rows], last_got[:, :-rows]]
        whole = [
            wide(in_order(halves[2 * h][:, :rows], halves[2 * h + 1][:, :rows]).reshape(-1, D)) for h in range(3)
        ]
        kinds = [jnp.concatenate([w[k * 64 : k * 64 + 64] for w in whole], axis=0) for k in range(3)]
        bias = [jnp.concatenate([w[192, k : k + 64] for w in whole]) for k in (0, 128)]
        o_total = in_order(halves[4][:, rows:-8], halves[5][:, rows:-8]).transpose(1, 0, 2, 3).reshape(-1, D)
        total = sum(wide(v[0, -8:-7]) + wide(v[0, -4:-3]) for v in halves[4:])
        return *kinds, *bias, wide(o_total), (total / wide(gain))[0]

    return first, second, third, last, close


def local(
    inputs,
    cotangent,
    lengths,
    norm1_gain,
    query_weight,
    query_bias,
    key_weight,
    value_weight,
    value_bias,
    inner_gain,
    output_weight,
    output_bias,
    norm2_gain,
    hidden_weight,
    hidden_bias,
    hidden_gain,
    project_weight,
    project_bias,
):
    dp_count = lax.axis_size("dp")
    far_count = dp_count // 2
    me = lax.axis_index("head")
    heads = query_weight.shape[1] // HEAD_DIM
    shard_rows = hidden_weight.shape[0]
    slice_cols = hidden_weight.shape[1]
    inner_rows = output_weight.shape[0]

    first_length = lengths[0, 0]
    limits = [
        jnp.where(first_length > SHORT, first_length - SHORT * (me ^ r), lengths[0, me ^ r])
        for r in range(4)
    ]
    place = lax.axis_index("dp")
    info = jnp.stack([first_length] + limits + [me, place & 1, place >> 1]).astype(jnp.int32)

    first_weight, second_weight = hidden_weight, project_weight.T
    straight = shard_rows % 16 == 0

    below = jnp.zeros((16, D), BF16)
    below = below.at[0, :slice_cols].set(hidden_bias).at[1, :slice_cols].set(hidden_gain)
    pack = jnp.concatenate([output_weight, below.at[2, :inner_rows].set(inner_gain)], axis=0)
    normed1 = first_norm(inputs, norm1_gain)
    near = swap(normed1, 1)
    across = swap(normed1, 2)

    if straight:
        both = jnp.concatenate([first_weight, second_weight], axis=0)
        both_far = [both] + far_swaps(lambda m: both)

    pack_across = swap(pack, 2)
    pack_near = swap(pack, 1)

    def per_head(weight):
        return weight.T.reshape(heads, HEAD_DIM, D)

    zero_bias = jnp.zeros_like(query_bias)
    packed_weight = jnp.concatenate(
        [per_head(query_weight), per_head(key_weight), per_head(value_weight)], axis=1
    )
    packed_bias = wide(
        jnp.concatenate(
            [b.reshape(heads, 1, HEAD_DIM) for b in (query_bias, zero_bias, value_bias)], axis=2
        )
    )
    across, info, packed_weight, packed_bias, pack = lax.optimization_barrier(
        (across, info, packed_weight, packed_bias, pack)
    )
    far = swap(across, 1)
    rows = (normed1, near, across, far)
    waits = []
    if straight:
        first_own = jnp.stack([w[:shard_rows] for w in both_far])
        second_own = jnp.stack([w[shard_rows:] for w in both_far])
        first_own, second_own = lax.optimization_barrier((first_own, second_own))
        first_near = dp_swap(first_own, 1)
        second_across = swap(second_own, 2)
        waits = [first_own, second_own]
    early = attention_forward(after(info, *waits), rows, packed_weight, packed_bias, 0, 1, [])
    waits = []
    if straight:
        pack_across, first_near, second_across, early = lax.optimization_barrier(
            (pack_across, first_near, second_across, early)
        )
        first_block = jnp.stack([first_own, first_near])
        second_block = jnp.stack([second_own, second_across])
        first_across = swap(first_block, 2)
        second_near = dp_swap(second_block, 1)
        first_sides = [first_block, swap(first_block, 1), first_across]
        second_sides = [second_block, second_near, swap(second_block, 1)]
        waits = [first_block, second_block, first_sides[1], second_sides[2]]
    pack_far = swap(pack_across, 1)
    packs = (pack, pack_near, pack_across, pack_far)
    info_now = after(info, early[0], pack_far, pack_near, *waits)
    late = attention_forward(info_now, rows, packed_weight, packed_bias, 1, heads - 1, early[:4])
    attended_heads = late[:4]

    def exchange(pieces):
        return [pieces[0]] + [swap(pieces[r], r) for r in (1, 2, 3)]

    attended = exchange(attended_heads)
    vectors = jnp.concatenate(
        [wide(jnp.stack([output_bias, norm2_gain, project_bias])), jnp.zeros((5, D), F32)], axis=0
    )
    if straight:
        first_across, second_near = (after(v, late[0]) for v in (first_across, second_near))
        first_sides.append(swap(first_across, 1))
        second_sides.append(swap(second_near, 1))
        sources = first_sides + second_sides

        def pieces(info, refs, which, r):
            found = []
            for n in range(2):
                for m in range(far_count):
                    start = ((info[7] ^ m) * 2 + (info[6] ^ n)) * shard_rows
                    if which == 0:
                        source = refs[r].at[n, m]
                    else:
                        source = refs[4 + (r % 2) * 2 + n].at[r // 2, m]
                    found.append((source, pl.multiple_of(start, shard_rows)))
            return found

        piece_count = dp_count
    else:
        shards = jnp.concatenate([first_weight, second_weight], axis=0)
        gathered = lax.all_gather(shards, ("dp", "head"), axis=0, tiled=False)
        gathered = gathered.reshape(dp_count, 4, 2, shard_rows, slice_cols)
        sources = [gathered.transpose(1, 2, 0, 3, 4).reshape(4, 2, D, slice_cols)]
        pieces = lambda info, refs, which, r: [(refs[0].at[info[5] ^ r, which], 0)]
        piece_count = 1
    output, d_middle, *rest = token_section(
        info, attended, packs, inputs, cotangent, vectors, sources, pieces, piece_count
    )
    attended_grad, (in_keep, in_send, out_keep, out_send) = rest[:4], rest[4:]

    if out_keep.shape[1] != dp_count:
        def recut(v):
            o_rows = inner_rows // v.shape[1]
            end = v.shape[2] - 8
            weight = v[:, :, : end - o_rows].reshape(2, dp_count, -1, slice_cols)
            o_part = v[:, :, end - o_rows : end].reshape(2, dp_count, -1, slice_cols)
            vec_part = jnp.broadcast_to(v[:, 0:1, end:], (2, dp_count, 8, slice_cols))
            return jnp.concatenate([weight, o_part, vec_part], axis=2)

        out_keep, out_send = recut(out_keep), recut(out_send)
    grads = exchange(attended_grad)
    out_got, in_got = swap(out_send, 1), swap(in_send, 1)
    pairs = lambda v: v.reshape(2, far_count, 2, -1, slice_cols)
    out_keep, out_got = pairs(out_keep), pairs(out_got)
    in_keep, in_got = (v.reshape(2, -1, slice_cols) for v in (in_keep, in_got))
    mine = lambda v: pick(v, place & 1, 1)
    theirs = lambda v: pick(v, 1 - (place & 1), 1)
    out_part = lambda q, take: wide(take(out_keep[q])) + wide(take(out_got[q]))

    head_rows = 256 // dp_count
    by_place = lambda v: v.reshape(2, far_count, head_rows, D)
    other_half = lambda v: pick(by_place(v), 1 - (place & 1), 0)

    def half_sum(d_w, got):
        return (wide(keep_near(by_place(d_w), 0)) + wide(got)).astype(BF16)

    def head_step(h, info):
        saved, local_head = (early[4:], 0) if h == 0 else (late[4:], h - 1)
        return attention_backward(h, info, grads, attended_heads, saved, local_head, rows)

    lane_halves = (slice(0, slice_cols // 2), slice(slice_cols // 2, slice_cols))

    def across_part(lanes):
        return (wide(in_keep[1][..., lanes]) + wide(in_got[1][..., lanes])).astype(BF16)

    across_a = across_part(lane_halves[0])
    own_sent = out_part(0, theirs).astype(BF16)
    own_sent, across_a, grads = lax.optimization_barrier((own_sent, across_a, grads))
    across_got_a = swap(across_a, 2)
    own_near = dp_swap(own_sent, 1)
    packed_0, d_weight_0 = head_step(0, after(info, own_sent, across_a))

    packed_0, d_weight_0, own_near, across_got_a, in_keep, in_got = lax.optimization_barrier(
        (packed_0, d_weight_0, own_near, across_got_a, in_keep, in_got)
    )
    across_b = across_part(lane_halves[1])
    own_half = out_part(0, mine) + wide(own_near)
    own_payload = [far_of(own_half, m, 0) for m in range(1, far_count)]
    near_sent = jnp.concatenate([out_part(1, theirs).astype(BF16), other_half(d_weight_0)], axis=1)
    near_sent, across_b, *own_payload = lax.optimization_barrier((near_sent, across_b, *own_payload))
    across_got_b = swap(across_b, 2)
    near_got = dp_swap(near_sent, 1)
    own_far = [dp_swap(p, 2 * (m + 1)) for m, p in enumerate(own_payload)]
    packed_1, d_weight_1 = head_step(1, after(info, near_sent, across_b, *own_payload))

    packed_1, d_weight_1, near_got, across_got_b, *own_far = lax.optimization_barrier(
        (packed_1, d_weight_1, near_got, across_got_b, *own_far)
    )
    half_0 = half_sum(d_weight_0, near_got[:, -head_rows:])
    cross_half = out_part(1, mine) + wide(near_got[:, :-head_rows])
    cross_payload = [
        jnp.concatenate([far_of(half_0, m, 0), far_of(cross_half, m, 0)], axis=0) for m in range(1, far_count)
    ]
    across_got = jnp.concatenate([across_got_a, across_got_b], axis=-1)
    in_sum = wide(in_keep[0]) + wide(in_got[0]) + wide(across_got)
    in_sum = in_sum.reshape(far_count, 2, shard_rows, slice_cols)
    near_sent = jnp.concatenate([theirs(in_sum).astype(BF16), other_half(d_weight_1)], axis=1)
    near_sent, *cross_payload = lax.optimization_barrier((near_sent, *cross_payload))
    near_got = dp_swap(near_sent, 1)
    cross_far = [dp_swap(p, 2 * (m + 1)) for m, p in enumerate(cross_payload)]
    packed_2, d_weight_2 = head_step(2, after(info, near_sent, *cross_payload))

    d_weight_2, packed_2, near_got, *cross_far = lax.optimization_barrier(
        (d_weight_2, packed_2, near_got, *cross_far)
    )
    hr = head_rows
    steps = opening, middle_step, third_step, last_step, finish
    if hr % 16:
        steps = plain_steps(place, in_order_of(place, far_count))
    step_a, step_b, step_c, step_d, step_e = steps
    sent_2 = other_half(d_weight_2)
    got_2 = dp_swap(sent_2, 1)
    quarter_0, half_1, cross_total, own_total, *payload = step_a(
        after(info, sent_2), half_0, d_weight_1, near_got, cross_half, own_half, cross_far, own_far
    )
    step_1 = [dp_swap(p, 2 * (m + 1)) for m, p in enumerate(payload)]
    out_across = swap(cross_total, 2)
    dx_keep, dx_send, gain_part = input_part(
        [packed_0, packed_1, after(packed_2, cross_total, *payload)], packed_weight, [d_weight_0, d_weight_1, d_weight_2]
    )
    d_weight_2, got_2, step_1, out_across, dx_send, gain_part = lax.optimization_barrier(
        (d_weight_2, got_2, step_1, out_across, dx_send, gain_part)
    )
    near_rows = swap(dx_send, 1)
    gains = [gain_part] + [swap(gain_part, r) for r in (1, 2, 3)]

    whole_0, quarter_1, half_2, *payload = step_b(info, quarter_0, half_1, d_weight_2, got_2, step_1)
    whole_0, near_rows, *payload = lax.optimization_barrier((whole_0, near_rows, *payload))
    step_2 = [dp_swap(p, 2 * (m + 1)) for m, p in enumerate(payload)]
    other_0 = dp_swap(whole_0, 1)
    cross_sum = (wide(dx_keep[1]) + wide(after(near_rows[1], *step_2))).astype(BF16)
    cross_got = swap(cross_sum, 2)

    whole_1, third, project_grad, vec_total = step_c(
        after(info, cross_sum), quarter_1, half_2, own_total, out_across, gains, step_2, shard_rows
    )
    step_3 = far_swaps(lambda m: third)
    in_half = mine(in_sum) + wide(near_got[:, :-hr])

    last_own = step_d(after(info, other_0), third, whole_1, step_3)
    last_sent, in_half = lax.optimization_barrier((last_own, in_half))
    last_near = dp_swap(last_sent, 1)
    in_far = far_swaps(lambda m: far_of(in_half, m, 0))
    input_grad = input_gradient(inputs, norm1_gain, d_middle, dx_keep, near_rows, cross_got)
    query_grad, key_grad, value_grad, query_bias_grad, value_bias_grad, o_total, norm1_total = step_e(
        after(info, input_grad), [whole_0, other_0, whole_1, last_own, last_near], norm1_gain
    )
    *in_far, norm1_total = lax.optimization_barrier((*in_far, norm1_total))
    hidden_grad = keep_far(in_half, 0) + sum(wide(g) for g in in_far)
    return (
        output,
        input_grad,
        norm1_total,
        query_grad.T,
        query_bias_grad,
        key_grad.T,
        value_grad.T,
        value_bias_grad,
        vec_total[2, :inner_rows],
        o_total,
        vec_total[5],
        vec_total[3],
        hidden_grad,
        vec_total[1],
        vec_total[0],
        project_grad.T,
        vec_total[4],
    )


def solution(mesh):
    rows = P(("dp", "head"), None)
    columns = P(None, "head")
    head = P("head")
    return jax.shard_map(
        local,
        mesh=mesh,
        in_specs=(
            rows, rows, P("dp", None), P(), columns, head, columns, columns, head, head,
            P("head", None), P(), P(), P("dp", "head"), head, head, P("head", "dp"), P(),
        ),
        out_specs=(
            rows, rows, P(), columns, head, columns, columns, head, head, P("head", None),
            P(), P(), P("dp", "head"), head, head, P("head", "dp"), P(),
        ),
        check_vma=False,
    )
```
